128 devices in a mesh: gx: 8 (over x, core), gy: 16 (over y, z).
Axes of the slice: x: 4, y: 4, z: 4, core: 2. Of those that a mesh axis runs over, the one named last changes fastest.
Arguments:
- positions: float32 [3, 32, 32, 32, 16], P(None, None, 'gx', 'gy'), may hold values from 0 to 8
- charges: float32 [32, 32, 32, 16], P(None, 'gx', 'gy'), may hold values from -4 to 4
- types: int32 [32, 32, 32, 16], P(None, 'gx', 'gy'), may hold values from 0 to 63
- counts: int32 [32, 32, 16], P('gx', 'gy'), may hold values from 20 to 32
- eps_type: float32 [64], replicated, may hold values from 0.05 to 0.5
- sig_type: float32 [64], replicated, may hold values from 1.5 to 3
Outputs:
- pair_force: float32 [3, 32, 32, 32, 16], P(None, None, 'gx', 'gy')
- mesh_force: float32 [3, 32, 32, 32, 16], P(None, None, 'gx', 'gy')
The draws below stay inside these ranges and needn't reach their ends.
All inputs are finite; a program needn't handle non-finite values.
Results may differ from the reference program's by a relative error of at most 0.0003.
Values sent between devices are 32-bit elements; how exact they have to be, the bound alone decides.
No kernel may reach another device: no remote copies, remote signals or barrier semaphores. Data moves between devices by JAX's collectives and lax.ppermute only.
A program may use at most 256 MiB of HBM per device.

```python
import math
import jax
import jax.numpy as jnp
from jax import lax

P_SIZE = 32
CELL = 8
NCZ = 16
NT = 64
NCX = 32
NCY = 32


def place_ends(result, own_key, low, largest):
    shape = result.shape
    spot = [jax.random.randint(jax.random.fold_in(own_key, axis), (), 0, shape[axis]) for axis in range(len(shape))]
    result = result.at[tuple(spot)].set(low)
    longest = shape.index(max(shape))
    spot[longest] = (spot[longest] + 1) % shape[longest]
    return result.at[tuple(spot)].set(largest)


def levels(own_key, extent, cuts, smallest, largest):
    def one(axis_at, shards_of):
        steps = jax.random.uniform(jax.random.fold_in(jax.random.fold_in(own_key, 6), axis_at), (shards_of,), jnp.float32, smallest / len(cuts), largest / len(cuts))
        return jnp.repeat(jnp.exp(steps), extent[axis_at] // shards_of).reshape((-1,) + (1,) * (len(extent) - axis_at - 1))

    level = one(*cuts[0])
    for cut in cuts[1:]:
        level = level * one(*cut)
    return level


def gaussian(stream_key, extent, spread, bound, pieces=(), kind=jnp.bfloat16):
    result = spread * jax.random.normal(stream_key, extent, jnp.float32)
    if pieces:
        result = result * levels(stream_key, extent, pieces, -0.22, 0.18)
    return jnp.clip(result, -bound, bound).astype(kind)


def setup_inputs(seed: int = 0) -> dict:
    key_of = jax.random.split(jax.random.key(seed), 7)
    return {
        "positions": jnp.clip(8.0 * jax.random.uniform(key_of[0], (3, P_SIZE, NCX, NCY, NCZ), jnp.float32) ** levels(key_of[0], (3, P_SIZE, NCX, NCY, NCZ), ((2, 8), (3, 16)), -0.2, 0.2), 0.0, 8.0),
        "charges": gaussian(key_of[1], (P_SIZE, NCX, NCY, NCZ), 1.0, 4.0, ((1, 8), (2, 16)), jnp.float32),
        "types": place_ends(jax.random.randint(key_of[2], (P_SIZE, NCX, NCY, NCZ), 0, NT), jax.random.fold_in(key_of[2], 1), 0, NT - 1).astype(jnp.int32),
        "counts": place_ends(jax.random.randint(key_of[3], (NCX, NCY, NCZ), 5 * P_SIZE // 8, P_SIZE + 1), jax.random.fold_in(key_of[3], 1), 5 * P_SIZE // 8, P_SIZE).astype(jnp.int32),
        "eps_type": jnp.clip(jnp.exp(jax.random.uniform(key_of[4], (NT,), jnp.float32, math.log(0.05), math.log(0.5))), 0.05, 0.5),
        "sig_type": jnp.clip(jax.random.uniform(key_of[5], (NT,), jnp.float32, 1.5, 3.0), 1.5, 3.0),
    }


GEWALD = 0.7
HIGHEST = lax.Precision.HIGHEST

def spline_weights(offsets):
    points = jnp.arange(CELL + 4).astype(offsets.dtype) - 2.0
    target_shape = (CELL + 4,) + (1,) * offsets.ndim
    spans = jnp.abs(offsets[None] - points.reshape(target_shape))
    inside_part = (4.0 - 6.0 * spans * spans + 3.0 * spans * spans * spans) / 6.0
    outside_part = (2.0 - spans) * (2.0 - spans) * (2.0 - spans) / 6.0
    return jnp.where(spans < 1.0, inside_part, jnp.where(spans < 2.0, outside_part, 0.0))

def pair_energy(squared, charge_prod, eps_prod, sigma):
    sigma_sq = sigma * sigma
    ratios = sigma_sq / (squared + sigma_sq)
    ratio_cube = ratios * ratios * ratios
    softened = jnp.sqrt(squared + 1.0)
    inside = 4.0 * eps_prod * (ratio_cube * ratio_cube - ratio_cube) + charge_prod * lax.erfc(GEWALD * softened) / softened
    cutoff_square = float(CELL * CELL)
    fraction = 1.0 - squared / cutoff_square
    switch = jnp.where(squared < cutoff_square, fraction * fraction, 0.0)
    return switch * inside

def pair_slope(squared, charge_prod, eps_prod, sigma):
    return jax.grad(lambda squared_in: jnp.sum(pair_energy(squared_in, charge_prod, eps_prod, sigma)))(squared)

def cell_forces(padded):
    length_a = padded.shape[2] - 2
    length_b = padded.shape[3] - 2
    length_c = padded.shape[4] - 2
    centre = padded[:, :, 1:1 + length_a, 1:1 + length_b, 1:1 + length_c]
    totals = [jnp.zeros(centre.shape[1:], padded.dtype) for component in range(3)]
    for shift_a in (-1, 0, 1):
        for shift_b in (-1, 0, 1):
            for shift_c in (-1, 0, 1):
                partner = padded[:, :, 1 + shift_a:1 + shift_a + length_a, 1 + shift_b:1 + shift_b + length_b, 1 + shift_c:1 + shift_c + length_c]
                shifts = (shift_a, shift_b, shift_c)
                separation = [CELL * shifts[component] + partner[component][None] - centre[component][:, None] for component in range(3)]
                squared = separation[0] * separation[0] + separation[1] * separation[1] + separation[2] * separation[2]
                derivative = pair_slope(squared, centre[3][:, None] * partner[3][None], centre[4][:, None] * partner[4][None], 0.5 * (centre[5][:, None] + partner[5][None]))
                totals = [totals[component] + lax.optimization_barrier(jnp.sum(2.0 * derivative * separation[component], axis=1)) for component in range(3)]
    return jnp.stack(totals)

def fold_wrap(blocks):
    cell_count = blocks.shape[-2]
    first_half = blocks[..., :CELL]
    second_half = jnp.pad(blocks[..., CELL:], [(0, 0)] * (blocks.ndim - 1) + [(0, CELL - 4)])
    summed = (first_half + jnp.roll(second_half, 1, axis=-2)).reshape(blocks.shape[:-2] + (cell_count * CELL,))
    return jnp.roll(summed, -2, axis=-1)

def windows_wrap(fields):
    cell_count = fields.shape[-1] // CELL
    leading = jnp.roll(fields, 2, axis=-1).reshape(fields.shape[:-1] + (cell_count, CELL))
    trailing = jnp.roll(leading, -1, axis=-2)[..., :4]
    return jnp.concatenate([leading, trailing], axis=-1)

def interpolate(windowed, weight_x, weight_y, weight_z):
    reduced = jnp.einsum('dczbyax,xpabc->dzypabc', windowed, weight_x, precision=HIGHEST)
    reduced = jnp.einsum('dzypabc,ypabc->dzpabc', reduced, weight_y, precision=HIGHEST)
    return jnp.einsum('dzpabc,zpabc->dpabc', reduced, weight_z, precision=HIGHEST)

def folded(indices, length):
    return jnp.where(indices < length // 2, indices, indices - length)

def green(mode_x, mode_y, mode_z, length_x, length_y, length_z, normalize):
    freq_x = mode_x.astype(jnp.float32)
    freq_y = mode_y.astype(jnp.float32)
    freq_z = mode_z.astype(jnp.float32)
    wave_x = freq_x * (2.0 * math.pi / length_x)
    wave_y = freq_y * (2.0 * math.pi / length_y)
    wave_z = freq_z * (2.0 * math.pi / length_z)
    norm_sq = wave_x * wave_x + wave_y * wave_y + wave_z * wave_z
    shaped = jnp.sinc(freq_x / length_x) * jnp.sinc(freq_y / length_y) * jnp.sinc(freq_z / length_z)
    shaped = shaped * shaped
    shaped = shaped * shaped
    shaped = shaped * shaped
    safe_sq = jnp.where(norm_sq > 0.0, norm_sq, 1.0)
    values = jnp.where(norm_sq > 0.0, normalize * 4.0 * math.pi * jnp.exp(-norm_sq / (4.0 * GEWALD * GEWALD)) / (safe_sq * shaped), 0.0)
    return (values * wave_x, values * wave_y, values * wave_z)

def atom_table(positions, charges, types, counts, eps_type, sig_type):
    slot_count = charges.shape[0]
    occupied = (jnp.arange(slot_count, dtype=jnp.int32)[:, None, None, None] < counts[None]).astype(charges.dtype)
    epsilon = jnp.take(eps_type, types)
    sigmas = jnp.take(sig_type, types)
    atoms = jnp.concatenate([positions, (charges * occupied)[None], (jnp.sqrt(epsilon) * occupied)[None], sigmas[None]], axis=0)
    return (atoms, occupied)

def reference(positions, charges, types, counts, eps_type, sig_type):
    atoms, occupied = atom_table(positions, charges, types, counts, eps_type, sig_type)
    wrapped = jnp.pad(atoms, ((0, 0), (0, 0), (1, 1), (1, 1), (1, 1)), mode='wrap')
    slab_ids = jnp.arange(NCX, dtype=jnp.int32)

    def slab_pairs(slab_index):
        return cell_forces(lax.dynamic_slice_in_dim(wrapped, slab_index, 3, axis=2))
    pair_blocks = lax.map(slab_pairs, slab_ids)
    pair_force = jnp.transpose(pair_blocks[:, :, :, 0], (1, 2, 0, 3, 4)) * occupied[None]
    weight_x = spline_weights(atoms[0])
    weight_y = spline_weights(atoms[1])
    plain_z = spline_weights(atoms[2])
    weight_z = plain_z * atoms[3][None]

    def slab_charge(slab_index):
        part_x = lax.dynamic_slice_in_dim(weight_x, slab_index, 1, axis=2)
        part_y = lax.dynamic_slice_in_dim(weight_y, slab_index, 1, axis=2)
        part_z = lax.dynamic_slice_in_dim(weight_z, slab_index, 1, axis=2)
        planes = jnp.einsum('ypabc,zpabc->yzpabc', part_y, part_z, precision=HIGHEST)
        blocks = jnp.einsum('xpabc,yzpabc->xyzabc', part_x, planes, precision=HIGHEST)
        along_z = fold_wrap(jnp.moveaxis(blocks, 2, -1))
        along_y = fold_wrap(jnp.transpose(along_z, (0, 2, 4, 3, 1)))
        return along_y[:, 0]
    layers = lax.map(slab_charge, slab_ids)
    density = jnp.transpose(fold_wrap(jnp.transpose(layers, (2, 3, 0, 1))), (2, 1, 0))
    spectrum = jnp.fft.fftn(density)
    length_x, length_y, length_z = density.shape
    mode_x = folded(jnp.arange(length_x, dtype=jnp.int32), length_x)[:, None, None]
    mode_y = folded(jnp.arange(length_y, dtype=jnp.int32), length_y)[None, :, None]
    mode_z = folded(jnp.arange(length_z, dtype=jnp.int32), length_z)[None, None, :]
    waves = green(mode_x, mode_y, mode_z, length_x, length_y, length_z, 1.0)
    fields = jnp.stack([jnp.real(jnp.fft.ifftn(-1j * component * spectrum)) for component in waves])
    extended = jnp.concatenate([fields[:, -2:], fields, fields[:, :2]], axis=1)

    def slab_force(slab_index):
        window = lax.dynamic_slice_in_dim(extended, slab_index * CELL, CELL + 4, axis=1)
        along_z = windows_wrap(window)
        along_y = windows_wrap(jnp.transpose(along_z, (0, 1, 3, 4, 2)))
        windowed = jnp.transpose(along_y, (0, 2, 3, 4, 5, 1))[:, :, :, :, :, None, :]
        part_x = lax.dynamic_slice_in_dim(weight_x, slab_index, 1, axis=2)
        part_y = lax.dynamic_slice_in_dim(weight_y, slab_index, 1, axis=2)
        part_z = lax.dynamic_slice_in_dim(plain_z, slab_index, 1, axis=2)
        return interpolate(windowed, part_x, part_y, part_z)
    force_blocks = lax.map(slab_force, slab_ids)
    mesh_force = jnp.transpose(force_blocks[:, :, :, 0], (1, 2, 0, 3, 4)) * atoms[3][None]
    return (pair_force, mesh_force)
```

```python
import functools
import math

import jax
import jax.numpy as jnp
import ml_dtypes
import numpy as np
from jax import lax
from jax.experimental import pallas as pl
from jax.experimental.pallas import tpu as pltpu
from jax.sharding import PartitionSpec as P

CELL = 8
GEWALD = 0.7
CUT = 64.0
F32 = jnp.float32
BF16 = jnp.bfloat16

SLOTS = 32
CX, CY, CZ = 4, 2, 16
CELLS = CX * CY * CZ
DX, DY = 8, 16
LX, LY, LZ = 256, 256, 128
BX, BY = CX * CELL + 4, CY * CELL + 4
BLOCK = 768
GROUPS = CELLS // 4
KZ = 48
KX = 48
VMEM = pl.BlockSpec(memory_space=pltpu.VMEM)
SMEM = pl.BlockSpec(memory_space=pltpu.SMEM)


def params(mib=40):
    return pltpu.CompilerParams(vmem_limit_bytes=mib << 20)


def split(array):
    high = array.astype(ml_dtypes.bfloat16)
    low = (array - high.astype(np.float64)).astype(ml_dtypes.bfloat16)
    return high, low


def basis(length):
    half = length // 2
    modes = np.concatenate([np.arange(half + 1), np.arange(1, half)])
    sines = np.arange(length) > half
    return modes, sines


def wave(points, modes, sines, length):
    angle = 2.0 * np.pi * (np.outer(modes, points) % length) / length
    return np.where(sines[:, None], np.sin(angle), np.cos(angle))


def wave_slope(points, modes, sines, length):
    angle = 2.0 * np.pi * (np.outer(modes, points) % length) / length
    k = 2.0 * np.pi * modes / length
    k = np.where(modes == length // 2, 0.0, k)[:, None]
    return np.where(sines[:, None], -k * np.cos(angle), k * np.sin(angle))


def damping(modes, length):
    k = 2.0 * np.pi * modes / length
    return np.exp(-k * k / (4.0 * GEWALD * GEWALD)) / np.sinc(modes / length) ** 8


def norms(modes, length):
    return np.where((modes == 0) | (modes == length // 2), 1.0, 2.0) / length


@functools.cache
def tables():
    mz, sz = basis(LZ)
    tz = np.zeros((4, LZ, KZ))
    for zg in range(4):
        tz[zg, :, :36] = wave(32 * zg - 2 + np.arange(36), mz, sz, LZ)
    mx, sx = basis(LX)
    my, sy = basis(LY)
    tx = np.zeros((DX, KX, LX))
    gain_x = damping(mx, LX) * norms(mx, LX)
    ix = np.zeros((2, LX, DX * BX))
    for gx in range(DX):
        points = gx * CX * CELL - 2 + np.arange(BX)
        tx[gx, :BX] = (wave(points, mx, sx, LX) * gain_x[:, None]).T
        ix[0, :, gx * BX : (gx + 1) * BX] = wave(points, mx, sx, LX)
        ix[1, :, gx * BX : (gx + 1) * BX] = wave_slope(points, mx, sx, LX)
    points = (np.arange(DY)[None, :] * CY * CELL - 2 + np.arange(BY)[:, None]).reshape(-1)
    gain_y = damping(my, LY) * norms(my, LY)
    ty = wave(points, my, sy, LY) * gain_y[:, None]
    iy = np.concatenate([wave(points, my, sy, LY).T, wave_slope(points, my, sy, LY).T])
    kx2 = ((2.0 * np.pi * mx / LX) ** 2).astype(np.float32)[None, :]
    ky2 = ((2.0 * np.pi * my / LY) ** 2).astype(np.float32)[:, None]
    kz = 2.0 * np.pi * mz / LZ
    plane = np.stack([kz * kz, 4.0 * np.pi * damping(mz, LZ) * norms(mz, LZ)], 1)
    half = LZ // 2
    swap = 2.0 * np.pi * np.arange(half) / LZ
    swap = np.concatenate([-swap, swap]).astype(np.float32)[None, :]
    return dict(
        tz=split(tz),
        tx=split(tx),
        ty=split(ty),
        iy=split(iy),
        ix=split(ix),
        kx2=kx2,
        ky2=np.broadcast_to(ky2, (LY, 128)).astype(np.float32),
        plane=plane.astype(np.float32),
        swap=swap,
    )


def halves(value):
    high = value.astype(BF16)
    return high, (value - high.astype(F32)).astype(BF16)


def dot3(left, right, dims=((1,), (0,))):
    dot = lambda a, b: lax.dot_general(a, b, (dims, ((), ())), preferred_element_type=F32)
    return dot(left[0], right[0]) + (dot(left[0], right[1]) + dot(left[1], right[0]))


def table_kernel(pos_ref, charge_ref, type_ref, count_ref, eps_ref, sig_ref, atoms_ref, rows_ref):
    slots = lax.broadcasted_iota(jnp.int32, (SLOTS, CELLS), 0)
    occupied = slots < count_ref[...]
    kinds = type_ref[...].T
    eps = jnp.zeros((SLOTS, CELLS), F32)
    sig = jnp.zeros((SLOTS, CELLS), F32)
    for kind in range(eps_ref.shape[0]):
        match = kinds == kind
        eps = jnp.where(match, eps_ref[kind], eps)
        sig = jnp.where(match, sig_ref[kind], sig)
    charge = jnp.where(occupied, charge_ref[...].T, 0.0)
    for d in range(3):
        atoms_ref[d] = pos_ref[d].T
    atoms_ref[3] = charge
    atoms_ref[4] = jnp.where(occupied, jnp.sqrt(eps), 0.0)
    atoms_ref[5] = sig
    charge = charge.T
    for c in range(4):
        value = pos_ref[c] if c < 3 else charge
        value = value.reshape(GROUPS, 4, SLOTS)
        rows_ref[c] = jnp.concatenate([value[:, s, :] for s in range(4)], axis=1)


def spline(offset):
    span = jnp.abs(offset)
    outer = jnp.maximum(2.0 - span, 0.0)
    inner = jnp.maximum(1.0 - span, 0.0)
    return (outer * outer * outer) * (1.0 / 6.0) - (inner * inner * inner) * (2.0 / 3.0)


def weights(rows_ref, tz_high, tz_low, col, charged):
    point = (lax.broadcasted_iota(jnp.int32, (16, 128), 0) - 2).astype(F32)
    point_z = (lax.broadcasted_iota(jnp.int32, (KZ, 128), 0) - 2).astype(F32)
    shift = ((lax.broadcasted_iota(jnp.int32, (1, 128), 1) // SLOTS) * CELL).astype(F32)
    modes, planes = [], []
    for zg in range(4):
        row = [rows_ref[c, pl.ds(col * 4 + zg, 1), :] for c in range(4)]
        along_x = spline(row[0] - point)
        along_y = spline(row[1] - point)
        if charged:
            along_y = along_y * row[3]
        along_z = spline(row[2] + shift - point_z)
        modes.append(dot3((tz_high[zg], tz_low[zg]), halves(along_z)))
        planes.append((along_y[:12, None, :] * along_x[None, :, :]).reshape(192, 128))
    return jnp.concatenate(modes, axis=1), jnp.concatenate(planes, axis=1)


def spread_kernel(rows_ref, tz_high, tz_low, out_ref, total, packed):
    total[...] = jnp.zeros_like(total)

    def column(col, carry):
        modes, planes = weights(rows_ref, tz_high, tz_low, col, True)
        part = dot3(halves(planes), halves(modes), ((1,), (1,))).reshape(12, 16, LZ)
        y = (col % CY) * CELL
        x = pl.multiple_of((col // CY) * CELL, CELL)
        total[pl.ds(y, 12), pl.ds(x, 16), :] += part
        return carry

    lax.fori_loop(0, CX * CY, column, 0)
    for y in range(BY):
        packed[y * BX : (y + 1) * BX, :] = total[y, :BX, :]
    packed[BX * BY :, :] = jnp.zeros((BLOCK - BX * BY, LZ), F32)
    out_ref[...] = packed[...].T


def plane_kernel(
    plane_ref, in_ref, txh, txl, tyh, tyl, iyh, iyl, ixh, ixl, kx2, ky2, out_ref, stacked
):
    for y in range(BY):
        value = in_ref[:, y * BX : y * BX + KX]
        for gx in range(DX):
            stacked[gx, y * DY : (y + 1) * DY, :KX] = value[gx * DY : (gx + 1) * DY]
    lines = jnp.zeros((BY * DY, LX), F32)
    for gx in range(DX):
        lines = lines + dot3(halves(stacked[gx, :, :KX]), (txh[gx], txl[gx]))
    modes = dot3((tyh[...], tyl[...]), halves(lines))
    k2 = kx2[...] + jnp.concatenate([ky2[...], ky2[...]], axis=1) + plane_ref[0]
    positive = k2 > 0.0
    modes = jnp.where(positive, modes * (plane_ref[1] / jnp.where(positive, k2, 1.0)), 0.0)
    both = dot3((iyh[...], iyl[...]), halves(modes))
    rows = BY * DY
    plain = halves(both[:rows])
    slope = halves(both[rows:])
    fields = (
        dot3(plain, (ixh[1], ixl[1])),
        dot3(slope, (ixh[0], ixl[0])),
        dot3(plain, (ixh[0], ixl[0])),
    )
    for d in range(3):
        out_ref[:, d * BLOCK + BX * BY : (d + 1) * BLOCK] = jnp.zeros(
            (DX * DY, BLOCK - BX * BY), F32
        )
        for gx in range(DX):
            piece = fields[d][:, gx * BX : (gx + 1) * BX]
            for y in range(BY):
                lane = d * BLOCK + y * BX
                out_ref[gx * DY : (gx + 1) * DY, lane : lane + BX] = piece[y * DY : (y + 1) * DY]


def force_kernel(in_ref, rows_ref, tz_high, tz_low, swap_ref, out_ref, packed, padded, rows_out):
    for d in range(3):
        value = in_ref[:, d * BLOCK : (d + 1) * BLOCK].T
        if d == 2:
            value = pltpu.roll(value, LZ // 2, 1) * swap_ref[...]
        packed[...] = value
        for y in range(BY):
            padded[d, y, :BX, :] = packed[y * BX : (y + 1) * BX, :]
            padded[d, y, BX:, :] = jnp.zeros((40 - BX, LZ), F32)

    def column(col, carry):
        modes, planes = weights(rows_ref, tz_high, tz_low, col, False)
        modes = halves(modes)
        y = (col % CY) * CELL
        x = pl.multiple_of((col // CY) * CELL, CELL)
        for d in range(3):
            block = padded[d, pl.ds(y, 12), pl.ds(x, 16), :].reshape(192, LZ)
            along = dot3(halves(block), modes)
            force = jnp.sum(along * planes, axis=0, keepdims=True)
            for zg in range(4):
                at = pl.ds(col * 4 + zg, 1)
                rows_out[d, at, :] = force[:, 128 * zg : 128 * (zg + 1)] * rows_ref[3, at, :]
        return carry

    lax.fori_loop(0, CX * CY, column, 0)
    for d in range(3):
        value = rows_out[d]
        pieces = [value[:, s * SLOTS : (s + 1) * SLOTS][:, None, :] for s in range(4)]
        out_ref[d] = jnp.concatenate(pieces, axis=1).reshape(CELLS, SLOTS)


COULOMB = (
    -0.006157896808528851,
    -0.00037761534771162467,
    0.4246826287075061,
    -0.032594054879277516,
    0.5289809248435148,
    -0.3643412334667553,
    0.147196623703603,
    -0.012411731315994238,
    -0.015640759195296648,
    0.00499632789350256,
)
SCALES = (0.125, 0.125, 0.125, 1.0, 1.0, 0.0625)


def pair_term(own, other):
    dx = other[0] - own[0]
    dy = other[1] - own[1]
    dz = other[2] - own[2]
    r2 = dx * dx + dy * dy + dz * dz
    fade = jnp.maximum(1.0 - r2, 0.0)
    t = lax.rsqrt(r2 + 1.0 / CUT)
    decay = jnp.exp2(r2 * (-0.49 * CUT * math.log2(math.e)))
    scale = -16.0 * math.exp(-0.49)
    terms = [scale * c * 0.125**n for n, c in enumerate(COULOMB)]
    poly = terms[-1] * t + terms[-2]
    for c in terms[-3::-1]:
        poly = poly * t + c
    sigma = own[5] + other[5]
    square = sigma * sigma
    inverse = 1.0 / (r2 + square)
    x = square * inverse
    x3 = x * x * x
    rest = 1.0 - (x3 + x3)
    lj = x3 * (rest * ((fade * inverse) * 3.0 + 1.0) + 1.0)
    w = fade * ((own[4] * other[4]) * lj + (own[3] * other[3]) * (decay * poly))
    return w * dx, w * dy, w * dz


def pair_kernel(*refs, shifts, unroll):
    wide_refs = refs[:-3]
    out_ref, others, own = refs[-3:]
    low = (lax.broadcasted_iota(jnp.int32, (SLOTS, 256), 1) & CZ) == 0
    at_z = lax.broadcasted_iota(jnp.int32, (SLOTS, CELLS), 1) & (CZ - 1)
    for c in range(6):
        wides = []
        for ref in wide_refs:
            value = ref[c] * SCALES[c]
            wides.append(jnp.concatenate([value, jnp.zeros((SLOTS, 64), F32)], axis=1))
        own[c] = wides[0][:, 32:160]
        layers = {0: wides[0]}
        if len(wides) > 1:
            above, below = wides[1:]
            layers[1] = jnp.where(
                low, pltpu.roll(wides[0], 256 - CZ, 1), pltpu.roll(above, CZ, 1)
            )
            layers[-1] = jnp.where(
                low, pltpu.roll(below, 256 - CZ, 1), pltpu.roll(wides[0], CZ, 1)
            )
        for n, (a, b) in enumerate(shifts):
            value = layers[b][:, 32 * (a + 1) : 32 * (a + 1) + CELLS]
            if c == 0:
                value = value + float(a)
            if c == 1:
                value = value + float(b)
            up = jnp.where(
                at_z == CZ - 1, pltpu.roll(value, CZ - 1, 1), pltpu.roll(value, CELLS - 1, 1)
            )
            down = jnp.where(at_z == 0, pltpu.roll(value, CELLS - CZ + 1, 1), pltpu.roll(value, 1, 1))
            if c == 2:
                up = up + 1.0
                down = down - 1.0
            for m, part in enumerate((down, value, up)):
                row = (n * 3 + m) * SLOTS
                others[c, row : row + SLOTS] = part

    def step(n, sums):
        sums = list(sums)
        for jj in range(unroll):
            j = n * unroll + jj
            other = [others[c, pl.ds(j, 8, stride=0), :] for c in range(6)]
            for block in range(4):
                mine = [own[c, 8 * block : 8 * block + 8, :] for c in range(6)]
                force = pair_term(mine, other)
                for d in range(3):
                    sums[block * 3 + d] = sums[block * 3 + d] + force[d]
        return tuple(sums)

    zero = jnp.zeros((8, CELLS), F32)
    steps = len(shifts) * 3 * SLOTS // unroll
    sums = lax.fori_loop(0, steps, step, (zero,) * 12)
    for d in range(3):
        out_ref[d] = jnp.concatenate([sums[block * 3 + d] for block in range(4)], axis=0).T


def pair_forces(wides, shifts, unroll=4):
    rows = len(shifts) * 3 * SLOTS
    pairs = rows * SLOTS * CELLS
    return pl.pallas_call(
        functools.partial(pair_kernel, shifts=tuple(shifts), unroll=unroll),
        out_shape=jax.ShapeDtypeStruct((3, CELLS, SLOTS), F32),
        in_specs=[VMEM] * len(wides),
        out_specs=VMEM,
        scratch_shapes=[pltpu.VMEM((6, rows + 8, CELLS), F32), pltpu.VMEM((6, SLOTS, CELLS), F32)],
        compiler_params=params(),
        cost_estimate=pl.CostEstimate(flops=70 * pairs, bytes_accessed=1 << 20, transcendentals=0),
    )(*wides)


def ring(axis, step):
    count = lax.axis_size(axis)
    return [(i, (i + step) % count) for i in range(count)]


def body(positions, charges, types, counts, eps_type, sig_type):
    tab = tables()
    slot_last = lambda a: jnp.moveaxis(a, -4, -1).reshape(a.shape[:-4] + (CELLS, SLOTS))
    atoms, rows = pl.pallas_call(
        table_kernel,
        out_shape=(
            jax.ShapeDtypeStruct((6, SLOTS, CELLS), F32),
            jax.ShapeDtypeStruct((4, GROUPS, 128), F32),
        ),
        in_specs=[VMEM] * 4 + [SMEM] * 2,
        out_specs=(VMEM, VMEM),
        compiler_params=params(),
    )(
        slot_last(positions),
        slot_last(charges),
        slot_last(types),
        counts.reshape(1, CELLS),
        eps_type,
        sig_type,
    )
    right = lax.ppermute(atoms[:, :, CELLS - 32 :], "gx", ring("gx", 1))
    left = lax.ppermute(atoms[:, :, :32], "gx", ring("gx", -1))

    spread = pl.pallas_call(
        spread_kernel,
        out_shape=jax.ShapeDtypeStruct((LZ, BLOCK), F32),
        in_specs=[VMEM] * 3,
        out_specs=VMEM,
        scratch_shapes=[pltpu.VMEM((BY, 40, LZ), F32), pltpu.VMEM((BLOCK, LZ), F32)],
        compiler_params=params(),
    )(rows, *tab["tz"])
    lines = lax.all_to_all(spread, ("gx", "gy"), split_axis=0, concat_axis=0, tiled=True)

    wide = jnp.concatenate([right, atoms, left], axis=2)
    below = lax.ppermute(wide, "gy", ring("gy", 1))
    above = lax.ppermute(wide, "gy", ring("gy", -1))
    near = pair_forces((wide,), [(a, 0) for a in (-1, 0, 1)])

    index = lax.axis_index("gx") * DY + lax.axis_index("gy")
    plane = lax.dynamic_index_in_dim(jnp.asarray(tab["plane"]), index, 0, keepdims=False)
    fields = pl.pallas_call(
        plane_kernel,
        out_shape=jax.ShapeDtypeStruct((DX * DY, 3 * BLOCK), F32),
        in_specs=[SMEM] + [VMEM] * 11,
        out_specs=VMEM,
        scratch_shapes=[pltpu.VMEM((DX, BY * DY, 128), F32)],
        compiler_params=params(),
    )(plane, lines, *tab["tx"], *tab["ty"], *tab["iy"], *tab["ix"], tab["kx2"], tab["ky2"])
    fields = lax.all_to_all(fields, ("gx", "gy"), split_axis=0, concat_axis=0, tiled=True)
    far = pair_forces((wide, above, below), [(a, b) for b in (-1, 1) for a in (-1, 0, 1)])

    mesh_force = pl.pallas_call(
        force_kernel,
        out_shape=jax.ShapeDtypeStruct((3, CELLS, SLOTS), F32),
        in_specs=[VMEM] * 5,
        out_specs=VMEM,
        scratch_shapes=[
            pltpu.VMEM((BLOCK, LZ), F32),
            pltpu.VMEM((3, BY, 40, LZ), F32),
            pltpu.VMEM((3, GROUPS, 128), F32),
        ],
        compiler_params=params(),
    )(fields, rows, *tab["tz"], tab["swap"])

    slot_first = lambda a: jnp.moveaxis(a.reshape(3, CX, CY, CZ, SLOTS), -1, 1)
    return slot_first(near + far), slot_first(mesh_force)


def solution(mesh):
    placed = (
        P(None, None, "gx", "gy", None),
        P(None, "gx", "gy", None),
        P(None, "gx", "gy", None),
        P("gx", "gy", None),
        P(),
        P(),
    )
    return jax.shard_map(
        body,
        mesh=mesh,
        in_specs=placed,
        out_specs=(P(None, None, "gx", "gy", None), P(None, None, "gx", "gy", None)),
        check_vma=False,
    )
```

```python
import functools
import math

import jax
import jax.numpy as jnp
import ml_dtypes
import numpy as np
from jax import lax
from jax.experimental import pallas as pl
from jax.experimental.pallas import tpu as pltpu
from jax.sharding import PartitionSpec as P

CELL = 8
GEWALD = 0.7
CUT = 64.0
F32 = jnp.float32
BF16 = jnp.bfloat16

SLOTS = 32
CX, CY, CZ = 4, 2, 16
CELLS = CX * CY * CZ
DX, DY = 8, 16
LX, LY, LZ = 256, 256, 128
BX, BY = CX * CELL + 4, CY * CELL + 4
BLOCK = 768
GROUPS = CELLS // 4
KZ = 48
KX = 64
VMEM = pl.BlockSpec(memory_space=pltpu.VMEM)
SMEM = pl.BlockSpec(memory_space=pltpu.SMEM)
ANY = pl.BlockSpec(memory_space=pl.ANY)


def params(mib=40):
    return pltpu.CompilerParams(vmem_limit_bytes=mib << 20)


def split(array):
    high = array.astype(ml_dtypes.bfloat16)
    low = (array - high.astype(np.float64)).astype(ml_dtypes.bfloat16)
    return high, low


def left_parts(array):
    high, low = split(array)
    return np.concatenate([high, high, low], axis=-1)


def right_parts(array):
    high, low = split(array)
    return np.concatenate([high, low, high], axis=-2)


def basis(length):
    half = length // 2
    modes = np.concatenate([np.arange(half + 1), np.arange(1, half)])
    sines = np.arange(length) > half
    return modes, sines


def wave(points, modes, sines, length):
    angle = 2.0 * np.pi * (np.outer(modes, points) % length) / length
    return np.where(sines[:, None], np.sin(angle), np.cos(angle))


def wave_slope(points, modes, sines, length):
    angle = 2.0 * np.pi * (np.outer(modes, points) % length) / length
    k = 2.0 * np.pi * modes / length
    k = np.where(modes == length // 2, 0.0, k)[:, None]
    return np.where(sines[:, None], -k * np.cos(angle), k * np.sin(angle))


def damping(modes, length):
    k = 2.0 * np.pi * modes / length
    return np.exp(-k * k / (4.0 * GEWALD * GEWALD)) / np.sinc(modes / length) ** 8


def norms(modes, length):
    return np.where((modes == 0) | (modes == length // 2), 1.0, 2.0) / length


@functools.cache
def tables():
    mz, sz = basis(LZ)
    tz = np.zeros((4, LZ, KZ))
    for zg in range(4):
        tz[zg, :, :36] = wave(32 * zg - 2 + np.arange(36), mz, sz, LZ)
    mx, sx = basis(LX)
    my, sy = basis(LY)
    tx = np.zeros((DX // 2, 128, LX))
    gain_x = damping(mx, LX) * norms(mx, LX)
    ix = np.zeros((2, LX, DX * BX))
    for gx in range(DX):
        points = gx * CX * CELL - 2 + np.arange(BX)
        at = KX * (gx % 2)
        tx[gx // 2, at : at + BX] = (wave(points, mx, sx, LX) * gain_x[:, None]).T
        ix[0, :, gx * BX : (gx + 1) * BX] = wave(points, mx, sx, LX)
        ix[1, :, gx * BX : (gx + 1) * BX] = wave_slope(points, mx, sx, LX)
    points = (np.arange(DY)[None, :] * CY * CELL - 2 + np.arange(BY)[:, None]).reshape(-1)
    gain_y = damping(my, LY) * norms(my, LY)
    ty = wave(points, my, sy, LY) * gain_y[:, None]
    iy = np.concatenate([wave(points, my, sy, LY).T, wave_slope(points, my, sy, LY).T])
    kx2 = ((2.0 * np.pi * mx / LX) ** 2).astype(np.float32)[None, :]
    ky2 = ((2.0 * np.pi * my / LY) ** 2).astype(np.float32)[:, None]
    kz = 2.0 * np.pi * mz / LZ
    plane = np.stack([kz * kz, 4.0 * np.pi * damping(mz, LZ) * norms(mz, LZ)], 1)
    half = LZ // 2
    swap = 2.0 * np.pi * np.arange(half) / LZ
    swap = np.concatenate([-swap, swap]).astype(np.float32)[None, :]
    return dict(
        tz=left_parts(tz),
        tx=right_parts(tx).reshape(-1, LX),
        ty=left_parts(ty),
        iy=left_parts(iy),
        ix=right_parts(np.concatenate([ix[0], ix[1]], axis=1)),
        kx2=kx2,
        ky2=np.broadcast_to(ky2, (LY, 128)).astype(np.float32),
        plane=plane.astype(np.float32),
        swap=swap,
    )


def halves(value):
    high = value.astype(BF16)
    return high, (value - high.astype(F32)).astype(BF16)


def left_split(value):
    high, low = halves(value)
    return jnp.concatenate([high, high, low], axis=1)


def right_split(value, axis=0):
    high, low = halves(value)
    return jnp.concatenate([high, low, high], axis=axis)


def dot(left, right, dims=((1,), (0,))):
    return lax.dot_general(left, right, (dims, ((), ())), preferred_element_type=F32)


def spline(offset):
    span = jnp.abs(offset)
    outer = jnp.maximum(2.0 - span, 0.0)
    inner = jnp.maximum(1.0 - span, 0.0)
    return (outer * outer * outer) * (1.0 / 6.0) - (inner * inner * inner) * (2.0 / 3.0)


def weights(rows_ref, tz_ref, col):
    point = (lax.broadcasted_iota(jnp.int32, (16, 128), 0) - 2).astype(F32)
    point_z = (lax.broadcasted_iota(jnp.int32, (KZ, 128), 0) - 2).astype(F32)
    shift = ((lax.broadcasted_iota(jnp.int32, (1, 128), 1) // SLOTS) * CELL).astype(F32)
    modes, edges = [], []
    for zg in range(4):
        row = [rows_ref[c, pl.ds(col * 4 + zg, 1), :] for c in range(4)]
        along_x = spline(row[0] - point)
        along_y = spline(row[1] - point) * row[3]
        along_z = spline(row[2] + shift - point_z)
        modes.append(dot(tz_ref[zg], right_split(along_z)))
        edges.append(jnp.concatenate([along_x, along_y], axis=0))
    return jnp.concatenate(modes, axis=1), jnp.concatenate(edges, axis=1)


def products(edges):
    return (edges[16:28][:, None, :] * edges[:16][None, :, :]).reshape(192, edges.shape[1])


def started(*copies):
    copies = [pltpu.make_async_copy(*copy) for copy in copies]
    for copy in copies:
        copy.start()
    return copies


def spread_kernel(*refs):
    sources, (atoms_out, spread_out, modes_out, edges_out) = refs[:7], refs[7:11]
    pos_ref, charge_ref, type_ref, count_ref, eps_ref, sig_ref, tz_ref = refs[11:18]
    atoms_ref, rows_ref, modes_ref, edges_ref, total, packed, turned, sems = refs[18:]
    incoming = started(*((s, t, sems.at[n]) for n, (s, t) in enumerate(zip(sources, refs[11:18]))))
    total[...] = jnp.zeros_like(total)
    for copy in incoming[:-1]:
        copy.wait()
    slots = lax.broadcasted_iota(jnp.int32, (SLOTS, CELLS), 0)
    counts = [count_ref[cx, cy : cy + 1, :] for cx in range(CX) for cy in range(CY)]
    occupied = slots < jnp.concatenate(counts, axis=1)
    kinds = type_ref[...].T
    eps = jnp.zeros((SLOTS, CELLS), F32)
    sig = jnp.zeros((SLOTS, CELLS), F32)
    for kind in range(eps_ref.shape[0]):
        match = kinds == kind
        eps = jnp.where(match, eps_ref[kind], eps)
        sig = jnp.where(match, sig_ref[kind], sig)
    charge = jnp.where(occupied, charge_ref[...].T, 0.0)
    for d in range(3):
        atoms_ref[d] = pos_ref[d].T
    atoms_ref[3] = charge
    atoms_ref[4] = jnp.where(occupied, jnp.sqrt(eps), 0.0)
    atoms_ref[5] = sig
    outgoing = started((atoms_ref, atoms_out, sems.at[7]))
    charge = charge.T
    for c in range(4):
        value = pos_ref[c] if c < 3 else charge
        value = value.reshape(GROUPS, 4, SLOTS)
        rows_ref[c] = jnp.concatenate([value[:, s, :] for s in range(4)], axis=1)
    incoming[-1].wait()

    def column(col, carry):
        modes, edges = weights(rows_ref, tz_ref, col)
        edges_ref[col] = edges
        high, low = halves(modes)
        modes_ref[col] = jnp.concatenate([high, low, high], axis=0)
        started((modes_ref.at[col], modes_out.at[col], sems.at[10 + col]))
        modes = jnp.concatenate([high, low, high], axis=1)
        part = dot(left_split(products(edges)), modes, ((1,), (1,))).reshape(12, 16, LZ)
        y = (col % CY) * CELL
        x = pl.multiple_of((col // CY) * CELL, CELL)
        total[pl.ds(y, 12), pl.ds(x, 16), :] += part
        return carry

    lax.fori_loop(0, CX * CY, column, 0, unroll=2)
    outgoing += started((edges_ref, edges_out, sems.at[8]))
    for y in range(BY):
        packed[y * BX : (y + 1) * BX, :] = total[y, :BX, :]
    packed[BX * BY :, :] = jnp.zeros((BLOCK - BX * BY, LZ), F32)
    turned[...] = packed[...].T
    outgoing += started((turned, spread_out.at[:, 0, :], sems.at[9]))
    for copy in outgoing:
        copy.wait()
    for col in range(CX * CY):
        pltpu.make_async_copy(modes_ref.at[col], modes_out.at[col], sems.at[10 + col]).wait()


def plane_kernel(plane_ref, in_ref, *refs):
    sources, out_ref, held = refs[:6], refs[6], refs[7:13]
    lines, stacked, turned, sems = refs[13:]
    tx, ty, iy, ix, kx2, ky2 = held
    (arrival,) = started((in_ref.at[:, 0, :], lines, sems.at[3]))
    constants = started(*((s, t, sems.at[4 + n]) for n, (s, t) in enumerate(zip(sources, held))))
    arrival.wait()
    for y in range(BY):
        value = lines[:, y * BX : y * BX + KX]
        for gx in range(DX):
            at = KX * (gx % 2)
            stacked[gx // 2, y * DY : (y + 1) * DY, at : at + KX] = value[gx * DY : (gx + 1) * DY]
    pairs = jnp.concatenate([left_split(stacked[n]) for n in range(DX // 2)], axis=1)
    for copy in constants:
        copy.wait()
    modes = dot(ty[...], right_split(dot(pairs, tx[...])))
    k2 = kx2[...] + jnp.concatenate([ky2[...], ky2[...]], axis=1) + plane_ref[0]
    positive = k2 > 0.0
    modes = jnp.where(positive, modes * (plane_ref[1] / jnp.where(positive, k2, 1.0)), 0.0)
    both = dot(iy[...], right_split(modes))
    rows = BY * DY
    width = DX * BX
    plain = dot(left_split(both[:rows]), ix[...])
    slope = dot(left_split(both[rows:]), ix[:, :width])
    fields = (plain[:, width:], slope, plain[:, :width])
    outgoing = []
    for d in range(3):
        turned[d, :, BX * BY :] = jnp.zeros((DX * DY, BLOCK - BX * BY), F32)
        for gx in range(DX):
            piece = fields[d][:, gx * BX : (gx + 1) * BX]
            for y in range(BY):
                lane = y * BX
                turned[d, gx * DY : (gx + 1) * DY, lane : lane + BX] = piece[y * DY : (y + 1) * DY]
        outgoing += started(
            (turned.at[d], out_ref.at[:, 0, d * BLOCK : (d + 1) * BLOCK], sems.at[d])
        )
    for copy in outgoing:
        copy.wait()


def force_kernel(in_ref, *refs):
    sources, out_ref, held = refs[:3], refs[3], refs[4:7]
    turned, packed, padded, rows_out, sems = refs[7:]
    modes_ref, edges_ref, swap_ref = held
    incoming = started(
        *(
            (in_ref.at[:, 0, d * BLOCK : (d + 1) * BLOCK], turned.at[d], sems.at[d])
            for d in range(3)
        )
    )
    kept = started(*((s, t, sems.at[3 + n]) for n, (s, t) in enumerate(zip(sources, held))))
    kept[2].wait()
    for d in range(3):
        incoming[d].wait()
        value = turned[d].T
        if d == 2:
            value = pltpu.roll(value, LZ // 2, 1) * swap_ref[...]
        packed[...] = value
        for y in range(BY):
            padded[d, y, :BX, :] = packed[y * BX : (y + 1) * BX, :]
            padded[d, y, BX:, :] = jnp.zeros((40 - BX, LZ), F32)
    kept[0].wait()
    kept[1].wait()

    def column(col, carry):
        y = (col % CY) * CELL
        x = pl.multiple_of((col // CY) * CELL, CELL)
        planes = products(edges_ref[col])
        for d in range(3):
            block = padded[d, pl.ds(y, 12), pl.ds(x, 16), :].reshape(192, LZ)
            along = dot(left_split(block), modes_ref[col])
            force = jnp.sum(along * planes, axis=0, keepdims=True)
            for zg in range(4):
                rows_out[d, pl.ds(col * 4 + zg, 1), :] = force[:, 128 * zg : 128 * (zg + 1)]
        return carry

    lax.fori_loop(0, CX * CY, column, 0, unroll=2)
    for d in range(3):
        value = rows_out[d]
        pieces = [value[:, s * SLOTS : (s + 1) * SLOTS][:, None, :] for s in range(4)]
        out_ref[d] = jnp.concatenate(pieces, axis=1).reshape(CELLS, SLOTS)


COULOMB = (
    -0.006157896808528851,
    -0.00037761534771162467,
    0.4246826287075061,
    -0.032594054879277516,
    0.5289809248435148,
    -0.3643412334667553,
    0.147196623703603,
    -0.012411731315994238,
    -0.015640759195296648,
    0.00499632789350256,
)
SCALES = (0.125, 0.125, 0.125, 1.0, 1.0, 0.0625)


def pair_term(own, other):
    dx = other[0] - own[0]
    dy = other[1] - own[1]
    dz = other[2] - own[2]
    r2 = dx * dx + dy * dy + dz * dz
    fade = jnp.maximum(1.0 - r2, 0.0)
    t = lax.rsqrt(r2 + 1.0 / CUT)
    decay = jnp.exp2(r2 * (-0.49 * CUT * math.log2(math.e)))
    scale = -16.0 * math.exp(-0.49)
    terms = [scale * c * 0.125**n for n, c in enumerate(COULOMB)]
    poly = terms[-1] * t + terms[-2]
    for c in terms[-3::-1]:
        poly = poly * t + c
    sigma = own[5] + other[5]
    square = sigma * sigma
    inverse = 1.0 / (r2 + square)
    x = square * inverse
    x3 = x * x * x
    rest = 1.0 - (x3 + x3)
    lj = x3 * (rest * ((fade * inverse) * 3.0 + 1.0) + 1.0)
    w = fade * ((own[4] * other[4]) * lj + (own[3] * other[3]) * (decay * poly))
    return w * dx, w * dy, w * dz


def pair_kernel(*refs, shifts, unroll, begun):
    wide_refs = refs[begun:-3]
    out_ref, others, own = refs[-3:]
    low = (lax.broadcasted_iota(jnp.int32, (SLOTS, 256), 1) & CZ) == 0
    at_z = lax.broadcasted_iota(jnp.int32, (SLOTS, CELLS), 1) & (CZ - 1)
    for c in range(6):
        wides = []
        for ref in wide_refs:
            value = ref[c] * SCALES[c]
            wides.append(jnp.concatenate([value, jnp.zeros((SLOTS, 64), F32)], axis=1))
        own[c] = wides[0][:, 32:160]
        layers = {0: wides[0]}
        if len(wides) > 1:
            above, below = wides[1:]
            layers[1] = jnp.where(
                low, pltpu.roll(wides[0], 256 - CZ, 1), pltpu.roll(above, CZ, 1)
            )
            layers[-1] = jnp.where(
                low, pltpu.roll(below, 256 - CZ, 1), pltpu.roll(wides[0], CZ, 1)
            )
        for n, (a, b) in enumerate(shifts):
            value = layers[b][:, 32 * (a + 1) : 32 * (a + 1) + CELLS]
            if c == 0:
                value = value + float(a)
            if c == 1:
                value = value + float(b)
            up = jnp.where(
                at_z == CZ - 1, pltpu.roll(value, CZ - 1, 1), pltpu.roll(value, CELLS - 1, 1)
            )
            down = jnp.where(at_z == 0, pltpu.roll(value, CELLS - CZ + 1, 1), pltpu.roll(value, 1, 1))
            if c == 2:
                up = up + 1.0
                down = down - 1.0
            for m, part in enumerate((down, value, up)):
                row = (n * 3 + m) * SLOTS
                others[c, row : row + SLOTS] = part

    def step(n, sums):
        sums = list(sums)
        for jj in range(unroll):
            j = n * unroll + jj
            other = [others[c, pl.ds(j, 8, stride=0), :] for c in range(6)]
            for block in range(4):
                mine = [own[c, 8 * block : 8 * block + 8, :] for c in range(6)]
                force = pair_term(mine, other)
                for d in range(3):
                    sums[block * 3 + d] = sums[block * 3 + d] + force[d]
        return tuple(sums)

    zero = jnp.zeros((8, CELLS), F32)
    steps = len(shifts) * 3 * SLOTS // unroll
    sums = lax.fori_loop(0, steps, step, (zero,) * 12)
    for d in range(3):
        force = jnp.concatenate([sums[block * 3 + d] for block in range(4)], axis=0).T
        out_ref[d] = refs[0][d] + force if begun else force


def pair_forces(wides, shifts, start=(), unroll=4):
    rows = len(shifts) * 3 * SLOTS
    pairs = rows * SLOTS * CELLS
    return pl.pallas_call(
        functools.partial(pair_kernel, shifts=tuple(shifts), unroll=unroll, begun=len(start)),
        out_shape=jax.ShapeDtypeStruct((3, CELLS, SLOTS), F32),
        in_specs=[VMEM] * (len(start) + len(wides)),
        out_specs=VMEM,
        scratch_shapes=[pltpu.VMEM((6, rows + 8, CELLS), F32), pltpu.VMEM((6, SLOTS, CELLS), F32)],
        compiler_params=params(8),
        cost_estimate=pl.CostEstimate(flops=70 * pairs, bytes_accessed=1 << 20, transcendentals=0),
    )(*start, *wides)


def ring(axis, step):
    count = lax.axis_size(axis)
    return [(i, (i + step) % count) for i in range(count)]


def body(positions, charges, types, counts, eps_type, sig_type):
    tab = tables()
    slot_last = lambda a: jnp.moveaxis(a, -4, -1).reshape(a.shape[:-4] + (CELLS, SLOTS))
    atoms, spread, modes, edges = pl.pallas_call(
        spread_kernel,
        out_shape=(
            jax.ShapeDtypeStruct((6, SLOTS, CELLS), F32),
            jax.ShapeDtypeStruct((LZ, 1, BLOCK), F32),
            jax.ShapeDtypeStruct((CX * CY, 3 * LZ, 512), BF16),
            jax.ShapeDtypeStruct((CX * CY, 32, 512), F32),
        ),
        in_specs=[ANY] * 7,
        out_specs=(ANY,) * 4,
        scratch_shapes=[
            pltpu.VMEM((3, CELLS, SLOTS), F32),
            pltpu.VMEM((CELLS, SLOTS), F32),
            pltpu.VMEM((CELLS, SLOTS), jnp.int32),
            pltpu.VMEM((CX, CY, CZ), jnp.int32),
            pltpu.SMEM(eps_type.shape, F32),
            pltpu.SMEM(sig_type.shape, F32),
            pltpu.VMEM(tab["tz"].shape, BF16),
            pltpu.VMEM((6, SLOTS, CELLS), F32),
            pltpu.VMEM((4, GROUPS, 128), F32),
            pltpu.VMEM((CX * CY, 3 * LZ, 512), BF16),
            pltpu.VMEM((CX * CY, 32, 512), F32),
            pltpu.VMEM((BY, 40, LZ), F32),
            pltpu.VMEM((BLOCK, LZ), F32),
            pltpu.VMEM((LZ, BLOCK), F32),
            pltpu.SemaphoreType.DMA((10 + CX * CY,)),
        ],
        compiler_params=params(56),
    )(
        slot_last(positions),
        slot_last(charges),
        slot_last(types),
        counts,
        eps_type,
        sig_type,
        tab["tz"],
    )
    before = lax.ppermute(atoms[:, :, CELLS - 32 :], "gx", ring("gx", 1))
    after = lax.ppermute(atoms[:, :, :32], "gx", ring("gx", -1))
    lines = lax.all_to_all(spread, ("gx", "gy"), split_axis=0, concat_axis=0, tiled=True)

    wide = jnp.concatenate([before, atoms, after], axis=2)
    below = lax.ppermute(wide, "gy", ring("gy", 1))
    above = lax.ppermute(wide, "gy", ring("gy", -1))
    near = pair_forces((wide,), [(a, 0) for a in (-1, 0, 1)])
    lines, near, below, above = lax.optimization_barrier((lines, near, below, above))

    index = lax.axis_index("gx") * DY + lax.axis_index("gy")
    plane = lax.dynamic_index_in_dim(jnp.asarray(tab["plane"]), index, 0, keepdims=False)
    fields = pl.pallas_call(
        plane_kernel,
        out_shape=jax.ShapeDtypeStruct((DX * DY, 1, 3 * BLOCK), F32),
        in_specs=[SMEM] + [ANY] * 7,
        out_specs=ANY,
        scratch_shapes=[
            *(pltpu.VMEM(tab[name].shape, BF16) for name in ("tx", "ty", "iy", "ix")),
            *(pltpu.VMEM(tab[name].shape, F32) for name in ("kx2", "ky2")),
            pltpu.VMEM((DX * DY, BLOCK), F32),
            pltpu.VMEM((DX // 2, BY * DY, 128), F32),
            pltpu.VMEM((3, DX * DY, BLOCK), F32),
            pltpu.SemaphoreType.DMA((10,)),
        ],
        compiler_params=params(56),
    )(plane, lines, tab["tx"], tab["ty"], tab["iy"], tab["ix"], tab["kx2"], tab["ky2"])
    fields = lax.all_to_all(fields, ("gx", "gy"), split_axis=0, concat_axis=0, tiled=True)
    far = pair_forces(
        (wide, above, below), [(a, b) for b in (-1, 1) for a in (-1, 0, 1)], (near,)
    )
    fields, far = lax.optimization_barrier((fields, far))

    mesh_force = pl.pallas_call(
        force_kernel,
        out_shape=jax.ShapeDtypeStruct((3, CELLS, SLOTS), F32),
        in_specs=[ANY] * 4,
        out_specs=VMEM,
        scratch_shapes=[
            pltpu.VMEM((CX * CY, 3 * LZ, 512), BF16),
            pltpu.VMEM((CX * CY, 32, 512), F32),
            pltpu.VMEM((1, LZ), F32),
            pltpu.VMEM((3, LZ, BLOCK), F32),
            pltpu.VMEM((BLOCK, LZ), F32),
            pltpu.VMEM((3, BY, 40, LZ), F32),
            pltpu.VMEM((3, GROUPS, 128), F32),
            pltpu.SemaphoreType.DMA((6,)),
        ],
        compiler_params=params(56),
    )(fields, modes, edges, tab["swap"])

    slot_first = lambda a: jnp.moveaxis(a.reshape(3, CX, CY, CZ, SLOTS), -1, 1)
    return slot_first(far), slot_first(mesh_force)


def solution(mesh):
    placed = (
        P(None, None, "gx", "gy", None),
        P(None, "gx", "gy", None),
        P(None, "gx", "gy", None),
        P("gx", "gy", None),
        P(),
        P(),
    )
    return jax.shard_map(
        body,
        mesh=mesh,
        in_specs=placed,
        out_specs=(P(None, None, "gx", "gy", None), P(None, None, "gx", "gy", None)),
        check_vma=False,
    )
```

```python
import functools
import math

import jax
import jax.numpy as jnp
import ml_dtypes
import numpy as np
from jax import lax
from jax.experimental import pallas as pl
from jax.experimental.pallas import tpu as pltpu
from jax.sharding import PartitionSpec as P

CELL = 8
GEWALD = 0.7
CUT = 64.0
F32 = jnp.float32
BF16 = jnp.bfloat16

SLOTS = 32
CX, CY, CZ = 4, 2, 16
CELLS = CX * CY * CZ
COLUMNS = CY * CZ
DX, DY = 8, 16
LX, LY, LZ = 256, 256, 128
BX, BY = CX * CELL + 4, CY * CELL + 4
BLOCK = 768
GROUPS = CELLS // 4
KZ = 48
KX = 64
LENGTH = math.sqrt(GEWALD * GEWALD * math.log2(math.e))
FAR = CUT * LENGTH * LENGTH
SCALES = (LENGTH, LENGTH, LENGTH, 1.0, 1.0 / math.sqrt(8.0 * FAR * LENGTH), 0.5 * LENGTH)
VMEM = pl.BlockSpec(memory_space=pltpu.VMEM)
SMEM = pl.BlockSpec(memory_space=pltpu.SMEM)
ANY = pl.BlockSpec(memory_space=pl.ANY)


def params(mib=40):
    return pltpu.CompilerParams(vmem_limit_bytes=mib << 20)


def split(array):
    high = array.astype(ml_dtypes.bfloat16)
    low = (array - high.astype(np.float64)).astype(ml_dtypes.bfloat16)
    return high, low


def left_parts(array):
    high, low = split(array)
    return np.concatenate([high, high, low], axis=-1)


def right_parts(array):
    high, low = split(array)
    return np.concatenate([high, low, high], axis=-2)


def basis(length):
    half = length // 2
    modes = np.concatenate([np.arange(half + 1), np.arange(1, half)])
    sines = np.arange(length) > half
    return modes, sines


def wave(points, modes, sines, length):
    angle = 2.0 * np.pi * (np.outer(modes, points) % length) / length
    return np.where(sines[:, None], np.sin(angle), np.cos(angle))


def wave_slope(points, modes, sines, length):
    angle = 2.0 * np.pi * (np.outer(modes, points) % length) / length
    k = 2.0 * np.pi * modes / length
    k = np.where(modes == length // 2, 0.0, k)[:, None]
    return np.where(sines[:, None], -k * np.cos(angle), k * np.sin(angle))


def damping(modes, length):
    k = 2.0 * np.pi * modes / length
    return np.exp(-k * k / (4.0 * GEWALD * GEWALD)) / np.sinc(modes / length) ** 8


def norms(modes, length):
    return np.where((modes == 0) | (modes == length // 2), 1.0, 2.0) / length


@functools.cache
def tables():
    mz, sz = basis(LZ)
    tz = np.zeros((4, LZ, KZ))
    for zg in range(4):
        tz[zg, :, :36] = wave(32 * zg - 2 + np.arange(36), mz, sz, LZ)
    mx, sx = basis(LX)
    my, sy = basis(LY)
    tx = np.zeros((DX // 2, 128, LX))
    gain_x = damping(mx, LX) * norms(mx, LX)
    ix = np.zeros((2, LX, DX * BX))
    for gx in range(DX):
        points = gx * CX * CELL - 2 + np.arange(BX)
        at = KX * (gx % 2)
        tx[gx // 2, at : at + BX] = (wave(points, mx, sx, LX) * gain_x[:, None]).T
        ix[0, :, gx * BX : (gx + 1) * BX] = wave(points, mx, sx, LX)
        ix[1, :, gx * BX : (gx + 1) * BX] = wave_slope(points, mx, sx, LX)
    points = (np.arange(DY)[None, :] * CY * CELL - 2 + np.arange(BY)[:, None]).reshape(-1)
    gain_y = damping(my, LY) * norms(my, LY)
    ty = wave(points, my, sy, LY) * gain_y[:, None]
    iy = np.concatenate([wave(points, my, sy, LY).T, wave_slope(points, my, sy, LY).T])
    kx2 = ((2.0 * np.pi * mx / LX) ** 2).astype(np.float32)[None, :]
    ky2 = ((2.0 * np.pi * my / LY) ** 2).astype(np.float32)[:, None]
    kz = 2.0 * np.pi * mz / LZ
    plane = np.stack([kz * kz, 4.0 * np.pi * damping(mz, LZ) * norms(mz, LZ)], 1)
    half = LZ // 2
    swap = 2.0 * np.pi * np.arange(half) / LZ
    swap = np.concatenate([-swap, swap]).astype(np.float32)[None, :]
    return dict(
        tz=left_parts(tz),
        tx=right_parts(tx).reshape(-1, LX),
        ty=left_parts(ty),
        iy=left_parts(iy),
        ix=right_parts(np.concatenate([ix[0], ix[1]], axis=1)),
        kx2=kx2,
        ky2=np.broadcast_to(ky2, (LY, 128)).astype(np.float32),
        plane=plane.astype(np.float32),
        swap=swap,
    )


def halves(value):
    high = value.astype(BF16)
    return high, (value - high.astype(F32)).astype(BF16)


def left_split(value):
    high, low = halves(value)
    return jnp.concatenate([high, high, low], axis=1)


def right_split(value, axis=0):
    high, low = halves(value)
    return jnp.concatenate([high, low, high], axis=axis)


def dot(left, right, dims=((1,), (0,))):
    return lax.dot_general(left, right, (dims, ((), ())), preferred_element_type=F32)


def spline(offset):
    span = jnp.abs(offset)
    outer = jnp.maximum(2.0 - span, 0.0)
    inner = jnp.maximum(1.0 - span, 0.0)
    return (outer * outer * outer) * (1.0 / 6.0) - (inner * inner * inner) * (2.0 / 3.0)


def weights(rows_ref, tz_ref, col):
    point = (lax.broadcasted_iota(jnp.int32, (16, 128), 0) - 2).astype(F32)
    point_z = (lax.broadcasted_iota(jnp.int32, (KZ, 128), 0) - 2).astype(F32)
    shift = ((lax.broadcasted_iota(jnp.int32, (1, 128), 1) // SLOTS) * CELL).astype(F32)
    modes, edges = [], []
    for zg in range(4):
        row = [rows_ref[c, pl.ds(col * 4 + zg, 1), :] for c in range(4)]
        along_x = spline(row[0] - point)
        along_y = spline(row[1] - point) * row[3]
        along_z = spline(row[2] + shift - point_z)
        modes.append(dot(tz_ref[zg], right_split(along_z)))
        edges.append(jnp.concatenate([along_x, along_y], axis=0))
    return jnp.concatenate(modes, axis=1), jnp.concatenate(edges, axis=1)


def products(edges):
    return (edges[16:28][:, None, :] * edges[:16][None, :, :]).reshape(192, edges.shape[1])


def started(*copies):
    copies = [pltpu.make_async_copy(*copy) for copy in copies]
    for copy in copies:
        copy.start()
    return copies


def table_kernel(*refs):
    sources, (atoms_ref, first_ref, last_ref, rows_ref, tz_ref) = refs[:7], refs[7:12]
    pos_ref, charge_ref, type_ref, count_ref, eps_ref, sig_ref, sems = refs[12:]
    targets = refs[12:18] + (tz_ref,)
    incoming = started(*((s, t, sems.at[n]) for n, (s, t) in enumerate(zip(sources, targets))))
    for copy in incoming[:-1]:
        copy.wait()
    slots = lax.broadcasted_iota(jnp.int32, (SLOTS, CELLS), 0)
    counts = [count_ref[cx, cy : cy + 1, :] for cx in range(CX) for cy in range(CY)]
    occupied = slots < jnp.concatenate(counts, axis=1)
    kinds = type_ref[...].T
    eps = jnp.zeros((SLOTS, CELLS), F32)
    sig = jnp.zeros((SLOTS, CELLS), F32)
    for kind in range(eps_ref.shape[0]):
        match = kinds == kind
        eps = jnp.where(match, eps_ref[kind], eps)
        sig = jnp.where(match, sig_ref[kind], sig)
    charge = jnp.where(occupied, charge_ref[...].T, 0.0)
    root = jnp.where(occupied, jnp.sqrt(eps), 0.0)
    for c, value in enumerate([pos_ref[d].T for d in range(3)] + [charge, root, sig]):
        value = value * SCALES[c]
        atoms_ref[c] = value
        first_ref[c] = value[:, :COLUMNS]
        last_ref[c] = value[:, CELLS - COLUMNS :]
    charge = charge.T
    for c in range(4):
        value = pos_ref[c] if c < 3 else charge
        value = value.reshape(GROUPS, 4, SLOTS)
        rows_ref[c] = jnp.concatenate([value[:, s, :] for s in range(4)], axis=1)
    incoming[-1].wait()


def spread_kernel(
    rows_ref, tz_ref, spread_out, modes_ref, edges_out, total, packed, turned, edges_ref, sems
):
    total[...] = jnp.zeros_like(total)

    def column(col, carry):
        modes, edges = weights(rows_ref, tz_ref, col)
        edges_ref[col] = edges
        high, low = halves(modes)
        modes_ref[col] = jnp.concatenate([high, low, high], axis=0)
        modes = jnp.concatenate([high, low, high], axis=1)
        part = dot(left_split(products(edges)), modes, ((1,), (1,))).reshape(12, 16, LZ)
        y = (col % CY) * CELL
        x = pl.multiple_of((col // CY) * CELL, CELL)
        total[pl.ds(y, 12), pl.ds(x, 16), :] += part
        return carry

    lax.fori_loop(0, CX * CY, column, 0, unroll=2)
    outgoing = started((edges_ref, edges_out, sems.at[0]))
    for y in range(BY):
        packed[y * BX : (y + 1) * BX, :] = total[y, :BX, :]
    packed[BX * BY :, :] = jnp.zeros((BLOCK - BX * BY, LZ), F32)
    turned[...] = packed[...].T
    outgoing += started((turned, spread_out.at[:, 0, :], sems.at[1]))
    for copy in outgoing:
        copy.wait()


def plane_kernel(plane_ref, in_ref, *refs):
    sources, out_ref, held = refs[:6], refs[6], refs[7:13]
    lines, stacked, turned, sems = refs[13:]
    tx, ty, iy, ix, kx2, ky2 = held
    (arrival,) = started((in_ref.at[:, 0, :], lines, sems.at[3]))
    constants = started(*((s, t, sems.at[4 + n]) for n, (s, t) in enumerate(zip(sources, held))))
    arrival.wait()
    for y in range(BY):
        value = lines[:, y * BX : y * BX + KX]
        for gx in range(DX):
            at = KX * (gx % 2)
            stacked[gx // 2, y * DY : (y + 1) * DY, at : at + KX] = value[gx * DY : (gx + 1) * DY]
    pairs = jnp.concatenate([left_split(stacked[n]) for n in range(DX // 2)], axis=1)
    for copy in constants:
        copy.wait()
    modes = dot(ty[...], right_split(dot(pairs, tx[...])))
    k2 = kx2[...] + jnp.concatenate([ky2[...], ky2[...]], axis=1) + plane_ref[0]
    positive = k2 > 0.0
    modes = jnp.where(positive, modes * (plane_ref[1] / jnp.where(positive, k2, 1.0)), 0.0)
    both = dot(iy[...], right_split(modes))
    rows = BY * DY
    width = DX * BX
    plain = dot(left_split(both[:rows]), ix[...])
    slope = dot(left_split(both[rows:]), ix[:, :width])
    fields = (plain[:, width:], slope, plain[:, :width])
    outgoing = []
    for d in range(3):
        turned[d, :, BX * BY :] = jnp.zeros((DX * DY, BLOCK - BX * BY), F32)
        for gx in range(DX):
            piece = fields[d][:, gx * BX : (gx + 1) * BX]
            for y in range(BY):
                lane = y * BX
                turned[d, gx * DY : (gx + 1) * DY, lane : lane + BX] = piece[y * DY : (y + 1) * DY]
        outgoing += started(
            (turned.at[d], out_ref.at[:, 0, d * BLOCK : (d + 1) * BLOCK], sems.at[d])
        )
    for copy in outgoing:
        copy.wait()


def force_kernel(
    in_ref, modes_ref, edges, swap_ref, out_ref, turned, packed, padded, rows_out, edges_ref, sems
):
    (kept,) = started((edges, edges_ref, sems.at[3]))
    incoming = started(
        *(
            (in_ref.at[:, 0, d * BLOCK : (d + 1) * BLOCK], turned.at[d], sems.at[d])
            for d in range(3)
        )
    )
    for d in range(3):
        incoming[d].wait()
        value = turned[d].T
        if d == 2:
            value = pltpu.roll(value, LZ // 2, 1) * swap_ref[...]
        packed[...] = value
        for y in range(BY):
            padded[d, y, :BX, :] = packed[y * BX : (y + 1) * BX, :]
            padded[d, y, BX:, :] = jnp.zeros((40 - BX, LZ), F32)
    kept.wait()

    def column(col, carry):
        y = (col % CY) * CELL
        x = pl.multiple_of((col // CY) * CELL, CELL)
        planes = products(edges_ref[col])
        for d in range(3):
            block = padded[d, pl.ds(y, 12), pl.ds(x, 16), :].reshape(192, LZ)
            along = dot(left_split(block), modes_ref[col])
            force = jnp.sum(along * planes, axis=0, keepdims=True)
            for zg in range(4):
                rows_out[d, pl.ds(col * 4 + zg, 1), :] = force[:, 128 * zg : 128 * (zg + 1)]
        return carry

    lax.fori_loop(0, CX * CY, column, 0, unroll=2)
    for d in range(3):
        value = rows_out[d]
        pieces = [value[:, s * SLOTS : (s + 1) * SLOTS][:, None, :] for s in range(4)]
        out_ref[d] = jnp.concatenate(pieces, axis=1).reshape(CELLS, SLOTS)


COULOMB = (
    -0.006156452396320011,
    -0.0004198503476764426,
    0.4251962050951751,
    -0.035971568956237085,
    0.5422242920959217,
    -0.3965913855606964,
    0.1962617265017834,
    -0.05766279059061346,
    0.007452967624700701,
)


def pair_term(own, other):
    dx = other[0] - own[0]
    dy = other[1] - own[1]
    dz = other[2] - own[2]
    r2 = dx * dx + dy * dy + dz * dz
    gap = FAR - r2
    fade = jnp.maximum(gap, 0.0)
    t = lax.rsqrt(r2 + LENGTH * LENGTH)
    scale = -2.0 * math.exp(-GEWALD * GEWALD) * 2.0**-FAR / (FAR * LENGTH)
    terms = [scale * c * LENGTH**n for n, c in enumerate(COULOMB)]
    poly = terms[-1] * t + terms[-2]
    for c in terms[-3::-1]:
        poly = poly * t + c
    sigma = own[5] + other[5]
    square = sigma * sigma
    inverse = 1.0 / (r2 + square)
    x = square * inverse
    x3 = x * x * x
    rest = 1.0 - (x3 + x3)
    lj = x3 * (rest * ((fade * inverse) * 3.0 + 1.0) + 1.0)
    w = fade * ((own[4] * other[4]) * lj + (own[3] * other[3]) * (jnp.exp2(gap) * poly))
    return w * dx, w * dy, w * dz


def shifted_z(value, at_z, step):
    if step == 0:
        return value
    if step > 0:
        return jnp.where(
            at_z == CZ - 1, pltpu.roll(value, CZ - 1, 1), pltpu.roll(value, CELLS - 1, 1)
        )
    return jnp.where(at_z == 0, pltpu.roll(value, CELLS - CZ + 1, 1), pltpu.roll(value, 1, 1))


def pair_kernel(*refs, passes, single, sources, unroll):
    blocks, outs = refs[:sources], refs[sources:-3]
    others, own, back = refs[-3:]
    low = (lax.broadcasted_iota(jnp.int32, (SLOTS, 256), 1) & CZ) == 0
    at_z = lax.broadcasted_iota(jnp.int32, (SLOTS, CELLS), 1) & (CZ - 1)
    empty = jnp.zeros((SLOTS, 64), F32)
    for c in range(6):
        wide = jnp.concatenate([blocks[1][c], blocks[0][c], blocks[2][c], empty], axis=1)
        own[c] = blocks[0][c]
        layers = {0: wide}
        if sources > 3:
            above = jnp.concatenate([blocks[4][c], blocks[3][c], blocks[5][c], empty], axis=1)
            layers[1] = jnp.where(low, pltpu.roll(wide, 256 - CZ, 1), pltpu.roll(above, CZ, 1))
        for n, offset in enumerate(passes):
            at = COLUMNS * (offset[0] + 1)
            value = layers[offset[1]][:, at : at + CELLS]
            value = shifted_z(value, at_z, offset[2])
            others[c, n * SLOTS : (n + 1) * SLOTS] = (
                value + offset[c] * CELL * LENGTH if c < 3 else value
            )

    def step(n, sums, reverse):
        sums = list(sums)
        for jj in range(unroll):
            j = n * unroll + jj
            other = [others[c, pl.ds(j, 8, stride=0), :] for c in range(6)]
            total = [None] * 3
            for block in range(4):
                mine = [own[c, 8 * block : 8 * block + 8, :] for c in range(6)]
                force = pair_term(mine, other)
                for d in range(3):
                    sums[block * 3 + d] = sums[block * 3 + d] + force[d]
                    total[d] = force[d] if block == 0 else total[d] + force[d]
            if reverse:
                for d in range(3):
                    back[d, pl.ds(pl.multiple_of((j - single * SLOTS) * 8, 8), 8), :] = total[d]
        return tuple(sums)

    per = SLOTS // unroll
    sums = (jnp.zeros((8, CELLS), F32),) * 12
    sums = lax.fori_loop(0, single * per, functools.partial(step, reverse=False), sums)
    sums = lax.fori_loop(
        single * per, len(passes) * per, functools.partial(step, reverse=True), sums
    )
    nothing = jnp.zeros((SLOTS, 128), F32)
    for d in range(3):
        force = jnp.concatenate([sums[block * 3 + d] for block in range(4)], axis=0)
        here = pltpu.roll(jnp.concatenate([force, nothing], axis=1), COLUMNS, 1)
        there = jnp.zeros((SLOTS, 256), F32)
        for n, offset in enumerate(passes):
            if n < single:
                continue
            base = (n - single) * SLOTS * 8
            value = back[d, pl.ds(base, SLOTS, stride=8), :]
            for s in range(1, 8):
                value = value + back[d, pl.ds(base + s, SLOTS, stride=8), :]
            value = shifted_z(value, at_z, -offset[2])
            value = jnp.concatenate([value, nothing], axis=1)
            at = COLUMNS * (offset[0] + 1)
            if offset[1]:
                here = here - pltpu.roll(jnp.where(low, value, 0.0), at + CZ, 1)
                there = there - pltpu.roll(jnp.where(low, 0.0, value), (at - CZ) % 256, 1)
            else:
                here = here - pltpu.roll(value, at, 1)
        if len(outs) == 1:
            outs[0][d] = here[:, COLUMNS : COLUMNS + CELLS]
            continue
        for at, total in ((0, here), (3, there)):
            outs[at][d] = total[:, COLUMNS : COLUMNS + CELLS]
            outs[at + 1][d] = total[:, :COLUMNS]
            outs[at + 2][d] = total[:, COLUMNS + CELLS : 2 * COLUMNS + CELLS]


def pair_forces(blocks, passes, single, unroll=4):
    rows = len(passes) * SLOTS
    pairs = rows * SLOTS * CELLS
    widths = (CELLS, COLUMNS, COLUMNS) * 2 if len(blocks) > 3 else (CELLS,)
    return pl.pallas_call(
        functools.partial(
            pair_kernel,
            passes=tuple(passes),
            single=single,
            sources=len(blocks),
            unroll=unroll,
        ),
        out_shape=[jax.ShapeDtypeStruct((3, SLOTS, width), F32) for width in widths],
        in_specs=[VMEM] * len(blocks),
        out_specs=[VMEM] * len(widths),
        scratch_shapes=[
            pltpu.VMEM((6, rows + 8, CELLS), F32),
            pltpu.VMEM((6, SLOTS, CELLS), F32),
            pltpu.VMEM((3, (rows - single * SLOTS) * 8, CELLS), F32),
        ],
        compiler_params=params(8),
        cost_estimate=pl.CostEstimate(flops=70 * pairs, bytes_accessed=1 << 20, transcendentals=0),
    )(*blocks)


def join_kernel(near_ref, here_ref, down_ref, first_a, first_b, last_a, last_b, out_ref):
    middle = jnp.zeros((SLOTS, CELLS - 2 * COLUMNS), F32)
    for d in range(3):
        sides = [first_a[d] + first_b[d], middle, last_a[d] + last_b[d]]
        out_ref[d] = (near_ref[d] + here_ref[d] + down_ref[d] + jnp.concatenate(sides, axis=1)).T


def hbm(array):
    return pltpu.with_memory_space_constraint(jnp.asarray(array), pltpu.HBM)


def send(value, step_x, step_y):
    route = [
        (x * DY + y, (x + step_x) % DX * DY + (y + step_y) % DY)
        for x in range(DX)
        for y in range(DY)
    ]
    return lax.ppermute(value, ("gx", "gy"), route)


def body(positions, charges, types, counts, eps_type, sig_type):
    tab = tables()
    slot_last = lambda a: jnp.moveaxis(a, -4, -1).reshape(a.shape[:-4] + (CELLS, SLOTS))
    side = jax.ShapeDtypeStruct((6, SLOTS, COLUMNS), F32)
    atoms, first, last, rows, tz = pl.pallas_call(
        table_kernel,
        out_shape=(
            jax.ShapeDtypeStruct((6, SLOTS, CELLS), F32),
            side,
            side,
            jax.ShapeDtypeStruct((4, GROUPS, 128), F32),
            jax.ShapeDtypeStruct(tab["tz"].shape, BF16),
        ),
        in_specs=[ANY] * 7,
        out_specs=(VMEM,) * 5,
        scratch_shapes=[
            pltpu.VMEM((3, CELLS, SLOTS), F32),
            pltpu.VMEM((CELLS, SLOTS), F32),
            pltpu.VMEM((CELLS, SLOTS), jnp.int32),
            pltpu.VMEM((CX, CY, CZ), jnp.int32),
            pltpu.SMEM(eps_type.shape, F32),
            pltpu.SMEM(sig_type.shape, F32),
            pltpu.SemaphoreType.DMA((7,)),
        ],
        compiler_params=params(8),
    )(
        hbm(slot_last(positions)),
        hbm(slot_last(charges)),
        hbm(slot_last(types)),
        hbm(counts),
        hbm(eps_type),
        hbm(sig_type),
        hbm(tab["tz"]),
    )
    after = send(first, -1, 0)
    before = send(last, 1, 0)
    above = send(atoms, 0, -1)
    above_after = send(first, -1, -1)
    above_before = send(last, 1, -1)

    spread, modes, edges = pl.pallas_call(
        spread_kernel,
        out_shape=(
            jax.ShapeDtypeStruct((LZ, 1, BLOCK), F32),
            jax.ShapeDtypeStruct((CX * CY, 3 * LZ, 512), BF16),
            jax.ShapeDtypeStruct((CX * CY, 32, 512), F32),
        ),
        in_specs=[VMEM] * 2,
        out_specs=(ANY, VMEM, ANY),
        scratch_shapes=[
            pltpu.VMEM((BY, 40, LZ), F32),
            pltpu.VMEM((BLOCK, LZ), F32),
            pltpu.VMEM((LZ, BLOCK), F32),
            pltpu.VMEM((CX * CY, 32, 512), F32),
            pltpu.SemaphoreType.DMA((2,)),
        ],
        compiler_params=params(16),
    )(rows, tz)
    spread, after, before, above, above_after, above_before = lax.optimization_barrier(
        (spread, after, before, above, above_after, above_before)
    )
    lines = lax.all_to_all(hbm(spread), ("gx", "gy"), split_axis=0, concat_axis=0, tiled=True)
    here, to_before, to_after, up, up_before, up_after = pair_forces(
        (atoms, before, after, above, above_before, above_after),
        [(a, 1, c) for a in (-1, 0, 1) for c in (-1, 0, 1)],
        0,
    )
    lines, here, to_before, to_after, up, up_before, up_after = lax.optimization_barrier(
        (lines, here, to_before, to_after, up, up_before, up_after)
    )
    sides = (
        send(up, 0, 1),
        send(to_after, 1, 0),
        send(up_after, 1, 1),
        send(to_before, -1, 0),
        send(up_before, -1, 1),
    )

    index = lax.axis_index("gx") * DY + lax.axis_index("gy")
    plane = lax.dynamic_index_in_dim(jnp.asarray(tab["plane"]), index, 0, keepdims=False)
    constants = [hbm(tab[name]) for name in ("tx", "ty", "iy", "ix", "kx2", "ky2")]
    fields = pl.pallas_call(
        plane_kernel,
        out_shape=jax.ShapeDtypeStruct((DX * DY, 1, 3 * BLOCK), F32),
        in_specs=[SMEM] + [ANY] * 7,
        out_specs=ANY,
        scratch_shapes=[
            *(pltpu.VMEM(tab[name].shape, BF16) for name in ("tx", "ty", "iy", "ix")),
            *(pltpu.VMEM(tab[name].shape, F32) for name in ("kx2", "ky2")),
            pltpu.VMEM((DX * DY, BLOCK), F32),
            pltpu.VMEM((DX // 2, BY * DY, 128), F32),
            pltpu.VMEM((3, DX * DY, BLOCK), F32),
            pltpu.SemaphoreType.DMA((10,)),
        ],
        compiler_params=params(20),
    )(plane, lines, *constants)
    fields = lax.all_to_all(hbm(fields), ("gx", "gy"), split_axis=0, concat_axis=0, tiled=True)
    beside = [(a, 0, c) for a in (-1, 1) for c in (-1, 0, 1)]
    (near,) = pair_forces((atoms, before, after), [(0, 0, 0), *beside, (0, 0, 1)], 7)
    pair_force = pl.pallas_call(
        join_kernel,
        out_shape=jax.ShapeDtypeStruct((3, CELLS, SLOTS), F32),
        in_specs=[VMEM] * 7,
        out_specs=VMEM,
        compiler_params=params(4),
    )(near, here, *sides)
    fields, pair_force = lax.optimization_barrier((fields, pair_force))

    mesh_force = pl.pallas_call(
        force_kernel,
        out_shape=jax.ShapeDtypeStruct((3, CELLS, SLOTS), F32),
        in_specs=[ANY, VMEM, ANY, VMEM],
        out_specs=VMEM,
        scratch_shapes=[
            pltpu.VMEM((3, LZ, BLOCK), F32),
            pltpu.VMEM((BLOCK, LZ), F32),
            pltpu.VMEM((3, BY, 40, LZ), F32),
            pltpu.VMEM((3, GROUPS, 128), F32),
            pltpu.VMEM((CX * CY, 32, 512), F32),
            pltpu.SemaphoreType.DMA((4,)),
        ],
        compiler_params=params(20),
    )(fields, modes, hbm(edges), tab["swap"])
    slot_first = lambda a: jnp.moveaxis(a.reshape(3, CX, CY, CZ, SLOTS), -1, 1)
    return slot_first(pair_force), slot_first(mesh_force)


def solution(mesh):
    placed = (
        P(None, None, "gx", "gy", None),
        P(None, "gx", "gy", None),
        P(None, "gx", "gy", None),
        P("gx", "gy", None),
        P(),
        P(),
    )
    return jax.shard_map(
        body,
        mesh=mesh,
        in_specs=placed,
        out_specs=(P(None, None, "gx", "gy", None), P(None, None, "gx", "gy", None)),
        check_vma=False,
    )
```

```python
import functools
import math

import jax
import jax.numpy as jnp
import ml_dtypes
import numpy as np
from jax import lax
from jax.experimental import pallas as pl
from jax.experimental.pallas import tpu as pltpu
from jax.sharding import PartitionSpec as P

CELL = 8
GEWALD = 0.7
CUT = 64.0
F32 = jnp.float32
BF16 = jnp.bfloat16

SLOTS = 32
CX, CY, CZ = 4, 2, 16
CELLS = CX * CY * CZ
COLUMNS = CY * CZ
DX, DY = 8, 16
LX, LY, LZ = 256, 256, 128
BX, BY = CX * CELL + 4, CY * CELL + 4
BLOCK = 768
GROUPS = CELLS // 4
KZ = 48
KX = 64
LENGTH = math.sqrt(GEWALD * GEWALD * math.log2(math.e))
FAR = CUT * LENGTH * LENGTH
SCALES = (LENGTH, LENGTH, LENGTH, 1.0, 1.0 / math.sqrt(8.0 * FAR * LENGTH), 0.5 * LENGTH)
VMEM = pl.BlockSpec(memory_space=pltpu.VMEM)
SMEM = pl.BlockSpec(memory_space=pltpu.SMEM)
ANY = pl.BlockSpec(memory_space=pl.ANY)


def params(mib=40):
    return pltpu.CompilerParams(vmem_limit_bytes=mib << 20)


def split(array):
    high = array.astype(ml_dtypes.bfloat16)
    low = (array - high.astype(np.float64)).astype(ml_dtypes.bfloat16)
    return high, low


def left_parts(array):
    high, low = split(array)
    return np.concatenate([high, high, low], axis=-1)


def right_parts(array):
    high, low = split(array)
    return np.concatenate([high, low, high], axis=-2)


def basis(length):
    half = length // 2
    modes = np.concatenate([np.arange(half + 1), np.arange(1, half)])
    sines = np.arange(length) > half
    return modes, sines


def wave(points, modes, sines, length):
    angle = 2.0 * np.pi * (np.outer(modes, points) % length) / length
    return np.where(sines[:, None], np.sin(angle), np.cos(angle))


def wave_slope(points, modes, sines, length):
    angle = 2.0 * np.pi * (np.outer(modes, points) % length) / length
    k = 2.0 * np.pi * modes / length
    k = np.where(modes == length // 2, 0.0, k)[:, None]
    return np.where(sines[:, None], -k * np.cos(angle), k * np.sin(angle))


def damping(modes, length):
    k = 2.0 * np.pi * modes / length
    return np.exp(-k * k / (4.0 * GEWALD * GEWALD)) / np.sinc(modes / length) ** 8


def norms(modes, length):
    return np.where((modes == 0) | (modes == length // 2), 1.0, 2.0) / length


@functools.cache
def tables():
    mz, sz = basis(LZ)
    tz = np.zeros((4, LZ, KZ))
    for zg in range(4):
        tz[zg, :, :36] = wave(32 * zg - 2 + np.arange(36), mz, sz, LZ)
    mx, sx = basis(LX)
    my, sy = basis(LY)
    tx = np.zeros((DX // 2, 128, LX))
    gain_x = damping(mx, LX) * norms(mx, LX)
    ix = np.zeros((2, LX, DX * BX))
    for gx in range(DX):
        points = gx * CX * CELL - 2 + np.arange(BX)
        at = KX * (gx % 2)
        tx[gx // 2, at : at + BX] = (wave(points, mx, sx, LX) * gain_x[:, None]).T
        ix[0, :, gx * BX : (gx + 1) * BX] = wave(points, mx, sx, LX)
        ix[1, :, gx * BX : (gx + 1) * BX] = wave_slope(points, mx, sx, LX)
    points = (np.arange(DY)[None, :] * CY * CELL - 2 + np.arange(BY)[:, None]).reshape(-1)
    gain_y = damping(my, LY) * norms(my, LY)
    ty = wave(points, my, sy, LY) * gain_y[:, None]
    iy = np.concatenate([wave(points, my, sy, LY).T, wave_slope(points, my, sy, LY).T])
    kx2 = ((2.0 * np.pi * mx / LX) ** 2).astype(np.float32)[None, :]
    ky2 = ((2.0 * np.pi * my / LY) ** 2).astype(np.float32)[:, None]
    kz = 2.0 * np.pi * mz / LZ
    plane = np.stack([kz * kz, 4.0 * np.pi * damping(mz, LZ) * norms(mz, LZ)], 1)
    half = LZ // 2
    swap = 2.0 * np.pi * np.arange(half) / LZ
    swap = np.concatenate([-swap, swap]).astype(np.float32)[None, :]
    return dict(
        tz=left_parts(tz),
        tx=right_parts(tx).reshape(-1, LX),
        ty=left_parts(ty),
        iy=left_parts(iy),
        ix=right_parts(np.concatenate([ix[0], ix[1]], axis=1)),
        kx2=kx2,
        ky2=np.broadcast_to(ky2, (LY, 128)).astype(np.float32),
        plane=plane.astype(np.float32),
        swap=swap,
    )


def halves(value):
    high = value.astype(BF16)
    return high, (value - high.astype(F32)).astype(BF16)


def left_split(value):
    high, low = halves(value)
    return jnp.concatenate([high, high, low], axis=1)


def right_split(value, axis=0):
    high, low = halves(value)
    return jnp.concatenate([high, low, high], axis=axis)


def dot(left, right, dims=((1,), (0,))):
    return lax.dot_general(left, right, (dims, ((), ())), preferred_element_type=F32)


def spline(offset):
    span = jnp.abs(offset)
    outer = jnp.maximum(2.0 - span, 0.0)
    inner = jnp.maximum(1.0 - span, 0.0)
    return (outer * outer * outer) * (1.0 / 6.0) - (inner * inner * inner) * (2.0 / 3.0)


def weights(rows_ref, tz_ref, col):
    point = (lax.broadcasted_iota(jnp.int32, (16, 128), 0) - 2).astype(F32)
    point_z = (lax.broadcasted_iota(jnp.int32, (KZ, 128), 0) - 2).astype(F32)
    shift = ((lax.broadcasted_iota(jnp.int32, (1, 128), 1) // SLOTS) * CELL).astype(F32)
    modes, edges = [], []
    for zg in range(4):
        row = [rows_ref[c, pl.ds(col * 4 + zg, 1), :] for c in range(4)]
        along_x = spline(row[0] - point)
        along_y = spline(row[1] - point) * row[3]
        along_z = spline(row[2] + shift - point_z)
        modes.append(dot(tz_ref[zg], right_split(along_z)))
        edges.append(jnp.concatenate([along_x, along_y], axis=0))
    return jnp.concatenate(modes, axis=1), jnp.concatenate(edges, axis=1)


def products(edges):
    return (edges[16:28][:, None, :] * edges[:16][None, :, :]).reshape(192, edges.shape[1])


def started(*copies):
    copies = [pltpu.make_async_copy(*copy) for copy in copies]
    for copy in copies:
        copy.start()
    return copies


def table_kernel(*refs):
    sources, (atoms_ref, first_ref, last_ref, rows_ref, tz_ref) = refs[:7], refs[7:12]
    pos_ref, charge_ref, type_ref, count_ref, eps_ref, sig_ref, sems = refs[12:]
    targets = refs[12:18] + (tz_ref,)
    incoming = started(*((s, t, sems.at[n]) for n, (s, t) in enumerate(zip(sources, targets))))
    for copy in incoming[:-1]:
        copy.wait()
    slots = lax.broadcasted_iota(jnp.int32, (SLOTS, CELLS), 0)
    counts = [count_ref[cx, cy : cy + 1, :] for cx in range(CX) for cy in range(CY)]
    occupied = slots < jnp.concatenate(counts, axis=1)
    kinds = type_ref[...].T
    eps = jnp.zeros((SLOTS, CELLS), F32)
    sig = jnp.zeros((SLOTS, CELLS), F32)
    for kind in range(eps_ref.shape[0]):
        match = kinds == kind
        eps = jnp.where(match, eps_ref[kind], eps)
        sig = jnp.where(match, sig_ref[kind], sig)
    charge = jnp.where(occupied, charge_ref[...].T, 0.0)
    root = jnp.where(occupied, jnp.sqrt(eps), 0.0)
    for c, value in enumerate([pos_ref[d].T for d in range(3)] + [charge, root, sig]):
        value = value * SCALES[c]
        atoms_ref[c] = value
        first_ref[c] = value[:, :COLUMNS]
        last_ref[c] = value[:, CELLS - COLUMNS :]
    charge = charge.T
    for c in range(4):
        value = pos_ref[c] if c < 3 else charge
        value = value.reshape(GROUPS, 4, SLOTS)
        rows_ref[c] = jnp.concatenate([value[:, s, :] for s in range(4)], axis=1)
    incoming[-1].wait()


def spread_kernel(rows_ref, tz_ref, spread_out, total, packed, turned, sems):
    total[...] = jnp.zeros_like(total)

    def column(col, carry):
        modes, edges = weights(rows_ref, tz_ref, col)
        part = dot(left_split(products(edges)), right_split(modes, 1), ((1,), (1,)))
        y = (col % CY) * CELL
        x = pl.multiple_of((col // CY) * CELL, CELL)
        total[pl.ds(y, 12), pl.ds(x, 16), :] += part.reshape(12, 16, LZ)
        return carry

    lax.fori_loop(0, CX * CY, column, 0, unroll=2)
    for y in range(BY):
        packed[y * BX : (y + 1) * BX, :] = total[y, :BX, :]
    packed[BX * BY :, :] = jnp.zeros((BLOCK - BX * BY, LZ), F32)
    turned[...] = packed[...].T
    outgoing = started(
        *(
            (turned.at[gx * DY : (gx + 1) * DY, :], spread_out.at[:, gx, :], sems.at[gx])
            for gx in range(DX)
        )
    )
    for copy in outgoing:
        copy.wait()


def weight_kernel(rows_ref, tz_ref, modes_ref, edges_ref):
    def column(col, carry):
        modes, edges_ref[col] = weights(rows_ref, tz_ref, col)
        modes_ref[col] = jnp.concatenate(halves(modes), axis=0)
        return carry

    lax.fori_loop(0, CX * CY, column, 0, unroll=2)


def plane_kernel(plane_ref, lines, *refs):
    sources, out_ref, held = refs[:6], refs[6], refs[7:13]
    stacked, turned, sems = refs[13:]
    tx, ty, iy, ix, kx2, ky2 = held
    constants = started(*((s, t, sems.at[4 + n]) for n, (s, t) in enumerate(zip(sources, held))))
    for y in range(BY):
        value = lines[:, y * BX : y * BX + KX]
        for gx in range(DX):
            at = KX * (gx % 2)
            stacked[gx // 2, y * DY : (y + 1) * DY, at : at + KX] = value[gx * DY : (gx + 1) * DY]
    pairs = jnp.concatenate([left_split(stacked[n]) for n in range(DX // 2)], axis=1)
    for copy in constants:
        copy.wait()
    modes = dot(ty[...], right_split(dot(pairs, tx[...])))
    k2 = kx2[...] + jnp.concatenate([ky2[...], ky2[...]], axis=1) + plane_ref[0]
    positive = k2 > 0.0
    modes = jnp.where(positive, modes * (plane_ref[1] / jnp.where(positive, k2, 1.0)), 0.0)
    both = dot(iy[...], right_split(modes))
    rows = BY * DY
    width = DX * BX
    plain = dot(left_split(both[:rows]), ix[...])
    slope = dot(left_split(both[rows:]), ix[:, :width])
    fields = (plain[:, width:], slope, plain[:, :width])
    outgoing = []
    for d in range(3):
        turned[d, :, BX * BY :] = jnp.zeros((DX * DY, BLOCK - BX * BY), F32)
        for gx in range(DX):
            piece = fields[d][:, gx * BX : (gx + 1) * BX]
            for y in range(BY):
                lane = y * BX
                turned[d, gx * DY : (gx + 1) * DY, lane : lane + BX] = piece[y * DY : (y + 1) * DY]
        outgoing += started(
            (turned.at[d], out_ref.at[:, 0, d * BLOCK : (d + 1) * BLOCK], sems.at[d])
        )
    for copy in outgoing:
        copy.wait()


def force_kernel(
    in_ref, modes_ref, edges_ref, swap_ref, out_ref, turned, packed, padded, rows_out, sems
):
    incoming = started(
        *(
            (in_ref.at[:, 0, d * BLOCK : (d + 1) * BLOCK], turned.at[d], sems.at[d])
            for d in range(3)
        )
    )
    for d in range(3):
        incoming[d].wait()
        value = turned[d].T
        if d == 2:
            value = pltpu.roll(value, LZ // 2, 1) * swap_ref[...]
        packed[...] = value
        for y in range(BY):
            padded[d, y, :BX, :] = packed[y * BX : (y + 1) * BX, :]
            padded[d, y, BX:, :] = jnp.zeros((40 - BX, LZ), F32)

    def column(col, carry):
        y = (col % CY) * CELL
        x = pl.multiple_of((col // CY) * CELL, CELL)
        planes = products(edges_ref[col])
        modes = modes_ref[col]
        modes = jnp.concatenate([modes, modes[:LZ]], axis=0)
        for d in range(3):
            block = padded[d, pl.ds(y, 12), pl.ds(x, 16), :].reshape(192, LZ)
            along = dot(left_split(block), modes)
            force = jnp.sum(along * planes, axis=0, keepdims=True)
            for zg in range(4):
                rows_out[d, pl.ds(col * 4 + zg, 1), :] = force[:, 128 * zg : 128 * (zg + 1)]
        return carry

    lax.fori_loop(0, CX * CY, column, 0, unroll=2)
    for d in range(3):
        value = rows_out[d]
        pieces = [value[:, s * SLOTS : (s + 1) * SLOTS][:, None, :] for s in range(4)]
        out_ref[d] = jnp.concatenate(pieces, axis=1).reshape(CELLS, SLOTS)


COULOMB = (
    -0.006156452396320011,
    -0.0004198503476764426,
    0.4251962050951751,
    -0.035971568956237085,
    0.5422242920959217,
    -0.3965913855606964,
    0.1962617265017834,
    -0.05766279059061346,
    0.007452967624700701,
)


def pair_term(own, other):
    dx = other[0] - own[0]
    dy = other[1] - own[1]
    dz = other[2] - own[2]
    r2 = dx * dx + dy * dy + dz * dz
    gap = FAR - r2
    fade = jnp.maximum(gap, 0.0)
    t = lax.rsqrt(r2 + LENGTH * LENGTH)
    scale = -2.0 * math.exp(-GEWALD * GEWALD) * 2.0**-FAR / (FAR * LENGTH)
    terms = [scale * c * LENGTH**n for n, c in enumerate(COULOMB)]
    poly = terms[-1] * t + terms[-2]
    for c in terms[-3::-1]:
        poly = poly * t + c
    sigma = own[5] + other[5]
    square = sigma * sigma
    inverse = 1.0 / (r2 + square)
    x = square * inverse
    x3 = x * x * x
    rest = 1.0 - (x3 + x3)
    lj = x3 * (rest * ((fade * inverse) * 3.0 + 1.0) + 1.0)
    w = fade * ((own[4] * other[4]) * lj + (own[3] * other[3]) * (jnp.exp2(gap) * poly))
    return w * dx, w * dy, w * dz


def shifted_z(value, at_z, step):
    if step == 0:
        return value
    if step > 0:
        return jnp.where(
            at_z == CZ - 1, pltpu.roll(value, CZ - 1, 1), pltpu.roll(value, CELLS - 1, 1)
        )
    return jnp.where(at_z == 0, pltpu.roll(value, CELLS - CZ + 1, 1), pltpu.roll(value, 1, 1))


def pair_kernel(*refs, passes, single, sources, begun, unroll):
    blocks, start, outs = refs[:sources], refs[sources : sources + begun], refs[sources + begun : -3]
    others, own, back = refs[-3:]
    low = (lax.broadcasted_iota(jnp.int32, (SLOTS, 256), 1) & CZ) == 0
    at_z = lax.broadcasted_iota(jnp.int32, (SLOTS, CELLS), 1) & (CZ - 1)
    empty = jnp.zeros((SLOTS, 64), F32)
    for c in range(6):
        wide = jnp.concatenate([blocks[1][c], blocks[0][c], blocks[2][c], empty], axis=1)
        own[c] = blocks[0][c]
        layers = {0: wide}
        if sources > 3:
            above = jnp.concatenate([blocks[4][c], blocks[3][c], blocks[5][c], empty], axis=1)
            layers[1] = jnp.where(low, pltpu.roll(wide, 256 - CZ, 1), pltpu.roll(above, CZ, 1))
        for n, offset in enumerate(passes):
            at = COLUMNS * (offset[0] + 1)
            value = layers[offset[1]][:, at : at + CELLS]
            value = shifted_z(value, at_z, offset[2])
            others[c, n * SLOTS : (n + 1) * SLOTS] = (
                value + offset[c] * CELL * LENGTH if c < 3 else value
            )

    def step(n, sums, reverse):
        sums = list(sums)
        for jj in range(unroll):
            j = n * unroll + jj
            other = [others[c, pl.ds(j, 8, stride=0), :] for c in range(6)]
            total = [None] * 3
            for block in range(4):
                mine = [own[c, 8 * block : 8 * block + 8, :] for c in range(6)]
                force = pair_term(mine, other)
                for d in range(3):
                    sums[block * 3 + d] = sums[block * 3 + d] + force[d]
                    total[d] = force[d] if block == 0 else total[d] + force[d]
            if reverse:
                for d in range(3):
                    back[d, pl.ds(pl.multiple_of((j - single * SLOTS) * 8, 8), 8), :] = total[d]
        return tuple(sums)

    per = SLOTS // unroll
    sums = (jnp.zeros((8, CELLS), F32),) * 12
    sums = lax.fori_loop(0, single * per, functools.partial(step, reverse=False), sums)
    sums = lax.fori_loop(
        single * per, len(passes) * per, functools.partial(step, reverse=True), sums
    )
    nothing = jnp.zeros((SLOTS, 128), F32)
    for d in range(3):
        force = jnp.concatenate([sums[block * 3 + d] for block in range(4)], axis=0)
        here = pltpu.roll(jnp.concatenate([force, nothing], axis=1), COLUMNS, 1)
        there = jnp.zeros((SLOTS, 256), F32)
        for n, offset in enumerate(passes):
            if n < single:
                continue
            base = (n - single) * SLOTS * 8
            value = back[d, pl.ds(base, SLOTS, stride=8), :]
            for s in range(1, 8):
                value = value + back[d, pl.ds(base + s, SLOTS, stride=8), :]
            value = shifted_z(value, at_z, -offset[2])
            value = jnp.concatenate([value, nothing], axis=1)
            at = COLUMNS * (offset[0] + 1)
            if offset[1]:
                here = here - pltpu.roll(jnp.where(low, value, 0.0), at + CZ, 1)
                there = there - pltpu.roll(jnp.where(low, 0.0, value), (at - CZ) % 256, 1)
            else:
                here = here - pltpu.roll(value, at, 1)
        if not begun:
            outs[0][d] = here
            outs[1][d] = there
            continue
        here = here + start[0][d]
        there = there + start[1][d]
        for at, total in ((0, here), (3, there)):
            outs[at][d] = total[:, COLUMNS : COLUMNS + CELLS]
            outs[at + 1][d] = total[:, :COLUMNS]
            outs[at + 2][d] = total[:, COLUMNS + CELLS : 2 * COLUMNS + CELLS]


def pair_forces(blocks, passes, single=0, start=(), unroll=4):
    rows = len(passes) * SLOTS
    pairs = rows * SLOTS * CELLS
    widths = (CELLS, COLUMNS, COLUMNS) * 2 if start else (256, 256)
    return pl.pallas_call(
        functools.partial(
            pair_kernel,
            passes=tuple(passes),
            single=single,
            sources=len(blocks),
            begun=len(start),
            unroll=unroll,
        ),
        out_shape=[jax.ShapeDtypeStruct((3, SLOTS, width), F32) for width in widths],
        in_specs=[VMEM] * (len(blocks) + len(start)),
        out_specs=[VMEM] * len(widths),
        scratch_shapes=[
            pltpu.VMEM((6, rows + 8, CELLS), F32),
            pltpu.VMEM((6, SLOTS, CELLS), F32),
            pltpu.VMEM((3, (rows - single * SLOTS) * 8, CELLS), F32),
        ],
        compiler_params=params(8),
        cost_estimate=pl.CostEstimate(flops=70 * pairs, bytes_accessed=1 << 20, transcendentals=0),
    )(*blocks, *start)


def join_kernel(here_ref, down_ref, first_a, first_b, last_a, last_b, out_ref):
    middle = jnp.zeros((SLOTS, CELLS - 2 * COLUMNS), F32)
    for d in range(3):
        sides = [first_a[d] + first_b[d], middle, last_a[d] + last_b[d]]
        out_ref[d] = (here_ref[d] + down_ref[d] + jnp.concatenate(sides, axis=1)).T


def hbm(array):
    return pltpu.with_memory_space_constraint(jnp.asarray(array), pltpu.HBM)


def send(value, step_x, step_y):
    route = [
        (x * DY + y, (x + step_x) % DX * DY + (y + step_y) % DY)
        for x in range(DX)
        for y in range(DY)
    ]
    return lax.ppermute(value, ("gx", "gy"), route)


def body(positions, charges, types, counts, eps_type, sig_type):
    tab = tables()
    slot_last = lambda a: jnp.moveaxis(a, -4, -1).reshape(a.shape[:-4] + (CELLS, SLOTS))
    side = jax.ShapeDtypeStruct((6, SLOTS, COLUMNS), F32)
    atoms, first, last, rows, tz = pl.pallas_call(
        table_kernel,
        out_shape=(
            jax.ShapeDtypeStruct((6, SLOTS, CELLS), F32),
            side,
            side,
            jax.ShapeDtypeStruct((4, GROUPS, 128), F32),
            jax.ShapeDtypeStruct(tab["tz"].shape, BF16),
        ),
        in_specs=[ANY] * 7,
        out_specs=(VMEM,) * 5,
        scratch_shapes=[
            pltpu.VMEM((3, CELLS, SLOTS), F32),
            pltpu.VMEM((CELLS, SLOTS), F32),
            pltpu.VMEM((CELLS, SLOTS), jnp.int32),
            pltpu.VMEM((CX, CY, CZ), jnp.int32),
            pltpu.SMEM(eps_type.shape, F32),
            pltpu.SMEM(sig_type.shape, F32),
            pltpu.SemaphoreType.DMA((7,)),
        ],
        compiler_params=params(8),
    )(
        hbm(slot_last(positions)),
        hbm(slot_last(charges)),
        hbm(slot_last(types)),
        hbm(counts),
        hbm(eps_type),
        hbm(sig_type),
        hbm(tab["tz"]),
    )
    after = send(first, -1, 0)
    before = send(last, 1, 0)
    above = send(atoms, 0, -1)
    above_after = send(first, -1, -1)
    above_before = send(last, 1, -1)

    spread = pl.pallas_call(
        spread_kernel,
        out_shape=jax.ShapeDtypeStruct((DY, DX, BLOCK), F32),
        in_specs=[VMEM] * 2,
        out_specs=ANY,
        scratch_shapes=[
            pltpu.VMEM((BY, 40, LZ), F32),
            pltpu.VMEM((BLOCK, LZ), F32),
            pltpu.VMEM((LZ, BLOCK), F32),
            pltpu.SemaphoreType.DMA((DX,)),
        ],
        compiler_params=params(16),
    )(rows, tz)
    spread, after, before, above, above_after, above_before = lax.optimization_barrier(
        (spread, after, before, above, above_after, above_before)
    )
    blocks = (atoms, before, after, above, above_before, above_after)
    lines = lax.all_to_all(spread, "gy", split_axis=0, concat_axis=0, tiled=True)
    sums = pair_forces(
        blocks,
        [(0, 0, 0), (0, 0, 1)] + [(a, 1 - a, c) for a in (0, 1) for c in (-1, 0, 1)],
        single=1,
    )
    lines, *sums = lax.optimization_barrier((lines, *sums))
    lines = jnp.transpose(lines, (1, 0, 2))
    lines = lax.all_to_all(lines, "gx", split_axis=0, concat_axis=0, tiled=True)
    here, to_before, to_after, up, up_before, up_after = pair_forces(
        blocks, [(a, 1, c) for a in (-1, 1) for c in (-1, 0, 1)], start=sums
    )
    lines, here, to_before, to_after, up, up_before, up_after = lax.optimization_barrier(
        (lines, here, to_before, to_after, up, up_before, up_after)
    )
    lines = lines.reshape(DX * DY, BLOCK)
    sides = (
        send(up, 0, 1),
        send(to_after, 1, 0),
        send(up_after, 1, 1),
        send(to_before, -1, 0),
        send(up_before, -1, 1),
    )

    index = lax.axis_index("gx") * DY + lax.axis_index("gy")
    plane = lax.dynamic_index_in_dim(jnp.asarray(tab["plane"]), index, 0, keepdims=False)
    constants = [hbm(tab[name]) for name in ("tx", "ty", "iy", "ix", "kx2", "ky2")]
    fields = pl.pallas_call(
        plane_kernel,
        out_shape=jax.ShapeDtypeStruct((DX * DY, 1, 3 * BLOCK), F32),
        in_specs=[SMEM, VMEM] + [ANY] * 6,
        out_specs=ANY,
        scratch_shapes=[
            *(pltpu.VMEM(tab[name].shape, BF16) for name in ("tx", "ty", "iy", "ix")),
            *(pltpu.VMEM(tab[name].shape, F32) for name in ("kx2", "ky2")),
            pltpu.VMEM((DX // 2, BY * DY, 128), F32),
            pltpu.VMEM((3, DX * DY, BLOCK), F32),
            pltpu.SemaphoreType.DMA((10,)),
        ],
        compiler_params=params(20),
    )(plane, lines, *constants)
    fields = lax.all_to_all(hbm(fields), ("gx", "gy"), split_axis=0, concat_axis=0, tiled=True)
    pair_force = pl.pallas_call(
        join_kernel,
        out_shape=jax.ShapeDtypeStruct((3, CELLS, SLOTS), F32),
        in_specs=[VMEM] * 6,
        out_specs=VMEM,
        compiler_params=params(4),
    )(here, *sides)
    modes, edges = pl.pallas_call(
        weight_kernel,
        out_shape=(
            jax.ShapeDtypeStruct((CX * CY, 2 * LZ, 512), BF16),
            jax.ShapeDtypeStruct((CX * CY, 32, 512), F32),
        ),
        in_specs=[VMEM] * 2,
        out_specs=(VMEM, VMEM),
        compiler_params=params(8),
        cost_estimate=pl.CostEstimate(flops=1 << 28, bytes_accessed=1 << 20, transcendentals=0),
    )(rows, tz)
    fields, pair_force, modes, edges = lax.optimization_barrier(
        (fields, pair_force, modes, edges)
    )

    mesh_force = pl.pallas_call(
        force_kernel,
        out_shape=jax.ShapeDtypeStruct((3, CELLS, SLOTS), F32),
        in_specs=[ANY, VMEM, VMEM, VMEM],
        out_specs=VMEM,
        scratch_shapes=[
            pltpu.VMEM((3, LZ, BLOCK), F32),
            pltpu.VMEM((BLOCK, LZ), F32),
            pltpu.VMEM((3, BY, 40, LZ), F32),
            pltpu.VMEM((3, GROUPS, 128), F32),
            pltpu.SemaphoreType.DMA((3,)),
        ],
        compiler_params=params(20),
    )(fields, modes, edges, tab["swap"])
    slot_first = lambda a: jnp.moveaxis(a.reshape(3, CX, CY, CZ, SLOTS), -1, 1)
    return slot_first(pair_force), slot_first(mesh_force)


def solution(mesh):
    placed = (
        P(None, None, "gx", "gy", None),
        P(None, "gx", "gy", None),
        P(None, "gx", "gy", None),
        P("gx", "gy", None),
        P(),
        P(),
    )
    return jax.shard_map(
        body,
        mesh=mesh,
        in_specs=placed,
        out_specs=(P(None, None, "gx", "gy", None), P(None, None, "gx", "gy", None)),
        check_vma=False,
    )
```

```python
import functools
import math

import jax
import jax.numpy as jnp
import ml_dtypes
import numpy as np
from jax import lax
from jax.experimental import pallas as pl
from jax.experimental.pallas import tpu as pltpu
from jax.sharding import PartitionSpec as P

CELL = 8
GEWALD = 0.7
CUT = 64.0
F32 = jnp.float32
BF16 = jnp.bfloat16

SLOTS = 32
CX, CY, CZ = 4, 2, 16
CELLS = CX * CY * CZ
COLUMNS = CY * CZ
DX, DY = 8, 16
LX, LY, LZ = 256, 256, 128
BX, BY = CX * CELL + 4, CY * CELL + 4
BLOCK = 768
GROUPS = CELLS // 4
KZ = 48
KX = 64
LENGTH = math.sqrt(GEWALD * GEWALD * math.log2(math.e))
FAR = CUT * LENGTH * LENGTH
SCALES = (LENGTH, LENGTH, LENGTH, 1.0, 1.0 / math.sqrt(8.0 * FAR * LENGTH), 0.5 * LENGTH)
VMEM = pl.BlockSpec(memory_space=pltpu.VMEM)
SMEM = pl.BlockSpec(memory_space=pltpu.SMEM)
ANY = pl.BlockSpec(memory_space=pl.ANY)


def params(mib=40):
    return pltpu.CompilerParams(vmem_limit_bytes=mib << 20)


def split(array):
    high = array.astype(ml_dtypes.bfloat16)
    low = (array - high.astype(np.float64)).astype(ml_dtypes.bfloat16)
    return high, low


def left_parts(array):
    high, low = split(array)
    return np.concatenate([high, high, low], axis=-1)


def right_parts(array):
    high, low = split(array)
    return np.concatenate([high, low, high], axis=-2)


def basis(length):
    half = length // 2
    modes = np.concatenate([np.arange(half + 1), np.arange(1, half)])
    sines = np.arange(length) > half
    return modes, sines


def wave(points, modes, sines, length):
    angle = 2.0 * np.pi * (np.outer(modes, points) % length) / length
    return np.where(sines[:, None], np.sin(angle), np.cos(angle))


def wave_slope(points, modes, sines, length):
    angle = 2.0 * np.pi * (np.outer(modes, points) % length) / length
    k = 2.0 * np.pi * modes / length
    k = np.where(modes == length // 2, 0.0, k)[:, None]
    return np.where(sines[:, None], -k * np.cos(angle), k * np.sin(angle))


def damping(modes, length):
    k = 2.0 * np.pi * modes / length
    return np.exp(-k * k / (4.0 * GEWALD * GEWALD)) / np.sinc(modes / length) ** 8


def norms(modes, length):
    return np.where((modes == 0) | (modes == length // 2), 1.0, 2.0) / length


@functools.cache
def tables():
    mz, sz = basis(LZ)
    tz = np.zeros((4, LZ, KZ))
    for zg in range(4):
        tz[zg, :, :36] = wave(32 * zg - 2 + np.arange(36), mz, sz, LZ)
    mx, sx = basis(LX)
    my, sy = basis(LY)
    tx = np.zeros((DX // 2, 128, LX))
    gain_x = damping(mx, LX) * norms(mx, LX)
    ix = np.zeros((2, LX, DX * BX))
    for gx in range(DX):
        points = gx * CX * CELL - 2 + np.arange(BX)
        at = KX * (gx % 2)
        tx[gx // 2, at : at + BX] = (wave(points, mx, sx, LX) * gain_x[:, None]).T
        ix[0, :, gx * BX : (gx + 1) * BX] = wave(points, mx, sx, LX)
        ix[1, :, gx * BX : (gx + 1) * BX] = wave_slope(points, mx, sx, LX)
    points = (np.arange(DY)[None, :] * CY * CELL - 2 + np.arange(BY)[:, None]).reshape(-1)
    gain_y = damping(my, LY) * norms(my, LY)
    ty = wave(points, my, sy, LY) * gain_y[:, None]
    iy = np.concatenate([wave(points, my, sy, LY).T, wave_slope(points, my, sy, LY).T])
    kx2 = ((2.0 * np.pi * mx / LX) ** 2).astype(np.float32)[None, :]
    ky2 = ((2.0 * np.pi * my / LY) ** 2).astype(np.float32)[:, None]
    kz = 2.0 * np.pi * mz / LZ
    plane = np.stack([kz * kz, 4.0 * np.pi * damping(mz, LZ) * norms(mz, LZ)], 1)
    half = LZ // 2
    swap = 2.0 * np.pi * np.arange(half) / LZ
    swap = np.concatenate([-swap, swap]).astype(np.float32)[None, :]
    return dict(
        tz=left_parts(tz),
        tx=right_parts(tx).reshape(-1, LX),
        ty=left_parts(ty),
        iy=left_parts(iy),
        ix=right_parts(np.concatenate([ix[0], ix[1]], axis=1)),
        kx2=kx2,
        ky2=np.broadcast_to(ky2, (LY, 128)).astype(np.float32),
        plane=plane.astype(np.float32),
        swap=swap,
    )


def halves(value):
    high = value.astype(BF16)
    return high, (value - high.astype(F32)).astype(BF16)


def left_split(value):
    high, low = halves(value)
    return jnp.concatenate([high, high, low], axis=1)


def right_split(value, axis=0):
    high, low = halves(value)
    return jnp.concatenate([high, low, high], axis=axis)


def dot(left, right, dims=((1,), (0,))):
    return lax.dot_general(left, right, (dims, ((), ())), preferred_element_type=F32)


def spline(offset):
    span = jnp.abs(offset)
    outer = jnp.maximum(2.0 - span, 0.0)
    inner = jnp.maximum(1.0 - span, 0.0)
    return (outer * outer * outer) * (1.0 / 6.0) - (inner * inner * inner) * (2.0 / 3.0)


def weights(rows_ref, tz_ref, col):
    point = (lax.broadcasted_iota(jnp.int32, (16, 128), 0) - 2).astype(F32)
    point_z = (lax.broadcasted_iota(jnp.int32, (KZ, 128), 0) - 2).astype(F32)
    shift = ((lax.broadcasted_iota(jnp.int32, (1, 128), 1) // SLOTS) * CELL).astype(F32)
    modes, edges = [], []
    for zg in range(4):
        row = [rows_ref[c, pl.ds(col * 4 + zg, 1), :] for c in range(4)]
        along_x = spline(row[0] - point)
        along_y = spline(row[1] - point) * row[3]
        along_z = spline(row[2] + shift - point_z)
        modes.append(dot(tz_ref[zg], right_split(along_z)))
        edges.append(jnp.concatenate([along_x, along_y], axis=0))
    return jnp.concatenate(modes, axis=1), jnp.concatenate(edges, axis=1)


def products(edges):
    return (edges[16:28][:, None, :] * edges[:16][None, :, :]).reshape(192, edges.shape[1])


def started(*copies):
    copies = [pltpu.make_async_copy(*copy) for copy in copies]
    for copy in copies:
        copy.start()
    return copies


def table_kernel(*refs):
    sources, (atoms_ref, first_ref, last_ref, rows_ref, tz_ref) = refs[:7], refs[7:12]
    pos_ref, charge_ref, type_ref, count_ref, eps_ref, sig_ref, sems = refs[12:]
    targets = refs[12:18] + (tz_ref,)
    incoming = started(*((s, t, sems.at[n]) for n, (s, t) in enumerate(zip(sources, targets))))
    for copy in incoming[:-1]:
        copy.wait()
    slots = lax.broadcasted_iota(jnp.int32, (SLOTS, CELLS), 0)
    counts = [count_ref[cx, cy : cy + 1, :] for cx in range(CX) for cy in range(CY)]
    occupied = slots < jnp.concatenate(counts, axis=1)
    kinds = type_ref[...].T
    eps = jnp.zeros((SLOTS, CELLS), F32)
    sig = jnp.zeros((SLOTS, CELLS), F32)
    for kind in range(eps_ref.shape[0]):
        match = kinds == kind
        eps = jnp.where(match, eps_ref[kind], eps)
        sig = jnp.where(match, sig_ref[kind], sig)
    charge = jnp.where(occupied, charge_ref[...].T, 0.0)
    root = jnp.where(occupied, jnp.sqrt(eps), 0.0)
    for c, value in enumerate([pos_ref[d].T for d in range(3)] + [charge, root, sig]):
        value = value * SCALES[c]
        atoms_ref[c] = value
        first_ref[c] = value[:, :COLUMNS]
        last_ref[c] = value[:, CELLS - COLUMNS :]
    charge = charge.T
    for c in range(4):
        value = pos_ref[c] if c < 3 else charge
        value = value.reshape(GROUPS, 4, SLOTS)
        rows_ref[c] = jnp.concatenate([value[:, s, :] for s in range(4)], axis=1)
    incoming[-1].wait()


def spread_kernel(rows_ref, tz_ref, spread_out, total, packed, turned, sem):
    total[...] = jnp.zeros_like(total)

    def column(col, carry):
        modes, edges = weights(rows_ref, tz_ref, col)
        part = dot(left_split(products(edges)), right_split(modes, 1), ((1,), (1,)))
        y = (col % CY) * CELL
        x = pl.multiple_of((col // CY) * CELL, CELL)
        total[pl.ds(y, 12), pl.ds(x, 16), :] += part.reshape(12, 16, LZ)
        return carry

    lax.fori_loop(0, CX * CY, column, 0, unroll=2)
    for y in range(BY):
        packed[y * BX : (y + 1) * BX, :] = total[y, :BX, :]
    packed[BX * BY :, :] = jnp.zeros((BLOCK - BX * BY, LZ), F32)
    turned[...] = packed[...].T
    for copy in started((turned, spread_out.at[:, 0, :], sem)):
        copy.wait()


def weight_kernel(rows_ref, tz_ref, modes_ref, edges_ref):
    def column(col, carry):
        modes, edges_ref[col] = weights(rows_ref, tz_ref, col)
        modes_ref[col] = jnp.concatenate(halves(modes), axis=0)
        return carry

    lax.fori_loop(0, CX * CY, column, 0, unroll=2)


def plane_kernel(plane_ref, in_ref, *refs):
    sources, out_ref, held = refs[:6], refs[6], refs[7:13]
    lines, stacked, turned, sems = refs[13:]
    tx, ty, iy, ix, kx2, ky2 = held
    (arrival,) = started((in_ref.at[:, 0, :], lines, sems.at[3]))
    constants = started(*((s, t, sems.at[4 + n]) for n, (s, t) in enumerate(zip(sources, held))))
    arrival.wait()
    for y in range(BY):
        value = lines[:, y * BX : y * BX + KX]
        for gx in range(DX):
            at = KX * (gx % 2)
            stacked[gx // 2, y * DY : (y + 1) * DY, at : at + KX] = value[gx * DY : (gx + 1) * DY]
    pairs = jnp.concatenate([left_split(stacked[n]) for n in range(DX // 2)], axis=1)
    for copy in constants:
        copy.wait()
    modes = dot(ty[...], right_split(dot(pairs, tx[...])))
    k2 = kx2[...] + jnp.concatenate([ky2[...], ky2[...]], axis=1) + plane_ref[0]
    positive = k2 > 0.0
    modes = jnp.where(positive, modes * (plane_ref[1] / jnp.where(positive, k2, 1.0)), 0.0)
    both = dot(iy[...], right_split(modes))
    rows = BY * DY
    width = DX * BX
    plain = dot(left_split(both[:rows]), ix[...])
    slope = dot(left_split(both[rows:]), ix[:, :width])
    fields = (plain[:, width:], slope, plain[:, :width])
    outgoing = []
    for d in range(3):
        turned[d, :, BX * BY :] = jnp.zeros((DX * DY, BLOCK - BX * BY), F32)
        for gx in range(DX):
            piece = fields[d][:, gx * BX : (gx + 1) * BX]
            for y in range(BY):
                lane = y * BX
                turned[d, gx * DY : (gx + 1) * DY, lane : lane + BX] = piece[y * DY : (y + 1) * DY]
        outgoing += started(
            (turned.at[d], out_ref.at[:, 0, d * BLOCK : (d + 1) * BLOCK], sems.at[d])
        )
    for copy in outgoing:
        copy.wait()


def force_kernel(
    in_ref, modes_ref, edges_ref, swap_ref, out_ref, turned, packed, padded, rows_out, sems
):
    incoming = started(
        *(
            (in_ref.at[:, 0, d * BLOCK : (d + 1) * BLOCK], turned.at[d], sems.at[d])
            for d in range(3)
        )
    )
    for d in range(3):
        incoming[d].wait()
        value = turned[d].T
        if d == 2:
            value = pltpu.roll(value, LZ // 2, 1) * swap_ref[...]
        packed[...] = value
        for y in range(BY):
            padded[d, y, :BX, :] = packed[y * BX : (y + 1) * BX, :]
            padded[d, y, BX:, :] = jnp.zeros((40 - BX, LZ), F32)

    def column(col, carry):
        y = (col % CY) * CELL
        x = pl.multiple_of((col // CY) * CELL, CELL)
        planes = products(edges_ref[col])
        modes = modes_ref[col]
        modes = jnp.concatenate([modes, modes[:LZ]], axis=0)
        for d in range(3):
            block = padded[d, pl.ds(y, 12), pl.ds(x, 16), :].reshape(192, LZ)
            along = dot(left_split(block), modes)
            force = jnp.sum(along * planes, axis=0, keepdims=True)
            for zg in range(4):
                rows_out[d, pl.ds(col * 4 + zg, 1), :] = force[:, 128 * zg : 128 * (zg + 1)]
        return carry

    lax.fori_loop(0, CX * CY, column, 0, unroll=2)
    for d in range(3):
        value = rows_out[d]
        pieces = [value[:, s * SLOTS : (s + 1) * SLOTS][:, None, :] for s in range(4)]
        out_ref[d] = jnp.concatenate(pieces, axis=1).reshape(CELLS, SLOTS)


COULOMB = (
    -0.006156452396320011,
    -0.0004198503476764426,
    0.4251962050951751,
    -0.035971568956237085,
    0.5422242920959217,
    -0.3965913855606964,
    0.1962617265017834,
    -0.05766279059061346,
    0.007452967624700701,
)


def pair_term(own, other):
    dx = other[0] - own[0]
    dy = other[1] - own[1]
    dz = other[2] - own[2]
    r2 = dx * dx + dy * dy + dz * dz
    gap = FAR - r2
    fade = jnp.maximum(gap, 0.0)
    t = lax.rsqrt(r2 + LENGTH * LENGTH)
    scale = -2.0 * math.exp(-GEWALD * GEWALD) * 2.0**-FAR / (FAR * LENGTH)
    terms = [scale * c * LENGTH**n for n, c in enumerate(COULOMB)]
    poly = terms[-1] * t + terms[-2]
    for c in terms[-3::-1]:
        poly = poly * t + c
    sigma = own[5] + other[5]
    square = sigma * sigma
    inverse = 1.0 / (r2 + square)
    x = square * inverse
    x3 = x * x * x
    rest = 1.0 - (x3 + x3)
    lj = x3 * (rest * ((fade * inverse) * 3.0 + 1.0) + 1.0)
    w = fade * ((own[4] * other[4]) * lj + (own[3] * other[3]) * (jnp.exp2(gap) * poly))
    return w * dx, w * dy, w * dz


def shifted_z(value, at_z, step):
    if step == 0:
        return value
    if step > 0:
        return jnp.where(
            at_z == CZ - 1, pltpu.roll(value, CZ - 1, 1), pltpu.roll(value, CELLS - 1, 1)
        )
    return jnp.where(at_z == 0, pltpu.roll(value, CELLS - CZ + 1, 1), pltpu.roll(value, 1, 1))


def pair_kernel(*refs, passes, single, sources, begun, unroll):
    blocks, start, outs = refs[:sources], refs[sources : sources + begun], refs[sources + begun : -3]
    others, own, back = refs[-3:]
    low = (lax.broadcasted_iota(jnp.int32, (SLOTS, 256), 1) & CZ) == 0
    at_z = lax.broadcasted_iota(jnp.int32, (SLOTS, CELLS), 1) & (CZ - 1)
    empty = jnp.zeros((SLOTS, 64), F32)
    for c in range(6):
        wide = jnp.concatenate([blocks[1][c], blocks[0][c], blocks[2][c], empty], axis=1)
        own[c] = blocks[0][c]
        layers = {0: wide}
        if sources > 3:
            above = jnp.concatenate([blocks[4][c], blocks[3][c], blocks[5][c], empty], axis=1)
            layers[1] = jnp.where(low, pltpu.roll(wide, 256 - CZ, 1), pltpu.roll(above, CZ, 1))
        for n, offset in enumerate(passes):
            at = COLUMNS * (offset[0] + 1)
            value = layers[offset[1]][:, at : at + CELLS]
            value = shifted_z(value, at_z, offset[2])
            others[c, n * SLOTS : (n + 1) * SLOTS] = (
                value + offset[c] * CELL * LENGTH if c < 3 else value
            )

    def step(n, sums, reverse):
        sums = list(sums)
        for jj in range(unroll):
            j = n * unroll + jj
            other = [others[c, pl.ds(j, 8, stride=0), :] for c in range(6)]
            total = [None] * 3
            for block in range(4):
                mine = [own[c, 8 * block : 8 * block + 8, :] for c in range(6)]
                force = pair_term(mine, other)
                for d in range(3):
                    sums[block * 3 + d] = sums[block * 3 + d] + force[d]
                    total[d] = force[d] if block == 0 else total[d] + force[d]
            if reverse:
                for d in range(3):
                    back[d, pl.ds(pl.multiple_of((j - single * SLOTS) * 8, 8), 8), :] = total[d]
        return tuple(sums)

    per = SLOTS // unroll
    sums = (jnp.zeros((8, CELLS), F32),) * 12
    sums = lax.fori_loop(0, single * per, functools.partial(step, reverse=False), sums)
    sums = lax.fori_loop(
        single * per, len(passes) * per, functools.partial(step, reverse=True), sums
    )
    nothing = jnp.zeros((SLOTS, 128), F32)
    for d in range(3):
        force = jnp.concatenate([sums[block * 3 + d] for block in range(4)], axis=0)
        here = pltpu.roll(jnp.concatenate([force, nothing], axis=1), COLUMNS, 1)
        there = jnp.zeros((SLOTS, 256), F32)
        for n, offset in enumerate(passes):
            if n < single:
                continue
            base = (n - single) * SLOTS * 8
            value = back[d, pl.ds(base, SLOTS, stride=8), :]
            for s in range(1, 8):
                value = value + back[d, pl.ds(base + s, SLOTS, stride=8), :]
            value = shifted_z(value, at_z, -offset[2])
            value = jnp.concatenate([value, nothing], axis=1)
            at = COLUMNS * (offset[0] + 1)
            if offset[1]:
                here = here - pltpu.roll(jnp.where(low, value, 0.0), at + CZ, 1)
                there = there - pltpu.roll(jnp.where(low, 0.0, value), (at - CZ) % 256, 1)
            else:
                here = here - pltpu.roll(value, at, 1)
        if not begun:
            outs[0][d] = here
            outs[1][d] = there
            continue
        here = here + start[0][d]
        there = there + start[1][d]
        for at, total in ((0, here), (3, there)):
            outs[at][d] = total[:, COLUMNS : COLUMNS + CELLS]
            outs[at + 1][d] = total[:, :COLUMNS]
            outs[at + 2][d] = total[:, COLUMNS + CELLS : 2 * COLUMNS + CELLS]


def pair_forces(blocks, passes, single=0, start=(), unroll=4):
    rows = len(passes) * SLOTS
    pairs = rows * SLOTS * CELLS
    widths = (CELLS, COLUMNS, COLUMNS) * 2 if start else (256, 256)
    return pl.pallas_call(
        functools.partial(
            pair_kernel,
            passes=tuple(passes),
            single=single,
            sources=len(blocks),
            begun=len(start),
            unroll=unroll,
        ),
        out_shape=[jax.ShapeDtypeStruct((3, SLOTS, width), F32) for width in widths],
        in_specs=[VMEM] * (len(blocks) + len(start)),
        out_specs=[VMEM] * len(widths),
        scratch_shapes=[
            pltpu.VMEM((6, rows + 8, CELLS), F32),
            pltpu.VMEM((6, SLOTS, CELLS), F32),
            pltpu.VMEM((3, (rows - single * SLOTS) * 8, CELLS), F32),
        ],
        compiler_params=params(8),
        cost_estimate=pl.CostEstimate(flops=70 * pairs, bytes_accessed=1 << 20, transcendentals=0),
    )(*blocks, *start)


def join_kernel(here_ref, down_ref, first_a, first_b, last_a, last_b, out_ref):
    middle = jnp.zeros((SLOTS, CELLS - 2 * COLUMNS), F32)
    for d in range(3):
        sides = [first_a[d] + first_b[d], middle, last_a[d] + last_b[d]]
        out_ref[d] = (here_ref[d] + down_ref[d] + jnp.concatenate(sides, axis=1)).T


def hbm(array):
    return pltpu.with_memory_space_constraint(jnp.asarray(array), pltpu.HBM)


def send(value, step_x, step_y):
    route = [
        (x * DY + y, (x + step_x) % DX * DY + (y + step_y) % DY)
        for x in range(DX)
        for y in range(DY)
    ]
    return lax.ppermute(value, ("gx", "gy"), route)


def body(positions, charges, types, counts, eps_type, sig_type):
    tab = tables()
    slot_last = lambda a: jnp.moveaxis(a, -4, -1).reshape(a.shape[:-4] + (CELLS, SLOTS))
    side = jax.ShapeDtypeStruct((6, SLOTS, COLUMNS), F32)
    atoms, first, last, rows, tz = pl.pallas_call(
        table_kernel,
        out_shape=(
            jax.ShapeDtypeStruct((6, SLOTS, CELLS), F32),
            side,
            side,
            jax.ShapeDtypeStruct((4, GROUPS, 128), F32),
            jax.ShapeDtypeStruct(tab["tz"].shape, BF16),
        ),
        in_specs=[ANY] * 7,
        out_specs=(VMEM,) * 5,
        scratch_shapes=[
            pltpu.VMEM((3, CELLS, SLOTS), F32),
            pltpu.VMEM((CELLS, SLOTS), F32),
            pltpu.VMEM((CELLS, SLOTS), jnp.int32),
            pltpu.VMEM((CX, CY, CZ), jnp.int32),
            pltpu.SMEM(eps_type.shape, F32),
            pltpu.SMEM(sig_type.shape, F32),
            pltpu.SemaphoreType.DMA((7,)),
        ],
        compiler_params=params(8),
    )(
        hbm(slot_last(positions)),
        hbm(slot_last(charges)),
        hbm(slot_last(types)),
        hbm(counts),
        hbm(eps_type),
        hbm(sig_type),
        hbm(tab["tz"]),
    )
    after = send(first, -1, 0)
    before = send(last, 1, 0)
    above = send(atoms, 0, -1)
    above_after = send(first, -1, -1)
    above_before = send(last, 1, -1)

    spread = pl.pallas_call(
        spread_kernel,
        out_shape=jax.ShapeDtypeStruct((LZ, 1, BLOCK), F32),
        in_specs=[VMEM] * 2,
        out_specs=ANY,
        scratch_shapes=[
            pltpu.VMEM((BY, 40, LZ), F32),
            pltpu.VMEM((BLOCK, LZ), F32),
            pltpu.VMEM((LZ, BLOCK), F32),
            pltpu.SemaphoreType.DMA,
        ],
        compiler_params=params(16),
    )(rows, tz)
    spread, after, before, above, above_after, above_before = lax.optimization_barrier(
        (spread, after, before, above, above_after, above_before)
    )
    blocks = (atoms, before, after, above, above_before, above_after)
    lines = lax.all_to_all(hbm(spread), ("gx", "gy"), split_axis=0, concat_axis=0, tiled=True)
    sums = pair_forces(
        blocks,
        [(0, 0, 0), (0, 0, 1)] + [(a, 1 - a, c) for a in (0, 1) for c in (-1, 0, 1)],
        single=1,
    )
    modes, edges = pl.pallas_call(
        weight_kernel,
        out_shape=(
            jax.ShapeDtypeStruct((CX * CY, 2 * LZ, 512), BF16),
            jax.ShapeDtypeStruct((CX * CY, 32, 512), F32),
        ),
        in_specs=[VMEM] * 2,
        out_specs=(VMEM, VMEM),
        compiler_params=params(8),
        cost_estimate=pl.CostEstimate(flops=1 << 28, bytes_accessed=1 << 20, transcendentals=0),
    )(rows, tz)
    lines, modes, edges, *sums = lax.optimization_barrier((lines, modes, edges, *sums))

    index = lax.axis_index("gx") * DY + lax.axis_index("gy")
    plane = lax.dynamic_index_in_dim(jnp.asarray(tab["plane"]), index, 0, keepdims=False)
    constants = [hbm(tab[name]) for name in ("tx", "ty", "iy", "ix", "kx2", "ky2")]
    fields = pl.pallas_call(
        plane_kernel,
        out_shape=jax.ShapeDtypeStruct((DX * DY, 1, 3 * BLOCK), F32),
        in_specs=[SMEM] + [ANY] * 7,
        out_specs=ANY,
        scratch_shapes=[
            *(pltpu.VMEM(tab[name].shape, BF16) for name in ("tx", "ty", "iy", "ix")),
            *(pltpu.VMEM(tab[name].shape, F32) for name in ("kx2", "ky2")),
            pltpu.VMEM((DX * DY, BLOCK), F32),
            pltpu.VMEM((DX // 2, BY * DY, 128), F32),
            pltpu.VMEM((3, DX * DY, BLOCK), F32),
            pltpu.SemaphoreType.DMA((10,)),
        ],
        compiler_params=params(20),
    )(plane, lines, *constants)
    fields = lax.all_to_all(hbm(fields), ("gx", "gy"), split_axis=0, concat_axis=0, tiled=True)
    here, to_before, to_after, up, up_before, up_after = pair_forces(
        blocks, [(a, 1, c) for a in (-1, 1) for c in (-1, 0, 1)], start=sums
    )
    sides = (
        send(up, 0, 1),
        send(to_after, 1, 0),
        send(up_after, 1, 1),
        send(to_before, -1, 0),
        send(up_before, -1, 1),
    )

    fields, here = lax.optimization_barrier((fields, here))
    mesh_force = pl.pallas_call(
        force_kernel,
        out_shape=jax.ShapeDtypeStruct((3, CELLS, SLOTS), F32),
        in_specs=[ANY, VMEM, VMEM, VMEM],
        out_specs=VMEM,
        scratch_shapes=[
            pltpu.VMEM((3, LZ, BLOCK), F32),
            pltpu.VMEM((BLOCK, LZ), F32),
            pltpu.VMEM((3, BY, 40, LZ), F32),
            pltpu.VMEM((3, GROUPS, 128), F32),
            pltpu.SemaphoreType.DMA((3,)),
        ],
        compiler_params=params(20),
    )(fields, modes, edges, tab["swap"])
    mesh_force, here = lax.optimization_barrier((mesh_force, here))
    pair_force = pl.pallas_call(
        join_kernel,
        out_shape=jax.ShapeDtypeStruct((3, CELLS, SLOTS), F32),
        in_specs=[VMEM] * 6,
        out_specs=VMEM,
        compiler_params=params(4),
    )(here, *sides)

    slot_first = lambda a: jnp.moveaxis(a.reshape(3, CX, CY, CZ, SLOTS), -1, 1)
    return slot_first(pair_force), slot_first(mesh_force)


def solution(mesh):
    placed = (
        P(None, None, "gx", "gy", None),
        P(None, "gx", "gy", None),
        P(None, "gx", "gy", None),
        P("gx", "gy", None),
        P(),
        P(),
    )
    return jax.shard_map(
        body,
        mesh=mesh,
        in_specs=placed,
        out_specs=(P(None, None, "gx", "gy", None), P(None, None, "gx", "gy", None)),
        check_vma=False,
    )
```

```python
import functools
import math

import jax
import jax.numpy as jnp
import ml_dtypes
import numpy as np
from jax import lax
from jax.experimental import pallas as pl
from jax.experimental.pallas import tpu as pltpu
from jax.sharding import PartitionSpec as P

CELL = 8
GEWALD = 0.7
CUT = 64.0
F32 = jnp.float32
BF16 = jnp.bfloat16

SLOTS = 32
CX, CY, CZ = 4, 2, 16
CELLS = CX * CY * CZ
COLUMNS = CY * CZ
DX, DY = 8, 16
LX, LY, LZ = 256, 256, 128
BX, BY = CX * CELL + 4, CY * CELL + 4
BLOCK = 768
GROUPS = CELLS // 4
KZ = 48
KX = 64
LENGTH = math.sqrt(GEWALD * GEWALD * math.log2(math.e))
FAR = CUT * LENGTH * LENGTH
SCALES = (LENGTH, LENGTH, LENGTH, 1.0, 1.0 / math.sqrt(8.0 * FAR * LENGTH), 0.5 * LENGTH)
VMEM = pl.BlockSpec(memory_space=pltpu.VMEM)
ANY = pl.BlockSpec(memory_space=pl.ANY)


def params(mib=40):
    return pltpu.CompilerParams(vmem_limit_bytes=mib << 20)


def split(array):
    high = array.astype(ml_dtypes.bfloat16)
    low = (array - high.astype(np.float64)).astype(ml_dtypes.bfloat16)
    return high, low


def left_parts(array):
    high, low = split(array)
    return np.concatenate([high, high, low], axis=-1)


def right_parts(array):
    high, low = split(array)
    return np.concatenate([high, low, high], axis=-2)


def basis(length):
    half = length // 2
    modes = np.concatenate([np.arange(half + 1), np.arange(1, half)])
    sines = np.arange(length) > half
    return modes, sines


def wave(points, modes, sines, length):
    angle = 2.0 * np.pi * (np.outer(modes, points) % length) / length
    return np.where(sines[:, None], np.sin(angle), np.cos(angle))


def wave_slope(points, modes, sines, length):
    angle = 2.0 * np.pi * (np.outer(modes, points) % length) / length
    k = 2.0 * np.pi * modes / length
    k = np.where(modes == length // 2, 0.0, k)[:, None]
    return np.where(sines[:, None], -k * np.cos(angle), k * np.sin(angle))


def damping(modes, length):
    k = 2.0 * np.pi * modes / length
    return np.exp(-k * k / (4.0 * GEWALD * GEWALD)) / np.sinc(modes / length) ** 8


def norms(modes, length):
    return np.where((modes == 0) | (modes == length // 2), 1.0, 2.0) / length


@functools.cache
def tables():
    mz, sz = basis(LZ)
    tz = np.zeros((4, LZ, KZ))
    for zg in range(4):
        tz[zg, :, :36] = wave(32 * zg - 2 + np.arange(36), mz, sz, LZ)
    mx, sx = basis(LX)
    my, sy = basis(LY)
    tx = np.zeros((DX // 2, 128, LX))
    gain_x = damping(mx, LX) * norms(mx, LX)
    ix = np.zeros((2, LX, DX * BX))
    for gx in range(DX):
        points = gx * CX * CELL - 2 + np.arange(BX)
        at = KX * (gx % 2)
        tx[gx // 2, at : at + BX] = (wave(points, mx, sx, LX) * gain_x[:, None]).T
        ix[0, :, gx * BX : (gx + 1) * BX] = wave(points, mx, sx, LX)
        ix[1, :, gx * BX : (gx + 1) * BX] = wave_slope(points, mx, sx, LX)
    points = (np.arange(DY)[None, :] * CY * CELL - 2 + np.arange(BY)[:, None]).reshape(-1)
    gain_y = damping(my, LY) * norms(my, LY)
    ty = wave(points, my, sy, LY) * gain_y[:, None]
    iy = np.concatenate([wave(points, my, sy, LY).T, wave_slope(points, my, sy, LY).T])
    kx2 = ((2.0 * np.pi * mx / LX) ** 2).astype(np.float32)[None, :]
    ky2 = ((2.0 * np.pi * my / LY) ** 2).astype(np.float32)[:, None]
    kz = 2.0 * np.pi * mz / LZ
    plane = np.zeros((8, LZ))
    plane[6:] = kz * kz, 4.0 * np.pi * damping(mz, LZ) * norms(mz, LZ)
    half = LZ // 2
    swap = 2.0 * np.pi * np.arange(half) / LZ
    swap = np.concatenate([-swap, swap]).astype(np.float32)[None, :]
    return dict(
        tz=left_parts(tz),
        tx=right_parts(tx).reshape(-1, LX),
        ty=left_parts(ty),
        iy=left_parts(iy),
        ix=right_parts(np.concatenate([ix[0], ix[1]], axis=1)),
        kx2=kx2,
        ky2=np.broadcast_to(ky2, (LY, 128)).astype(np.float32),
        plane=plane.astype(np.float32),
        swap=swap,
    )


def halves(value):
    high = value.astype(BF16)
    return high, (value - high.astype(F32)).astype(BF16)


def left_split(value):
    high, low = halves(value)
    return jnp.concatenate([high, high, low], axis=1)


def right_split(value, axis=0):
    high, low = halves(value)
    return jnp.concatenate([high, low, high], axis=axis)


def dot(left, right, dims=((1,), (0,))):
    return lax.dot_general(left, right, (dims, ((), ())), preferred_element_type=F32)


def spline(offset):
    span = jnp.abs(offset)
    outer = jnp.maximum(2.0 - span, 0.0)
    inner = jnp.maximum(1.0 - span, 0.0)
    return (outer * outer * outer) * (1.0 / 6.0) - (inner * inner * inner) * (2.0 / 3.0)


def weights(rows_ref, tz_ref, col):
    point = (lax.broadcasted_iota(jnp.int32, (16, 128), 0) - 2).astype(F32)
    point_z = (lax.broadcasted_iota(jnp.int32, (KZ, 128), 0) - 2).astype(F32)
    shift = ((lax.broadcasted_iota(jnp.int32, (1, 128), 1) // SLOTS) * CELL).astype(F32)
    modes, edges = [], []
    for zg in range(4):
        row = [rows_ref[c, pl.ds(col * 4 + zg, 1), :] for c in range(4)]
        along_x = spline(row[0] - point)
        along_y = spline(row[1] - point) * row[3]
        along_z = spline(row[2] + shift - point_z)
        modes.append(dot(tz_ref[zg], right_split(along_z)))
        edges.append(jnp.concatenate([along_x, along_y], axis=0))
    return jnp.concatenate(modes, axis=1), jnp.concatenate(edges, axis=1)


def products(edges):
    return (edges[16:28][:, None, :] * edges[:16][None, :, :]).reshape(192, edges.shape[1])


def started(*copies):
    copies = [pltpu.make_async_copy(*copy) for copy in copies]
    for copy in copies:
        copy.start()
    return copies


def table_kernel(*refs):
    sources, (atoms_ref, first_ref, last_ref, rows_ref, tz_ref) = refs[:7], refs[7:12]
    pos_ref, charge_ref, type_ref, count_ref, eps_ref, sig_ref, sems = refs[12:]
    targets = refs[12:18] + (tz_ref,)
    incoming = started(*((s, t, sems.at[n]) for n, (s, t) in enumerate(zip(sources, targets))))
    for copy in incoming[:-1]:
        copy.wait()
    slots = lax.broadcasted_iota(jnp.int32, (SLOTS, CELLS), 0)
    counts = [count_ref[cx, cy : cy + 1, :] for cx in range(CX) for cy in range(CY)]
    occupied = slots < jnp.concatenate(counts, axis=1)
    kinds = type_ref[...].T
    eps = jnp.zeros((SLOTS, CELLS), F32)
    sig = jnp.zeros((SLOTS, CELLS), F32)
    for kind in range(eps_ref.shape[0]):
        match = kinds == kind
        eps = jnp.where(match, eps_ref[kind], eps)
        sig = jnp.where(match, sig_ref[kind], sig)
    charge = jnp.where(occupied, charge_ref[...].T, 0.0)
    root = jnp.where(occupied, jnp.sqrt(eps), 0.0)
    for c, value in enumerate([pos_ref[d].T for d in range(3)] + [charge, root, sig]):
        value = value * SCALES[c]
        atoms_ref[c] = value
        first_ref[c] = value[:, :COLUMNS]
        last_ref[c] = value[:, CELLS - COLUMNS :]
    charge = charge.T
    for c in range(4):
        value = pos_ref[c] if c < 3 else charge
        value = value.reshape(GROUPS, 4, SLOTS)
        rows_ref[c] = jnp.concatenate([value[:, s, :] for s in range(4)], axis=1)
    incoming[-1].wait()


def spread_kernel(rows_ref, tz_ref, plane_ref, spread_out, total, packed, turned, sems):
    (plane,) = started((plane_ref, packed.at[BLOCK - 8 :, :], sems.at[0]))
    total[...] = jnp.zeros_like(total)

    def column(col, carry):
        modes, edges = weights(rows_ref, tz_ref, col)
        part = dot(left_split(products(edges)), right_split(modes, 1), ((1,), (1,)))
        y = (col % CY) * CELL
        x = pl.multiple_of((col // CY) * CELL, CELL)
        total[pl.ds(y, 12), pl.ds(x, 16), :] += part.reshape(12, 16, LZ)
        return carry

    lax.fori_loop(0, CX * CY, column, 0, unroll=4)
    for y in range(BY):
        packed[y * BX : (y + 1) * BX, :] = total[y, :BX, :]
    packed[BX * BY : BLOCK - 8, :] = jnp.zeros((BLOCK - 8 - BX * BY, LZ), F32)
    plane.wait()
    turned[...] = packed[...].T
    for copy in started((turned, spread_out.at[:, 0, :], sems.at[1])):
        copy.wait()


def weight_kernel(rows_ref, tz_ref, modes_ref, edges_ref):
    def column(col, carry):
        modes, edges_ref[col] = weights(rows_ref, tz_ref, col)
        modes_ref[col] = jnp.concatenate(halves(modes), axis=0)
        return carry

    lax.fori_loop(0, CX * CY, column, 0, unroll=4)


def plane_kernel(in_ref, *refs):
    sources, out_ref, held = refs[:6], refs[6], refs[7:13]
    lines, stacked, turned, sems = refs[13:]
    tx, ty, iy, ix, kx2, ky2 = held
    (arrival,) = started((in_ref.at[:, 0, :], lines, sems.at[3]))
    constants = started(*((s, t, sems.at[4 + n]) for n, (s, t) in enumerate(zip(sources, held))))
    arrival.wait()
    kz2, gain = lines[:1, BLOCK - 2 : BLOCK - 1], lines[:1, BLOCK - 1 :]
    for y in range(BY):
        value = lines[:, y * BX : y * BX + KX]
        for gx in range(DX):
            at = KX * (gx % 2)
            stacked[gx // 2, y * DY : (y + 1) * DY, at : at + KX] = value[gx * DY : (gx + 1) * DY]
    pairs = jnp.concatenate([left_split(stacked[n]) for n in range(DX // 2)], axis=1)
    constants[0].wait()
    lines_y = right_split(dot(pairs, tx[...]))
    constants[1].wait()
    modes = dot(ty[...], lines_y)
    for copy in constants[4:]:
        copy.wait()
    k2 = kx2[...] + jnp.concatenate([ky2[...], ky2[...]], axis=1) + kz2
    positive = k2 > 0.0
    modes = jnp.where(positive, modes * (gain / jnp.where(positive, k2, 1.0)), 0.0)
    constants[2].wait()
    both = dot(iy[...], right_split(modes))
    constants[3].wait()
    rows = BY * DY
    width = DX * BX
    plain = dot(left_split(both[:rows]), ix[...])
    slope = dot(left_split(both[rows:]), ix[:, :width])
    fields = (plain[:, width:], slope, plain[:, :width])
    outgoing = []
    for d in range(3):
        turned[d, :, BX * BY :] = jnp.zeros((DX * DY, BLOCK - BX * BY), F32)
        for gx in range(DX):
            piece = fields[d][:, gx * BX : (gx + 1) * BX]
            for y in range(BY):
                lane = y * BX
                turned[d, gx * DY : (gx + 1) * DY, lane : lane + BX] = piece[y * DY : (y + 1) * DY]
        outgoing += started(
            (turned.at[d], out_ref.at[:, 0, d * BLOCK : (d + 1) * BLOCK], sems.at[d])
        )
    for copy in outgoing:
        copy.wait()


def force_kernel(
    in_ref, modes_ref, edges_ref, swap_ref, out_ref, turned, packed, padded, rows_out, sems
):
    incoming = started(
        *(
            (in_ref.at[:, 0, d * BLOCK : (d + 1) * BLOCK], turned.at[d], sems.at[d])
            for d in range(3)
        )
    )
    for d in range(3):
        incoming[d].wait()
        value = turned[d].T
        if d == 2:
            value = pltpu.roll(value, LZ // 2, 1) * swap_ref[...]
        packed[...] = value
        for y in range(BY):
            padded[d, y, :BX, :] = packed[y * BX : (y + 1) * BX, :]
            padded[d, y, BX:, :] = jnp.zeros((40 - BX, LZ), F32)

    def column(col, carry):
        y = (col % CY) * CELL
        x = pl.multiple_of((col // CY) * CELL, CELL)
        planes = products(edges_ref[col])
        modes = modes_ref[col]
        modes = jnp.concatenate([modes, modes[:LZ]], axis=0)
        for d in range(3):
            block = padded[d, pl.ds(y, 12), pl.ds(x, 16), :].reshape(192, LZ)
            along = dot(left_split(block), modes)
            force = jnp.sum(along * planes, axis=0, keepdims=True)
            for zg in range(4):
                rows_out[d, pl.ds(col * 4 + zg, 1), :] = force[:, 128 * zg : 128 * (zg + 1)]
        return carry

    lax.fori_loop(0, CX * CY, column, 0, unroll=4)
    for d in range(3):
        value = rows_out[d]
        pieces = [value[:, s * SLOTS : (s + 1) * SLOTS][:, None, :] for s in range(4)]
        out_ref[d] = jnp.concatenate(pieces, axis=1).reshape(CELLS, SLOTS)


COULOMB = (
    -0.006156452396320011,
    -0.0004198503476764426,
    0.4251962050951751,
    -0.035971568956237085,
    0.5422242920959217,
    -0.3965913855606964,
    0.1962617265017834,
    -0.05766279059061346,
    0.007452967624700701,
)


def pair_term(own, other):
    dx = other[0] - own[0]
    dy = other[1] - own[1]
    dz = other[2] - own[2]
    r2 = dx * dx + dy * dy + dz * dz
    gap = FAR - r2
    fade = jnp.maximum(gap, 0.0)
    t = lax.rsqrt(r2 + LENGTH * LENGTH)
    scale = -2.0 * math.exp(-GEWALD * GEWALD) * 2.0**-FAR / (FAR * LENGTH)
    terms = [scale * c * LENGTH**n for n, c in enumerate(COULOMB)]
    poly = terms[-1] * t + terms[-2]
    for c in terms[-3::-1]:
        poly = poly * t + c
    sigma = own[5] + other[5]
    square = sigma * sigma
    inverse = 1.0 / (r2 + square)
    x = square * inverse
    x3 = x * x * x
    rest = 1.0 - (x3 + x3)
    lj = x3 * (rest * ((fade * inverse) * 3.0 + 1.0) + 1.0)
    w = fade * ((own[4] * other[4]) * lj + (own[3] * other[3]) * (jnp.exp2(gap) * poly))
    return w * dx, w * dy, w * dz


def shifted_z(value, at_z, step):
    if step == 0:
        return value
    if step > 0:
        return jnp.where(
            at_z == CZ - 1, pltpu.roll(value, CZ - 1, 1), pltpu.roll(value, CELLS - 1, 1)
        )
    return jnp.where(at_z == 0, pltpu.roll(value, CELLS - CZ + 1, 1), pltpu.roll(value, 1, 1))


def pair_kernel(*refs, passes, single, sources, begun, unroll):
    blocks, start, outs = refs[:sources], refs[sources : sources + begun], refs[sources + begun : -3]
    others, own, back = refs[-3:]
    low = (lax.broadcasted_iota(jnp.int32, (SLOTS, 256), 1) & CZ) == 0
    at_z = lax.broadcasted_iota(jnp.int32, (SLOTS, CELLS), 1) & (CZ - 1)
    empty = jnp.zeros((SLOTS, 64), F32)
    for c in range(6):
        wide = jnp.concatenate([blocks[1][c], blocks[0][c], blocks[2][c], empty], axis=1)
        own[c] = blocks[0][c]
        layers = {0: wide}
        if sources > 3:
            above = jnp.concatenate([blocks[4][c], blocks[3][c], blocks[5][c], empty], axis=1)
            layers[1] = jnp.where(low, pltpu.roll(wide, 256 - CZ, 1), pltpu.roll(above, CZ, 1))
        for n, offset in enumerate(passes):
            at = COLUMNS * (offset[0] + 1)
            value = layers[offset[1]][:, at : at + CELLS]
            value = shifted_z(value, at_z, offset[2])
            others[c, n * SLOTS : (n + 1) * SLOTS] = (
                value + offset[c] * CELL * LENGTH if c < 3 else value
            )

    def step(n, sums, reverse):
        sums = list(sums)
        for jj in range(unroll):
            j = n * unroll + jj
            other = [others[c, pl.ds(j, 8, stride=0), :] for c in range(6)]
            total = [None] * 3
            for block in range(4):
                mine = [own[c, 8 * block : 8 * block + 8, :] for c in range(6)]
                force = pair_term(mine, other)
                for d in range(3):
                    sums[block * 3 + d] = sums[block * 3 + d] + force[d]
                    total[d] = force[d] if block == 0 else total[d] + force[d]
            if reverse:
                for d in range(3):
                    back[d, pl.ds(pl.multiple_of((j - single * SLOTS) * 8, 8), 8), :] = total[d]
        return tuple(sums)

    per = SLOTS // unroll
    sums = (jnp.zeros((8, CELLS), F32),) * 12
    sums = lax.fori_loop(0, single * per, functools.partial(step, reverse=False), sums)
    sums = lax.fori_loop(
        single * per, len(passes) * per, functools.partial(step, reverse=True), sums
    )
    nothing = jnp.zeros((SLOTS, 128), F32)
    for d in range(3):
        force = jnp.concatenate([sums[block * 3 + d] for block in range(4)], axis=0)
        here = pltpu.roll(jnp.concatenate([force, nothing], axis=1), COLUMNS, 1)
        there = jnp.zeros((SLOTS, 256), F32)
        for n, offset in enumerate(passes):
            if n < single:
                continue
            base = (n - single) * SLOTS * 8
            value = back[d, pl.ds(base, SLOTS, stride=8), :]
            for s in range(1, 8):
                value = value + back[d, pl.ds(base + s, SLOTS, stride=8), :]
            value = shifted_z(value, at_z, -offset[2])
            value = jnp.concatenate([value, nothing], axis=1)
            at = COLUMNS * (offset[0] + 1)
            if offset[1]:
                here = here - pltpu.roll(jnp.where(low, value, 0.0), at + CZ, 1)
                there = there - pltpu.roll(jnp.where(low, 0.0, value), (at - CZ) % 256, 1)
            else:
                here = here - pltpu.roll(value, at, 1)
        if not begun:
            outs[0][d] = here
            outs[1][d] = there
            continue
        here = here + start[0][d]
        there = there + start[1][d]
        for at, total in ((0, here), (3, there)):
            outs[at][d] = total[:, COLUMNS : COLUMNS + CELLS]
            outs[at + 1][d] = total[:, :COLUMNS]
            outs[at + 2][d] = total[:, COLUMNS + CELLS : 2 * COLUMNS + CELLS]


def pair_forces(blocks, passes, single=0, start=(), unroll=8):
    rows = len(passes) * SLOTS
    pairs = rows * SLOTS * CELLS
    widths = (CELLS, COLUMNS, COLUMNS) * 2 if start else (256, 256)
    return pl.pallas_call(
        functools.partial(
            pair_kernel,
            passes=tuple(passes),
            single=single,
            sources=len(blocks),
            begun=len(start),
            unroll=unroll,
        ),
        out_shape=[jax.ShapeDtypeStruct((3, SLOTS, width), F32) for width in widths],
        in_specs=[VMEM] * (len(blocks) + len(start)),
        out_specs=[VMEM] * len(widths),
        scratch_shapes=[
            pltpu.VMEM((6, rows + 8, CELLS), F32),
            pltpu.VMEM((6, SLOTS, CELLS), F32),
            pltpu.VMEM((3, (rows - single * SLOTS) * 8, CELLS), F32),
        ],
        compiler_params=params(8),
        cost_estimate=pl.CostEstimate(flops=70 * pairs, bytes_accessed=1 << 20, transcendentals=0),
    )(*blocks, *start)


def join_kernel(here_ref, down_ref, first_a, first_b, last_a, last_b, out_ref):
    middle = jnp.zeros((SLOTS, CELLS - 2 * COLUMNS), F32)
    for d in range(3):
        sides = [first_a[d] + first_b[d], middle, last_a[d] + last_b[d]]
        out_ref[d] = (here_ref[d] + down_ref[d] + jnp.concatenate(sides, axis=1)).T


def hbm(array):
    return pltpu.with_memory_space_constraint(jnp.asarray(array), pltpu.HBM)


def send(value, step_x, step_y):
    route = [
        (x * DY + y, (x + step_x) % DX * DY + (y + step_y) % DY)
        for x in range(DX)
        for y in range(DY)
    ]
    return lax.ppermute(value, ("gx", "gy"), route)


def body(positions, charges, types, counts, eps_type, sig_type):
    tab = tables()
    slot_last = lambda a: jnp.moveaxis(a, -4, -1).reshape(a.shape[:-4] + (CELLS, SLOTS))
    side = jax.ShapeDtypeStruct((6, SLOTS, COLUMNS), F32)
    atoms, first, last, rows, tz = pl.pallas_call(
        table_kernel,
        out_shape=(
            jax.ShapeDtypeStruct((6, SLOTS, CELLS), F32),
            side,
            side,
            jax.ShapeDtypeStruct((4, GROUPS, 128), F32),
            jax.ShapeDtypeStruct(tab["tz"].shape, BF16),
        ),
        in_specs=[ANY] * 7,
        out_specs=(VMEM,) * 5,
        scratch_shapes=[
            pltpu.VMEM((3, CELLS, SLOTS), F32),
            pltpu.VMEM((CELLS, SLOTS), F32),
            pltpu.VMEM((CELLS, SLOTS), jnp.int32),
            pltpu.VMEM((CX, CY, CZ), jnp.int32),
            pltpu.SMEM(eps_type.shape, F32),
            pltpu.SMEM(sig_type.shape, F32),
            pltpu.SemaphoreType.DMA((7,)),
        ],
        compiler_params=params(8),
    )(
        hbm(slot_last(positions)),
        hbm(slot_last(charges)),
        hbm(slot_last(types)),
        hbm(counts),
        hbm(eps_type),
        hbm(sig_type),
        hbm(tab["tz"]),
    )
    after = send(first, -1, 0)
    before = send(last, 1, 0)
    above = send(atoms, 0, -1)
    above_after = send(first, -1, -1)
    above_before = send(last, 1, -1)

    spread = pl.pallas_call(
        spread_kernel,
        out_shape=jax.ShapeDtypeStruct((LZ, 1, BLOCK), F32),
        in_specs=[VMEM, VMEM, ANY],
        out_specs=ANY,
        scratch_shapes=[
            pltpu.VMEM((BY, 40, LZ), F32),
            pltpu.VMEM((BLOCK, LZ), F32),
            pltpu.VMEM((LZ, BLOCK), F32),
            pltpu.SemaphoreType.DMA((2,)),
        ],
        compiler_params=params(16),
    )(rows, tz, hbm(tab["plane"]))
    spread, after, before, above, above_after, above_before = lax.optimization_barrier(
        (spread, after, before, above, above_after, above_before)
    )
    blocks = (atoms, before, after, above, above_before, above_after)
    lines = lax.all_to_all(hbm(spread), ("gx", "gy"), split_axis=0, concat_axis=0, tiled=True)
    sums = pair_forces(
        blocks,
        [(0, 0, 0), (0, 0, 1)] + [(a, 1 - a, c) for a in (0, 1) for c in (-1, 0, 1)],
        single=1,
    )
    lines, *sums = lax.optimization_barrier((lines, *sums))

    constants = [hbm(tab[name]) for name in ("tx", "ty", "iy", "ix", "kx2", "ky2")]
    fields = pl.pallas_call(
        plane_kernel,
        out_shape=jax.ShapeDtypeStruct((DX * DY, 1, 3 * BLOCK), F32),
        in_specs=[ANY] * 7,
        out_specs=ANY,
        scratch_shapes=[
            *(pltpu.VMEM(tab[name].shape, BF16) for name in ("tx", "ty", "iy", "ix")),
            *(pltpu.VMEM(tab[name].shape, F32) for name in ("kx2", "ky2")),
            pltpu.VMEM((DX * DY, BLOCK), F32),
            pltpu.VMEM((DX // 2, BY * DY, 128), F32),
            pltpu.VMEM((3, DX * DY, BLOCK), F32),
            pltpu.SemaphoreType.DMA((11,)),
        ],
        compiler_params=params(20),
    )(lines, *constants)
    fields = lax.all_to_all(hbm(fields), ("gx", "gy"), split_axis=0, concat_axis=0, tiled=True)
    here, to_before, to_after, up, up_before, up_after = pair_forces(
        blocks, [(a, 1, c) for a in (-1, 1) for c in (-1, 0, 1)], start=sums
    )
    sides = (
        send(up, 0, 1),
        send(to_after, 1, 0),
        send(up_after, 1, 1),
        send(to_before, -1, 0),
        send(up_before, -1, 1),
    )

    modes, edges = pl.pallas_call(
        weight_kernel,
        out_shape=(
            jax.ShapeDtypeStruct((CX * CY, 2 * LZ, 512), BF16),
            jax.ShapeDtypeStruct((CX * CY, 32, 512), F32),
        ),
        in_specs=[VMEM] * 2,
        out_specs=(VMEM, VMEM),
        compiler_params=params(8),
        cost_estimate=pl.CostEstimate(flops=1 << 28, bytes_accessed=1 << 20, transcendentals=0),
    )(rows, tz)
    fields, here, modes, edges = lax.optimization_barrier((fields, here, modes, edges))
    mesh_force = pl.pallas_call(
        force_kernel,
        out_shape=jax.ShapeDtypeStruct((3, CELLS, SLOTS), F32),
        in_specs=[ANY, VMEM, VMEM, VMEM],
        out_specs=VMEM,
        scratch_shapes=[
            pltpu.VMEM((3, LZ, BLOCK), F32),
            pltpu.VMEM((BLOCK, LZ), F32),
            pltpu.VMEM((3, BY, 40, LZ), F32),
            pltpu.VMEM((3, GROUPS, 128), F32),
            pltpu.SemaphoreType.DMA((3,)),
        ],
        compiler_params=params(20),
    )(fields, modes, edges, tab["swap"])
    mesh_force, here = lax.optimization_barrier((mesh_force, here))
    pair_force = pl.pallas_call(
        join_kernel,
        out_shape=jax.ShapeDtypeStruct((3, CELLS, SLOTS), F32),
        in_specs=[VMEM] * 6,
        out_specs=VMEM,
        compiler_params=params(4),
    )(here, *sides)

    slot_first = lambda a: jnp.moveaxis(a.reshape(3, CX, CY, CZ, SLOTS), -1, 1)
    return slot_first(pair_force), slot_first(mesh_force)


def solution(mesh):
    placed = (
        P(None, None, "gx", "gy", None),
        P(None, "gx", "gy", None),
        P(None, "gx", "gy", None),
        P("gx", "gy", None),
        P(),
        P(),
    )
    return jax.shard_map(
        body,
        mesh=mesh,
        in_specs=placed,
        out_specs=(P(None, None, "gx", "gy", None), P(None, None, "gx", "gy", None)),
        check_vma=False,
    )
```

```python
import functools
import math

import jax
import jax.numpy as jnp
import ml_dtypes
import numpy as np
from jax import lax
from jax.experimental import pallas as pl
from jax.experimental.pallas import tpu as pltpu
from jax.sharding import PartitionSpec as P

CELL = 8
GEWALD = 0.7
CUT = 64.0
F32 = jnp.float32
BF16 = jnp.bfloat16

SLOTS = 32
CX, CY, CZ = 4, 2, 16
CELLS = CX * CY * CZ
COLUMNS = CY * CZ
DX, DY = 8, 16
LX, LY, LZ = 256, 256, 128
BX, BY = CX * CELL + 4, CY * CELL + 4
BLOCK = 768
GROUPS = CELLS // 4
KZ = 48
KX = 64
KY = 384
LENGTH = math.sqrt(GEWALD * GEWALD * math.log2(math.e))
FAR = CUT * LENGTH * LENGTH
SCALES = (LENGTH, LENGTH, LENGTH, 1.0, 1.0 / math.sqrt(8.0 * FAR * LENGTH), 0.5 * LENGTH)
VMEM = pl.BlockSpec(memory_space=pltpu.VMEM)
ANY = pl.BlockSpec(memory_space=pl.ANY)


def params(mib=40):
    return pltpu.CompilerParams(vmem_limit_bytes=mib << 20)


def split(array):
    high = array.astype(ml_dtypes.bfloat16)
    low = (array - high.astype(np.float64)).astype(ml_dtypes.bfloat16)
    return high, low


def left_parts(array):
    high, low = split(array)
    return np.concatenate([high, high, low], axis=-1)


def basis(length):
    half = length // 2
    modes = np.concatenate([np.arange(half + 1), np.arange(1, half)])
    sines = np.arange(length) > half
    return modes, sines


def wave(points, modes, sines, length):
    angle = 2.0 * np.pi * (np.outer(modes, points) % length) / length
    return np.where(sines[:, None], np.sin(angle), np.cos(angle))


def wave_slope(points, modes, sines, length):
    angle = 2.0 * np.pi * (np.outer(modes, points) % length) / length
    k = 2.0 * np.pi * modes / length
    k = np.where(modes == length // 2, 0.0, k)[:, None]
    return np.where(sines[:, None], -k * np.cos(angle), k * np.sin(angle))


def damping(modes, length):
    k = 2.0 * np.pi * modes / length
    return np.exp(-k * k / (4.0 * GEWALD * GEWALD)) / np.sinc(modes / length) ** 8


def norms(modes, length):
    return np.where((modes == 0) | (modes == length // 2), 1.0, 2.0) / length


@functools.cache
def tables():
    mz, sz = basis(LZ)
    tz = np.zeros((4, LZ, KZ))
    for zg in range(4):
        tz[zg, :, :36] = wave(32 * zg - 2 + np.arange(36), mz, sz, LZ)
    mx, sx = basis(LX)
    my, sy = basis(LY)
    tx = np.zeros((DX // 2, 128, LX))
    gain_x = damping(mx, LX) * norms(mx, LX)
    ix = np.zeros((2, LX, DX * BX))
    for gx in range(DX):
        points = gx * CX * CELL - 2 + np.arange(BX)
        at = KX * (gx % 2)
        tx[gx // 2, at : at + BX] = (wave(points, mx, sx, LX) * gain_x[:, None]).T
        ix[0, :, gx * BX : (gx + 1) * BX] = wave(points, mx, sx, LX)
        ix[1, :, gx * BX : (gx + 1) * BX] = wave_slope(points, mx, sx, LX)
    points = (np.arange(DY)[None, :] * CY * CELL - 2 + np.arange(BY)[:, None]).reshape(-1)
    gain_y = damping(my, LY) * norms(my, LY)
    ty = wave(points, my, sy, LY) * gain_y[:, None]
    iy = np.concatenate([wave(points, my, sy, LY).T, wave_slope(points, my, sy, LY).T])
    kz = 2.0 * np.pi * mz / LZ
    plane = np.zeros((8, LZ))
    plane[6:] = kz * kz, 4.0 * np.pi * damping(mz, LZ) * norms(mz, LZ)
    half = LZ // 2
    swap = 2.0 * np.pi * np.arange(half) / LZ
    swap = np.concatenate([-swap, swap]).astype(np.float32)[None, :]
    return dict(
        tz=left_parts(tz),
        tx=np.concatenate(split(tx), axis=1).reshape(-1, LX),
        ty=np.concatenate(split(np.pad(ty, ((0, 0), (0, KY - BY * DY)))), axis=1),
        iy=np.concatenate(split(iy), axis=1),
        ix=np.concatenate(split(np.concatenate([ix[0], ix[1]], axis=1))),
        plane=plane.astype(np.float32),
        swap=swap,
    )


def halves(value):
    high = value.astype(BF16)
    return high, (value - high.astype(F32)).astype(BF16)


def left_split(value):
    high, low = halves(value)
    return jnp.concatenate([high, high, low], axis=1)


def right_split(value, axis=0):
    high, low = halves(value)
    return jnp.concatenate([high, low, high], axis=axis)


def dot(left, right, dims=((1,), (0,))):
    return lax.dot_general(left, right, (dims, ((), ())), preferred_element_type=F32)


def spline(offset):
    span = jnp.abs(offset)
    outer = jnp.maximum(2.0 - span, 0.0)
    inner = jnp.maximum(1.0 - span, 0.0)
    return (outer * outer * outer) * (1.0 / 6.0) - (inner * inner * inner) * (2.0 / 3.0)


def weights(rows_ref, tz_ref, col):
    point = (lax.broadcasted_iota(jnp.int32, (16, 128), 0) - 2).astype(F32)
    point_z = (lax.broadcasted_iota(jnp.int32, (KZ, 128), 0) - 2).astype(F32)
    shift = ((lax.broadcasted_iota(jnp.int32, (1, 128), 1) // SLOTS) * CELL).astype(F32)
    modes, edges = [], []
    for zg in range(4):
        row = [rows_ref[c, pl.ds(col * 4 + zg, 1), :] for c in range(4)]
        along_x = spline(row[0] - point)
        along_y = spline(row[1] - point) * row[3]
        along_z = spline(row[2] + shift - point_z)
        modes.append(dot(tz_ref[zg], right_split(along_z)))
        edges.append(jnp.concatenate([along_x, along_y], axis=0))
    return jnp.concatenate(modes, axis=1), jnp.concatenate(edges, axis=1)


def products(edges):
    return (edges[16:28][:, None, :] * edges[:16][None, :, :]).reshape(192, edges.shape[1])


def started(*copies):
    copies = [pltpu.make_async_copy(*copy) for copy in copies]
    for copy in copies:
        copy.start()
    return copies


def table_kernel(*refs):
    sources, (atoms_ref, first_ref, last_ref, rows_ref, tz_ref) = refs[:7], refs[7:12]
    pos_ref, charge_ref, type_ref, count_ref, eps_ref, sig_ref, sems = refs[12:]
    targets = refs[12:18] + (tz_ref,)
    incoming = started(*((s, t, sems.at[n]) for n, (s, t) in enumerate(zip(sources, targets))))
    for copy in incoming[:-1]:
        copy.wait()
    slots = lax.broadcasted_iota(jnp.int32, (SLOTS, CELLS), 0)
    counts = [count_ref[cx, cy : cy + 1, :] for cx in range(CX) for cy in range(CY)]
    occupied = slots < jnp.concatenate(counts, axis=1)
    kinds = type_ref[...].T
    eps = jnp.zeros((SLOTS, CELLS), F32)
    sig = jnp.zeros((SLOTS, CELLS), F32)
    for kind in range(eps_ref.shape[0]):
        match = kinds == kind
        eps = jnp.where(match, eps_ref[kind], eps)
        sig = jnp.where(match, sig_ref[kind], sig)
    charge = jnp.where(occupied, charge_ref[...].T, 0.0)
    root = jnp.where(occupied, jnp.sqrt(eps), 0.0)
    for c, value in enumerate([pos_ref[d].T for d in range(3)] + [charge, root, sig]):
        value = value * SCALES[c]
        atoms_ref[c] = value
        first_ref[c] = value[:, :COLUMNS]
        last_ref[c] = value[:, CELLS - COLUMNS :]
    charge = charge.T
    for c in range(4):
        value = pos_ref[c] if c < 3 else charge
        value = value.reshape(GROUPS, 4, SLOTS)
        rows_ref[c] = jnp.concatenate([value[:, s, :] for s in range(4)], axis=1)
    incoming[-1].wait()


def spread_kernel(rows_ref, tz_ref, plane_ref, spread_out, total, packed, turned, sems):
    (plane,) = started((plane_ref, packed.at[BLOCK - 8 :, :], sems.at[0]))
    total[...] = jnp.zeros_like(total)

    def column(col, carry):
        modes, edges = weights(rows_ref, tz_ref, col)
        part = dot(left_split(products(edges)), right_split(modes, 1), ((1,), (1,)))
        y = (col % CY) * CELL
        x = pl.multiple_of((col // CY) * CELL, CELL)
        total[pl.ds(y, 12), pl.ds(x, 16), :] += part.reshape(12, 16, LZ)
        return carry

    lax.fori_loop(0, CX * CY, column, 0, unroll=4)
    for y in range(BY):
        packed[y * BX : (y + 1) * BX, :] = total[y, :BX, :]
    packed[BX * BY : BLOCK - 8, :] = jnp.zeros((BLOCK - 8 - BX * BY, LZ), F32)
    plane.wait()
    outgoing = []
    for n in range(BLOCK // 128):
        part = pl.ds(128 * n, 128)
        turned[:, part] = packed[part, :].T
        outgoing += started((turned.at[:, part], spread_out.at[:, 0, part], sems.at[1 + n]))
    for copy in outgoing:
        copy.wait()


def weight_kernel(rows_ref, tz_ref, modes_ref, edges_ref):
    def column(col, carry):
        modes, edges_ref[col] = weights(rows_ref, tz_ref, col)
        modes_ref[col] = jnp.concatenate(halves(modes), axis=0)
        return carry

    lax.fori_loop(0, CX * CY, column, 0, unroll=4)


def plane_kernel(in_ref, *refs):
    sources, out_ref, held = refs[:4], refs[4], refs[5:9]
    lines, stacked, turned, sems = refs[9:]
    tx, ty, iy, ix = held
    (arrival,) = started((in_ref.at[:, 0, :], lines, sems.at[3]))
    copies = [(s, t, sems.at[4 + n]) for n, (s, t) in enumerate(zip(sources, held))]
    constants = started(*copies[:2])
    arrival.wait()
    constants += started(*copies[2:])
    kz2, gain = lines[:1, BLOCK - 2 : BLOCK - 1], lines[:1, BLOCK - 1 :]
    for y in range(BY):
        value = lines[:, y * BX : y * BX + KX]
        for gx in range(DX):
            at = KX * (gx % 2)
            stacked[gx // 2, y * DY : (y + 1) * DY, at : at + KX] = value[gx * DY : (gx + 1) * DY]
    pairs = jnp.concatenate([left_split(stacked[n]) for n in range(DX // 2)], axis=1)
    constants[0].wait()
    table = []
    for n in range(DX // 2):
        table += [tx[256 * n : 256 * (n + 1)], tx[256 * n : 256 * n + 128]]
    high, low = halves(dot(pairs, jnp.concatenate(table, axis=0)))
    empty = jnp.zeros((KY - BY * DY, LX), BF16)
    constants[1].wait()
    modes = dot(
        jnp.concatenate([ty[:, :KY], ty[:, :KY], ty[:, KY:]], axis=1),
        jnp.concatenate([high, empty, low, empty, high, empty], axis=0),
    )
    k2 = kz2
    for axis, length in ((0, LY), (1, LX)):
        mode = lax.broadcasted_iota(jnp.int32, (LY, LX), axis)
        mode = jnp.where(mode > length // 2, mode - length // 2, mode).astype(F32)
        k = mode * (2.0 * math.pi / length)
        k2 = k2 + k * k
    positive = k2 > 0.0
    modes = jnp.where(positive, modes * (gain / jnp.where(positive, k2, 1.0)), 0.0)
    constants[2].wait()
    table = [iy[:, :LY], iy[:, :LY], iy[:, LY:]]
    both = dot(jnp.concatenate(table, axis=1), right_split(modes))
    constants[3].wait()
    rows = BY * DY
    width = DX * BX
    table = jnp.concatenate([ix[...], ix[:LX]], axis=0)
    plain = dot(left_split(both[:rows]), table)
    slope = dot(left_split(both[rows:]), table[:, :width])
    fields = (plain[:, width:], slope, plain[:, :width])
    outgoing = []
    for d in range(3):
        turned[d, :, BX * BY :] = jnp.zeros((DX * DY, BLOCK - BX * BY), F32)
        for gx in range(DX):
            piece = fields[d][:, gx * BX : (gx + 1) * BX]
            for y in range(BY):
                lane = y * BX
                turned[d, gx * DY : (gx + 1) * DY, lane : lane + BX] = piece[y * DY : (y + 1) * DY]
            part = pl.ds(gx * DY, DY)
            outgoing += started(
                (
                    turned.at[d, part],
                    out_ref.at[part, 0, d * BLOCK : (d + 1) * BLOCK],
                    sems.at[10 + d * DX + gx],
                )
            )
    for copy in outgoing:
        copy.wait()


def force_kernel(
    in_ref, modes_ref, edges_ref, swap_ref, out_ref, turned, packed, padded, rows_out, sems
):
    incoming = started(
        *(
            (in_ref.at[:, 0, d * BLOCK : (d + 1) * BLOCK], turned.at[d], sems.at[d])
            for d in range(3)
        )
    )
    for d in range(3):
        incoming[d].wait()
        value = turned[d].T
        if d == 2:
            value = pltpu.roll(value, LZ // 2, 1) * swap_ref[...]
        packed[...] = value
        for y in range(BY):
            padded[d, y, :BX, :] = packed[y * BX : (y + 1) * BX, :]
            padded[d, y, BX:, :] = jnp.zeros((40 - BX, LZ), F32)

    def column(col, carry):
        y = (col % CY) * CELL
        x = pl.multiple_of((col // CY) * CELL, CELL)
        planes = products(edges_ref[col])
        modes = modes_ref[col]
        modes = jnp.concatenate([modes, modes[:LZ]], axis=0)
        for d in range(3):
            block = padded[d, pl.ds(y, 12), pl.ds(x, 16), :].reshape(192, LZ)
            along = dot(left_split(block), modes)
            force = jnp.sum(along * planes, axis=0, keepdims=True)
            for zg in range(4):
                rows_out[d, pl.ds(col * 4 + zg, 1), :] = force[:, 128 * zg : 128 * (zg + 1)]
        return carry

    lax.fori_loop(0, CX * CY, column, 0, unroll=4)
    for d in range(3):
        value = rows_out[d]
        pieces = [value[:, s * SLOTS : (s + 1) * SLOTS][:, None, :] for s in range(4)]
        out_ref[d] = jnp.concatenate(pieces, axis=1).reshape(CELLS, SLOTS)


COULOMB = (
    -0.006156452396320011,
    -0.0004198503476764426,
    0.4251962050951751,
    -0.035971568956237085,
    0.5422242920959217,
    -0.3965913855606964,
    0.1962617265017834,
    -0.05766279059061346,
    0.007452967624700701,
)


def pair_term(own, other):
    dx = other[0] - own[0]
    dy = other[1] - own[1]
    dz = other[2] - own[2]
    r2 = dx * dx + dy * dy + dz * dz
    gap = FAR - r2
    fade = jnp.maximum(gap, 0.0)
    t = lax.rsqrt(r2 + LENGTH * LENGTH)
    scale = -2.0 * math.exp(-GEWALD * GEWALD) * 2.0**-FAR / (FAR * LENGTH)
    terms = [scale * c * LENGTH**n for n, c in enumerate(COULOMB)]
    poly = terms[-1] * t + terms[-2]
    for c in terms[-3::-1]:
        poly = poly * t + c
    sigma = own[5] + other[5]
    square = sigma * sigma
    inverse = 1.0 / (r2 + square)
    x = square * inverse
    x3 = x * x * x
    rest = 1.0 - (x3 + x3)
    lj = x3 * (rest * ((fade * inverse) * 3.0 + 1.0) + 1.0)
    w = fade * ((own[4] * other[4]) * lj + (own[3] * other[3]) * (jnp.exp2(gap) * poly))
    return w * dx, w * dy, w * dz


def shifted_z(value, at_z, step):
    if step == 0:
        return value
    if step > 0:
        return jnp.where(
            at_z == CZ - 1, pltpu.roll(value, CZ - 1, 1), pltpu.roll(value, CELLS - 1, 1)
        )
    return jnp.where(at_z == 0, pltpu.roll(value, CELLS - CZ + 1, 1), pltpu.roll(value, 1, 1))


def pair_kernel(*refs, passes, single, sources, begun, unroll):
    blocks, start, outs = refs[:sources], refs[sources : sources + begun], refs[sources + begun : -3]
    others, own, back = refs[-3:]
    low = (lax.broadcasted_iota(jnp.int32, (SLOTS, 256), 1) & CZ) == 0
    at_z = lax.broadcasted_iota(jnp.int32, (SLOTS, CELLS), 1) & (CZ - 1)
    empty = jnp.zeros((SLOTS, 64), F32)
    for c in range(6):
        wide = jnp.concatenate([blocks[1][c], blocks[0][c], blocks[2][c], empty], axis=1)
        own[c] = blocks[0][c]
        layers = {0: wide}
        if sources > 3:
            above = jnp.concatenate([blocks[4][c], blocks[3][c], blocks[5][c], empty], axis=1)
            layers[1] = jnp.where(low, pltpu.roll(wide, 256 - CZ, 1), pltpu.roll(above, CZ, 1))
        for n, offset in enumerate(passes):
            at = COLUMNS * (offset[0] + 1)
            value = layers[offset[1]][:, at : at + CELLS]
            value = shifted_z(value, at_z, offset[2])
            others[c, n * SLOTS : (n + 1) * SLOTS] = (
                value + offset[c] * CELL * LENGTH if c < 3 else value
            )

    def step(n, sums, reverse):
        sums = list(sums)
        for jj in range(unroll):
            j = n * unroll + jj
            other = [others[c, pl.ds(j, 8, stride=0), :] for c in range(6)]
            total = [None] * 3
            for block in range(4):
                mine = [own[c, 8 * block : 8 * block + 8, :] for c in range(6)]
                force = pair_term(mine, other)
                for d in range(3):
                    sums[block * 3 + d] = sums[block * 3 + d] + force[d]
                    total[d] = force[d] if block == 0 else total[d] + force[d]
            if reverse:
                for d in range(3):
                    back[d, pl.ds(pl.multiple_of((j - single * SLOTS) * 8, 8), 8), :] = total[d]
        return tuple(sums)

    per = SLOTS // unroll
    sums = (jnp.zeros((8, CELLS), F32),) * 12
    sums = lax.fori_loop(0, single * per, functools.partial(step, reverse=False), sums)
    sums = lax.fori_loop(
        single * per, len(passes) * per, functools.partial(step, reverse=True), sums
    )
    nothing = jnp.zeros((SLOTS, 128), F32)
    for d in range(3):
        force = jnp.concatenate([sums[block * 3 + d] for block in range(4)], axis=0)
        here = pltpu.roll(jnp.concatenate([force, nothing], axis=1), COLUMNS, 1)
        there = jnp.zeros((SLOTS, 256), F32)
        for n, offset in enumerate(passes):
            if n < single:
                continue
            base = (n - single) * SLOTS * 8
            value = back[d, pl.ds(base, SLOTS, stride=8), :]
            for s in range(1, 8):
                value = value + back[d, pl.ds(base + s, SLOTS, stride=8), :]
            value = shifted_z(value, at_z, -offset[2])
            value = jnp.concatenate([value, nothing], axis=1)
            at = COLUMNS * (offset[0] + 1)
            if offset[1]:
                here = here - pltpu.roll(jnp.where(low, value, 0.0), at + CZ, 1)
                there = there - pltpu.roll(jnp.where(low, 0.0, value), (at - CZ) % 256, 1)
            else:
                here = here - pltpu.roll(value, at, 1)
        if not begun:
            outs[0][d] = here
            outs[1][d] = there
            continue
        here = here + start[0][d]
        there = there + start[1][d]
        for at, total in ((0, here), (3, there)):
            outs[at][d] = total[:, COLUMNS : COLUMNS + CELLS]
            outs[at + 1][d] = total[:, :COLUMNS]
            outs[at + 2][d] = total[:, COLUMNS + CELLS : 2 * COLUMNS + CELLS]


def pair_forces(blocks, passes, single=0, start=(), unroll=8):
    rows = len(passes) * SLOTS
    pairs = rows * SLOTS * CELLS
    widths = (CELLS, COLUMNS, COLUMNS) * 2 if start else (256, 256)
    return pl.pallas_call(
        functools.partial(
            pair_kernel,
            passes=tuple(passes),
            single=single,
            sources=len(blocks),
            begun=len(start),
            unroll=unroll,
        ),
        out_shape=[jax.ShapeDtypeStruct((3, SLOTS, width), F32) for width in widths],
        in_specs=[VMEM] * (len(blocks) + len(start)),
        out_specs=[VMEM] * len(widths),
        scratch_shapes=[
            pltpu.VMEM((6, rows + 8, CELLS), F32),
            pltpu.VMEM((6, SLOTS, CELLS), F32),
            pltpu.VMEM((3, (rows - single * SLOTS) * 8, CELLS), F32),
        ],
        compiler_params=params(8),
        cost_estimate=pl.CostEstimate(flops=70 * pairs, bytes_accessed=1 << 20, transcendentals=0),
    )(*blocks, *start)


def join_kernel(here_ref, down_ref, first_a, first_b, last_a, last_b, out_ref):
    middle = jnp.zeros((SLOTS, CELLS - 2 * COLUMNS), F32)
    for d in range(3):
        sides = [first_a[d] + first_b[d], middle, last_a[d] + last_b[d]]
        out_ref[d] = (here_ref[d] + down_ref[d] + jnp.concatenate(sides, axis=1)).T


def hbm(array):
    return pltpu.with_memory_space_constraint(jnp.asarray(array), pltpu.HBM)


def send(value, step_x, step_y):
    route = [
        (x * DY + y, (x + step_x) % DX * DY + (y + step_y) % DY)
        for x in range(DX)
        for y in range(DY)
    ]
    return lax.ppermute(value, ("gx", "gy"), route)


def body(positions, charges, types, counts, eps_type, sig_type):
    tab = tables()
    slot_last = lambda a: jnp.moveaxis(a, -4, -1).reshape(a.shape[:-4] + (CELLS, SLOTS))
    side = jax.ShapeDtypeStruct((6, SLOTS, COLUMNS), F32)
    atoms, first, last, rows, tz = pl.pallas_call(
        table_kernel,
        out_shape=(
            jax.ShapeDtypeStruct((6, SLOTS, CELLS), F32),
            side,
            side,
            jax.ShapeDtypeStruct((4, GROUPS, 128), F32),
            jax.ShapeDtypeStruct(tab["tz"].shape, BF16),
        ),
        in_specs=[ANY] * 7,
        out_specs=(VMEM,) * 5,
        scratch_shapes=[
            pltpu.VMEM((3, CELLS, SLOTS), F32),
            pltpu.VMEM((CELLS, SLOTS), F32),
            pltpu.VMEM((CELLS, SLOTS), jnp.int32),
            pltpu.VMEM((CX, CY, CZ), jnp.int32),
            pltpu.SMEM(eps_type.shape, F32),
            pltpu.SMEM(sig_type.shape, F32),
            pltpu.SemaphoreType.DMA((7,)),
        ],
        compiler_params=params(8),
    )(
        hbm(slot_last(positions)),
        hbm(slot_last(charges)),
        hbm(slot_last(types)),
        hbm(counts),
        hbm(eps_type),
        hbm(sig_type),
        hbm(tab["tz"]),
    )
    after = send(first, -1, 0)
    before = send(last, 1, 0)
    above = send(atoms, 0, -1)
    above_after = send(first, -1, -1)
    above_before = send(last, 1, -1)

    spread = pl.pallas_call(
        spread_kernel,
        out_shape=jax.ShapeDtypeStruct((LZ, 1, BLOCK), F32),
        in_specs=[VMEM, VMEM, ANY],
        out_specs=ANY,
        scratch_shapes=[
            pltpu.VMEM((BY, 40, LZ), F32),
            pltpu.VMEM((BLOCK, LZ), F32),
            pltpu.VMEM((LZ, BLOCK), F32),
            pltpu.SemaphoreType.DMA((1 + BLOCK // 128,)),
        ],
        compiler_params=params(16),
    )(rows, tz, hbm(tab["plane"]))
    spread, after, before, above, above_after, above_before = lax.optimization_barrier(
        (spread, after, before, above, above_after, above_before)
    )
    blocks = (atoms, before, after, above, above_before, above_after)
    lines = lax.all_to_all(hbm(spread), ("gx", "gy"), split_axis=0, concat_axis=0, tiled=True)
    sums = pair_forces(
        blocks,
        [(0, 0, 0), (0, 0, 1), (1, 0, -1), (1, 0, 0), (1, 0, 1), (0, 1, -1), (0, 1, 0)],
        single=1,
    )
    lines, *sums = lax.optimization_barrier((lines, *sums))

    constants = [hbm(tab[name]) for name in ("tx", "ty", "iy", "ix")]
    fields = pl.pallas_call(
        plane_kernel,
        out_shape=jax.ShapeDtypeStruct((DX * DY, 1, 3 * BLOCK), F32),
        in_specs=[ANY] * 5,
        out_specs=ANY,
        scratch_shapes=[
            *(pltpu.VMEM(tab[name].shape, BF16) for name in ("tx", "ty", "iy", "ix")),
            pltpu.VMEM((DX * DY, BLOCK), F32),
            pltpu.VMEM((DX // 2, BY * DY, 128), F32),
            pltpu.VMEM((3, DX * DY, BLOCK), F32),
            pltpu.SemaphoreType.DMA((10 + 3 * DX,)),
        ],
        compiler_params=params(20),
    )(lines, *constants)
    fields = lax.all_to_all(hbm(fields), ("gx", "gy"), split_axis=0, concat_axis=0, tiled=True)
    here, to_before, to_after, up, up_before, up_after = pair_forces(
        blocks, [(0, 1, 1)] + [(a, 1, c) for a in (-1, 1) for c in (-1, 0, 1)], start=sums
    )
    sides = (
        send(up, 0, 1),
        send(to_after, 1, 0),
        send(up_after, 1, 1),
        send(to_before, -1, 0),
        send(up_before, -1, 1),
    )

    modes, edges = pl.pallas_call(
        weight_kernel,
        out_shape=(
            jax.ShapeDtypeStruct((CX * CY, 2 * LZ, 512), BF16),
            jax.ShapeDtypeStruct((CX * CY, 32, 512), F32),
        ),
        in_specs=[VMEM] * 2,
        out_specs=(VMEM, VMEM),
        compiler_params=params(8),
        cost_estimate=pl.CostEstimate(flops=1 << 28, bytes_accessed=1 << 20, transcendentals=0),
    )(rows, tz)
    fields, here, modes, edges = lax.optimization_barrier((fields, here, modes, edges))
    mesh_force = pl.pallas_call(
        force_kernel,
        out_shape=jax.ShapeDtypeStruct((3, CELLS, SLOTS), F32),
        in_specs=[ANY, VMEM, VMEM, VMEM],
        out_specs=VMEM,
        scratch_shapes=[
            pltpu.VMEM((3, LZ, BLOCK), F32),
            pltpu.VMEM((BLOCK, LZ), F32),
            pltpu.VMEM((3, BY, 40, LZ), F32),
            pltpu.VMEM((3, GROUPS, 128), F32),
            pltpu.SemaphoreType.DMA((3,)),
        ],
        compiler_params=params(20),
    )(fields, modes, edges, tab["swap"])
    mesh_force, here = lax.optimization_barrier((mesh_force, here))
    pair_force = pl.pallas_call(
        join_kernel,
        out_shape=jax.ShapeDtypeStruct((3, CELLS, SLOTS), F32),
        in_specs=[VMEM] * 6,
        out_specs=VMEM,
        compiler_params=params(4),
    )(here, *sides)

    slot_first = lambda a: jnp.moveaxis(a.reshape(3, CX, CY, CZ, SLOTS), -1, 1)
    return slot_first(pair_force), slot_first(mesh_force)


def solution(mesh):
    placed = (
        P(None, None, "gx", "gy", None),
        P(None, "gx", "gy", None),
        P(None, "gx", "gy", None),
        P("gx", "gy", None),
        P(),
        P(),
    )
    return jax.shard_map(
        body,
        mesh=mesh,
        in_specs=placed,
        out_specs=(P(None, None, "gx", "gy", None), P(None, None, "gx", "gy", None)),
        check_vma=False,
    )
```

```python
import functools
import math

import jax
import jax.numpy as jnp
import ml_dtypes
import numpy as np
from jax import lax
from jax.experimental import pallas as pl
from jax.experimental.pallas import tpu as pltpu
from jax.sharding import PartitionSpec as P

CELL = 8
GEWALD = 0.7
CUT = 64.0
F32 = jnp.float32
BF16 = jnp.bfloat16

SLOTS = 32
CX, CY, CZ = 4, 2, 16
CELLS = CX * CY * CZ
COLUMNS = CY * CZ
DX, DY = 8, 16
LX, LY, LZ = 256, 256, 128
BX, BY = CX * CELL + 4, CY * CELL + 4
BLOCK = 768
GROUPS = CELLS // 4
KZ = 48
KX = 64
KY = 384
LENGTH = math.sqrt(GEWALD * GEWALD * math.log2(math.e))
FAR = CUT * LENGTH * LENGTH
SCALES = (LENGTH, LENGTH, LENGTH, 1.0, 1.0 / math.sqrt(8.0 * FAR * LENGTH), 0.5 * LENGTH)
VMEM = pl.BlockSpec(memory_space=pltpu.VMEM)
ANY = pl.BlockSpec(memory_space=pl.ANY)


def params(mib=40):
    return pltpu.CompilerParams(vmem_limit_bytes=mib << 20)


def split(array):
    high = array.astype(ml_dtypes.bfloat16)
    low = (array - high.astype(np.float64)).astype(ml_dtypes.bfloat16)
    return high, low


def left_parts(array):
    high, low = split(array)
    return np.concatenate([high, high, low], axis=-1)


def basis(length):
    half = length // 2
    modes = np.concatenate([np.arange(half + 1), np.arange(1, half)])
    sines = np.arange(length) > half
    return modes, sines


def wave(points, modes, sines, length):
    angle = 2.0 * np.pi * (np.outer(modes, points) % length) / length
    return np.where(sines[:, None], np.sin(angle), np.cos(angle))


def wave_slope(points, modes, sines, length):
    angle = 2.0 * np.pi * (np.outer(modes, points) % length) / length
    k = 2.0 * np.pi * modes / length
    k = np.where(modes == length // 2, 0.0, k)[:, None]
    return np.where(sines[:, None], -k * np.cos(angle), k * np.sin(angle))


def damping(modes, length):
    k = 2.0 * np.pi * modes / length
    return np.exp(-k * k / (4.0 * GEWALD * GEWALD)) / np.sinc(modes / length) ** 8


def norms(modes, length):
    return np.where((modes == 0) | (modes == length // 2), 1.0, 2.0) / length


@functools.cache
def tables():
    mz, sz = basis(LZ)
    tz = np.zeros((4, LZ, KZ))
    for zg in range(4):
        tz[zg, :, :36] = wave(32 * zg - 2 + np.arange(36), mz, sz, LZ)
    mx, sx = basis(LX)
    my, sy = basis(LY)
    tx = np.zeros((DX // 2, 128, LX))
    gain_x = damping(mx, LX) * norms(mx, LX)
    ix = np.zeros((2, LX, DX * BX))
    for gx in range(DX):
        points = gx * CX * CELL - 2 + np.arange(BX)
        at = KX * (gx % 2)
        tx[gx // 2, at : at + BX] = (wave(points, mx, sx, LX) * gain_x[:, None]).T
        ix[0, :, gx * BX : (gx + 1) * BX] = wave(points, mx, sx, LX)
        ix[1, :, gx * BX : (gx + 1) * BX] = wave_slope(points, mx, sx, LX)
    points = (np.arange(DY)[None, :] * CY * CELL - 2 + np.arange(BY)[:, None]).reshape(-1)
    gain_y = damping(my, LY) * norms(my, LY)
    ty = wave(points, my, sy, LY) * gain_y[:, None]
    iy = np.concatenate([wave(points, my, sy, LY).T, wave_slope(points, my, sy, LY).T])
    kz = 2.0 * np.pi * mz / LZ
    plane = np.zeros((8, LZ))
    plane[6:] = kz * kz, 4.0 * np.pi * damping(mz, LZ) * norms(mz, LZ)
    half = LZ // 2
    swap = 2.0 * np.pi * np.arange(half) / LZ
    swap = np.concatenate([-swap, swap]).astype(np.float32)[None, :]
    return dict(
        tz=left_parts(tz),
        tx=np.concatenate(split(tx), axis=1).reshape(-1, LX),
        ty=np.concatenate(split(np.pad(ty, ((0, 0), (0, KY - BY * DY)))), axis=1),
        iy=np.concatenate(split(iy), axis=1),
        ix=np.concatenate(split(np.concatenate([ix[0], ix[1]], axis=1))),
        plane=plane.astype(np.float32),
        swap=swap,
    )


def halves(value):
    high = value.astype(BF16)
    return high, (value - high.astype(F32)).astype(BF16)


def left_split(value):
    high, low = halves(value)
    return jnp.concatenate([high, high, low], axis=1)


def right_split(value, axis=0):
    high, low = halves(value)
    return jnp.concatenate([high, low, high], axis=axis)


def dot(left, right, dims=((1,), (0,))):
    return lax.dot_general(left, right, (dims, ((), ())), preferred_element_type=F32)


def spline(offset):
    span = jnp.abs(offset)
    outer = jnp.maximum(2.0 - span, 0.0)
    inner = jnp.maximum(1.0 - span, 0.0)
    return (outer * outer * outer) * (1.0 / 6.0) - (inner * inner * inner) * (2.0 / 3.0)


def weights(rows_ref, tz_ref, col):
    point = (lax.broadcasted_iota(jnp.int32, (16, 128), 0) - 2).astype(F32)
    point_z = (lax.broadcasted_iota(jnp.int32, (KZ, 128), 0) - 2).astype(F32)
    shift = ((lax.broadcasted_iota(jnp.int32, (1, 128), 1) // SLOTS) * CELL).astype(F32)
    modes, edges = [], []
    for zg in range(4):
        row = [rows_ref[c, pl.ds(col * 4 + zg, 1), :] for c in range(4)]
        along_x = spline(row[0] - point)
        along_y = spline(row[1] - point) * row[3]
        along_z = spline(row[2] + shift - point_z)
        modes.append(dot(tz_ref[zg], right_split(along_z)))
        edges.append(jnp.concatenate([along_x, along_y], axis=0))
    return jnp.concatenate(modes, axis=1), jnp.concatenate(edges, axis=1)


def products(edges):
    return (edges[16:28][:, None, :] * edges[:16][None, :, :]).reshape(192, edges.shape[1])


def started(*copies):
    copies = [pltpu.make_async_copy(*copy) for copy in copies]
    for copy in copies:
        copy.start()
    return copies


def table_kernel(*refs):
    sources, (atoms_ref, first_ref, last_ref, rows_ref, tz_ref) = refs[:7], refs[7:12]
    pos_ref, charge_ref, type_ref, count_ref, eps_ref, sig_ref, sems = refs[12:]
    targets = refs[12:18] + (tz_ref,)
    incoming = started(*((s, t, sems.at[n]) for n, (s, t) in enumerate(zip(sources, targets))))
    for copy in incoming[:-1]:
        copy.wait()
    slots = lax.broadcasted_iota(jnp.int32, (SLOTS, CELLS), 0)
    counts = [count_ref[cx, cy : cy + 1, :] for cx in range(CX) for cy in range(CY)]
    occupied = slots < jnp.concatenate(counts, axis=1)
    kinds = type_ref[...].T
    eps = jnp.zeros((SLOTS, CELLS), F32)
    sig = jnp.zeros((SLOTS, CELLS), F32)
    for kind in range(eps_ref.shape[0]):
        match = kinds == kind
        eps = jnp.where(match, eps_ref[kind], eps)
        sig = jnp.where(match, sig_ref[kind], sig)
    charge = jnp.where(occupied, charge_ref[...].T, 0.0)
    root = jnp.where(occupied, jnp.sqrt(eps), 0.0)
    for c, value in enumerate([pos_ref[d].T for d in range(3)] + [charge, root, sig]):
        value = value * SCALES[c]
        atoms_ref[c] = value
        first_ref[c] = value[:, :COLUMNS]
        last_ref[c] = value[:, CELLS - COLUMNS :]
    charge = charge.T
    for c in range(4):
        value = pos_ref[c] if c < 3 else charge
        value = value.reshape(GROUPS, 4, SLOTS)
        rows_ref[c] = jnp.concatenate([value[:, s, :] for s in range(4)], axis=1)
    incoming[-1].wait()


def spread_kernel(rows_ref, tz_ref, plane_ref, spread_out, total, packed, turned, sems):
    (plane,) = started((plane_ref, packed.at[BLOCK - 8 :, :], sems.at[0]))
    total[...] = jnp.zeros_like(total)

    def column(col, carry):
        modes, edges = weights(rows_ref, tz_ref, col)
        part = dot(left_split(products(edges)), right_split(modes, 1), ((1,), (1,)))
        y = (col % CY) * CELL
        x = pl.multiple_of((col // CY) * CELL, CELL)
        total[pl.ds(y, 12), pl.ds(x, 16), :] += part.reshape(12, 16, LZ)
        return carry

    lax.fori_loop(0, CX * CY, column, 0, unroll=8)
    for y in range(BY):
        packed[y * BX : (y + 1) * BX, :] = total[y, :BX, :]
    packed[BX * BY : BLOCK - 8, :] = jnp.zeros((BLOCK - 8 - BX * BY, LZ), F32)
    plane.wait()
    turned[...] = packed[...].T
    for copy in started((turned, spread_out.at[:, 0, :], sems.at[1])):
        copy.wait()


def weight_kernel(rows_ref, tz_ref, modes_ref, edges_ref):
    def column(col, carry):
        modes, edges_ref[col] = weights(rows_ref, tz_ref, col)
        modes_ref[col] = jnp.concatenate(halves(modes), axis=0)
        return carry

    lax.fori_loop(0, CX * CY, column, 0, unroll=8)


def plane_kernel(in_ref, *refs):
    sources, out_ref, held = refs[:4], refs[4], refs[5:9]
    lines, stacked, turned, sems = refs[9:]
    tx, ty, iy, ix = held
    (arrival,) = started((in_ref.at[:, 0, :], lines, sems.at[3]))
    copies = [(s, t, sems.at[4 + n]) for n, (s, t) in enumerate(zip(sources, held))]
    constants = started(*copies[:2])
    arrival.wait()
    constants += started(*copies[2:])
    kz2, gain = lines[:1, BLOCK - 2 : BLOCK - 1], lines[:1, BLOCK - 1 :]
    for y in range(BY):
        value = lines[:, y * BX : y * BX + KX]
        for gx in range(DX):
            at = KX * (gx % 2)
            stacked[gx // 2, y * DY : (y + 1) * DY, at : at + KX] = value[gx * DY : (gx + 1) * DY]
    pairs = jnp.concatenate([left_split(stacked[n]) for n in range(DX // 2)], axis=1)
    constants[0].wait()
    table = []
    for n in range(DX // 2):
        table += [tx[256 * n : 256 * (n + 1)], tx[256 * n : 256 * n + 128]]
    high, low = halves(dot(pairs, jnp.concatenate(table, axis=0)))
    empty = jnp.zeros((KY - BY * DY, LX), BF16)
    constants[1].wait()
    modes = dot(
        jnp.concatenate([ty[:, :KY], ty[:, :KY], ty[:, KY:]], axis=1),
        jnp.concatenate([high, empty, low, empty, high, empty], axis=0),
    )
    k2 = kz2
    for axis, length in ((0, LY), (1, LX)):
        mode = lax.broadcasted_iota(jnp.int32, (LY, LX), axis)
        mode = jnp.where(mode > length // 2, mode - length // 2, mode).astype(F32)
        k = mode * (2.0 * math.pi / length)
        k2 = k2 + k * k
    positive = k2 > 0.0
    modes = jnp.where(positive, modes * (gain / jnp.where(positive, k2, 1.0)), 0.0)
    constants[2].wait()
    table = [iy[:, :LY], iy[:, :LY], iy[:, LY:]]
    both = dot(jnp.concatenate(table, axis=1), right_split(modes))
    constants[3].wait()
    rows = BY * DY
    width = DX * BX
    table = jnp.concatenate([ix[...], ix[:LX]], axis=0)
    plain = dot(left_split(both[:rows]), table)
    slope = dot(left_split(both[rows:]), table[:, :width])
    fields = (plain[:, width:], slope, plain[:, :width])
    outgoing = []
    for d in range(3):
        turned[d, :, BX * BY :] = jnp.zeros((DX * DY, BLOCK - BX * BY), F32)
        for gx in range(DX):
            piece = fields[d][:, gx * BX : (gx + 1) * BX]
            for y in range(BY):
                lane = y * BX
                turned[d, gx * DY : (gx + 1) * DY, lane : lane + BX] = piece[y * DY : (y + 1) * DY]
        outgoing += started(
            (turned.at[d], out_ref.at[:, 0, d * BLOCK : (d + 1) * BLOCK], sems.at[d])
        )
    for copy in outgoing:
        copy.wait()


def force_kernel(
    in_ref, modes_ref, edges_ref, swap_ref, out_ref, turned, packed, padded, rows_out, sems
):
    incoming = started(
        *(
            (in_ref.at[:, 0, d * BLOCK : (d + 1) * BLOCK], turned.at[d], sems.at[d])
            for d in range(3)
        )
    )
    for d in range(3):
        incoming[d].wait()
        value = turned[d].T
        if d == 2:
            value = pltpu.roll(value, LZ // 2, 1) * swap_ref[...]
        packed[...] = value
        for y in range(BY):
            padded[d, y, :BX, :] = packed[y * BX : (y + 1) * BX, :]
            padded[d, y, BX:, :] = jnp.zeros((40 - BX, LZ), F32)

    def column(col, carry):
        y = (col % CY) * CELL
        x = pl.multiple_of((col // CY) * CELL, CELL)
        planes = products(edges_ref[col])
        modes = modes_ref[col]
        modes = jnp.concatenate([modes, modes[:LZ]], axis=0)
        for d in range(3):
            block = padded[d, pl.ds(y, 12), pl.ds(x, 16), :].reshape(192, LZ)
            along = dot(left_split(block), modes)
            force = jnp.sum(along * planes, axis=0, keepdims=True)
            for zg in range(4):
                rows_out[d, pl.ds(col * 4 + zg, 1), :] = force[:, 128 * zg : 128 * (zg + 1)]
        return carry

    lax.fori_loop(0, CX * CY, column, 0, unroll=8)
    for d in range(3):
        value = rows_out[d]
        pieces = [value[:, s * SLOTS : (s + 1) * SLOTS][:, None, :] for s in range(4)]
        out_ref[d] = jnp.concatenate(pieces, axis=1).reshape(CELLS, SLOTS)


COULOMB = (
    -0.006156452396320011,
    -0.0004198503476764426,
    0.4251962050951751,
    -0.035971568956237085,
    0.5422242920959217,
    -0.3965913855606964,
    0.1962617265017834,
    -0.05766279059061346,
    0.007452967624700701,
)


def pair_term(own, other):
    dx = other[0] - own[0]
    dy = other[1] - own[1]
    dz = other[2] - own[2]
    r2 = dx * dx + dy * dy + dz * dz
    gap = FAR - r2
    fade = jnp.maximum(gap, 0.0)
    t = lax.rsqrt(r2 + LENGTH * LENGTH)
    scale = -2.0 * math.exp(-GEWALD * GEWALD) * 2.0**-FAR / (FAR * LENGTH)
    terms = [scale * c * LENGTH**n for n, c in enumerate(COULOMB)]
    poly = terms[-1] * t + terms[-2]
    for c in terms[-3::-1]:
        poly = poly * t + c
    sigma = own[5] + other[5]
    square = sigma * sigma
    inverse = 1.0 / (r2 + square)
    x = square * inverse
    x3 = x * x * x
    rest = 1.0 - (x3 + x3)
    lj = x3 * (rest * ((fade * inverse) * 3.0 + 1.0) + 1.0)
    w = fade * ((own[4] * other[4]) * lj + (own[3] * other[3]) * (jnp.exp2(gap) * poly))
    return w * dx, w * dy, w * dz


def shifted_z(value, at_z, step):
    if step == 0:
        return value
    if step > 0:
        return jnp.where(
            at_z == CZ - 1, pltpu.roll(value, CZ - 1, 1), pltpu.roll(value, CELLS - 1, 1)
        )
    return jnp.where(at_z == 0, pltpu.roll(value, CELLS - CZ + 1, 1), pltpu.roll(value, 1, 1))


def pair_kernel(*refs, passes, single, sources, begun, unroll):
    blocks, start, outs = refs[:sources], refs[sources : sources + begun], refs[sources + begun : -3]
    others, own, back = refs[-3:]
    low = (lax.broadcasted_iota(jnp.int32, (SLOTS, 256), 1) & CZ) == 0
    at_z = lax.broadcasted_iota(jnp.int32, (SLOTS, CELLS), 1) & (CZ - 1)
    empty = jnp.zeros((SLOTS, 64), F32)
    for c in range(6):
        wide = jnp.concatenate([blocks[1][c], blocks[0][c], blocks[2][c], empty], axis=1)
        own[c] = blocks[0][c]
        layers = {0: wide}
        if sources > 3:
            above = jnp.concatenate([blocks[4][c], blocks[3][c], blocks[5][c], empty], axis=1)
            layers[1] = jnp.where(low, pltpu.roll(wide, 256 - CZ, 1), pltpu.roll(above, CZ, 1))
        for n, offset in enumerate(passes):
            at = COLUMNS * (offset[0] + 1)
            value = layers[offset[1]][:, at : at + CELLS]
            value = shifted_z(value, at_z, offset[2])
            others[c, n * SLOTS : (n + 1) * SLOTS] = (
                value + offset[c] * CELL * LENGTH if c < 3 else value
            )

    def step(n, sums, reverse):
        sums = list(sums)
        for jj in range(unroll):
            j = n * unroll + jj
            other = [others[c, pl.ds(j, 8, stride=0), :] for c in range(6)]
            total = [None] * 3
            for block in range(4):
                mine = [own[c, 8 * block : 8 * block + 8, :] for c in range(6)]
                force = pair_term(mine, other)
                for d in range(3):
                    sums[block * 3 + d] = sums[block * 3 + d] + force[d]
                    total[d] = force[d] if block == 0 else total[d] + force[d]
            if reverse:
                for d in range(3):
                    back[d, pl.ds(pl.multiple_of((j - single * SLOTS) * 8, 8), 8), :] = total[d]
        return tuple(sums)

    per = SLOTS // unroll
    sums = (jnp.zeros((8, CELLS), F32),) * 12
    sums = lax.fori_loop(0, single * per, functools.partial(step, reverse=False), sums)
    sums = lax.fori_loop(
        single * per, len(passes) * per, functools.partial(step, reverse=True), sums
    )
    nothing = jnp.zeros((SLOTS, 128), F32)
    for d in range(3):
        force = jnp.concatenate([sums[block * 3 + d] for block in range(4)], axis=0)
        here = pltpu.roll(jnp.concatenate([force, nothing], axis=1), COLUMNS, 1)
        there = jnp.zeros((SLOTS, 256), F32)
        for n, offset in enumerate(passes):
            if n < single:
                continue
            base = (n - single) * SLOTS * 8
            value = back[d, pl.ds(base, SLOTS, stride=8), :]
            for s in range(1, 8):
                value = value + back[d, pl.ds(base + s, SLOTS, stride=8), :]
            value = shifted_z(value, at_z, -offset[2])
            value = jnp.concatenate([value, nothing], axis=1)
            at = COLUMNS * (offset[0] + 1)
            if offset[1]:
                here = here - pltpu.roll(jnp.where(low, value, 0.0), at + CZ, 1)
                there = there - pltpu.roll(jnp.where(low, 0.0, value), (at - CZ) % 256, 1)
            else:
                here = here - pltpu.roll(value, at, 1)
        if not begun:
            outs[0][d] = here
            outs[1][d] = there
            continue
        here = here + start[0][d]
        there = there + start[1][d]
        for at, total in ((0, here), (3, there)):
            outs[at][d] = total[:, COLUMNS : COLUMNS + CELLS]
            outs[at + 1][d] = total[:, :COLUMNS]
            outs[at + 2][d] = total[:, COLUMNS + CELLS : 2 * COLUMNS + CELLS]


def pair_forces(blocks, passes, single=0, start=(), unroll=8):
    rows = len(passes) * SLOTS
    pairs = rows * SLOTS * CELLS
    widths = (CELLS, COLUMNS, COLUMNS) * 2 if start else (256, 256)
    return pl.pallas_call(
        functools.partial(
            pair_kernel,
            passes=tuple(passes),
            single=single,
            sources=len(blocks),
            begun=len(start),
            unroll=unroll,
        ),
        out_shape=[jax.ShapeDtypeStruct((3, SLOTS, width), F32) for width in widths],
        in_specs=[VMEM] * (len(blocks) + len(start)),
        out_specs=[VMEM] * len(widths),
        scratch_shapes=[
            pltpu.VMEM((6, rows + 8, CELLS), F32),
            pltpu.VMEM((6, SLOTS, CELLS), F32),
            pltpu.VMEM((3, (rows - single * SLOTS) * 8, CELLS), F32),
        ],
        compiler_params=params(8),
        cost_estimate=pl.CostEstimate(flops=70 * pairs, bytes_accessed=1 << 20, transcendentals=0),
    )(*blocks, *start)


def join_kernel(here_ref, down_ref, first_a, first_b, last_a, last_b, out_ref):
    middle = jnp.zeros((SLOTS, CELLS - 2 * COLUMNS), F32)
    for d in range(3):
        sides = [first_a[d] + first_b[d], middle, last_a[d] + last_b[d]]
        out_ref[d] = (here_ref[d] + down_ref[d] + jnp.concatenate(sides, axis=1)).T


def hbm(array):
    return pltpu.with_memory_space_constraint(jnp.asarray(array), pltpu.HBM)


def send(value, step_x, step_y):
    route = [
        (x * DY + y, (x + step_x) % DX * DY + (y + step_y) % DY)
        for x in range(DX)
        for y in range(DY)
    ]
    return lax.ppermute(value, ("gx", "gy"), route)


def body(positions, charges, types, counts, eps_type, sig_type):
    tab = tables()
    slot_last = lambda a: jnp.moveaxis(a, -4, -1).reshape(a.shape[:-4] + (CELLS, SLOTS))
    side = jax.ShapeDtypeStruct((6, SLOTS, COLUMNS), F32)
    atoms, first, last, rows, tz = pl.pallas_call(
        table_kernel,
        out_shape=(
            jax.ShapeDtypeStruct((6, SLOTS, CELLS), F32),
            side,
            side,
            jax.ShapeDtypeStruct((4, GROUPS, 128), F32),
            jax.ShapeDtypeStruct(tab["tz"].shape, BF16),
        ),
        in_specs=[ANY] * 7,
        out_specs=(VMEM,) * 5,
        scratch_shapes=[
            pltpu.VMEM((3, CELLS, SLOTS), F32),
            pltpu.VMEM((CELLS, SLOTS), F32),
            pltpu.VMEM((CELLS, SLOTS), jnp.int32),
            pltpu.VMEM((CX, CY, CZ), jnp.int32),
            pltpu.SMEM(eps_type.shape, F32),
            pltpu.SMEM(sig_type.shape, F32),
            pltpu.SemaphoreType.DMA((7,)),
        ],
        compiler_params=params(8),
    )(
        hbm(slot_last(positions)),
        hbm(slot_last(charges)),
        hbm(slot_last(types)),
        hbm(counts),
        hbm(eps_type),
        hbm(sig_type),
        hbm(tab["tz"]),
    )
    after = send(first, -1, 0)
    before = send(last, 1, 0)
    above = send(atoms, 0, -1)
    above_after = send(first, -1, -1)
    above_before = send(last, 1, -1)

    spread = pl.pallas_call(
        spread_kernel,
        out_shape=jax.ShapeDtypeStruct((LZ, 1, BLOCK), F32),
        in_specs=[VMEM, VMEM, ANY],
        out_specs=ANY,
        scratch_shapes=[
            pltpu.VMEM((BY, 40, LZ), F32),
            pltpu.VMEM((BLOCK, LZ), F32),
            pltpu.VMEM((LZ, BLOCK), F32),
            pltpu.SemaphoreType.DMA((2,)),
        ],
        compiler_params=params(16),
    )(rows, tz, hbm(tab["plane"]))
    spread, after, before, above, above_after, above_before = lax.optimization_barrier(
        (spread, after, before, above, above_after, above_before)
    )
    blocks = (atoms, before, after, above, above_before, above_after)
    lines = lax.all_to_all(hbm(spread), ("gx", "gy"), split_axis=0, concat_axis=0, tiled=True)
    sums = pair_forces(
        blocks,
        [(0, 0, 0), (0, 0, 1), (1, 0, -1), (1, 0, 0), (1, 0, 1), (0, 1, -1), (0, 1, 0)],
        single=1,
    )
    lines, *sums = lax.optimization_barrier((lines, *sums))

    constants = [hbm(tab[name]) for name in ("tx", "ty", "iy", "ix")]
    fields = pl.pallas_call(
        plane_kernel,
        out_shape=jax.ShapeDtypeStruct((DX * DY, 1, 3 * BLOCK), F32),
        in_specs=[ANY] * 5,
        out_specs=ANY,
        scratch_shapes=[
            *(pltpu.VMEM(tab[name].shape, BF16) for name in ("tx", "ty", "iy", "ix")),
            pltpu.VMEM((DX * DY, BLOCK), F32),
            pltpu.VMEM((DX // 2, BY * DY, 128), F32),
            pltpu.VMEM((3, DX * DY, BLOCK), F32),
            pltpu.SemaphoreType.DMA((8,)),
        ],
        compiler_params=params(20),
    )(lines, *constants)
    fields = lax.all_to_all(hbm(fields), ("gx", "gy"), split_axis=0, concat_axis=0, tiled=True)
    here, to_before, to_after, up, up_before, up_after = pair_forces(
        blocks, [(0, 1, 1)] + [(a, 1, c) for a in (-1, 1) for c in (-1, 0, 1)], start=sums
    )
    sides = (
        send(up, 0, 1),
        send(to_after, 1, 0),
        send(up_after, 1, 1),
        send(to_before, -1, 0),
        send(up_before, -1, 1),
    )

    modes, edges = pl.pallas_call(
        weight_kernel,
        out_shape=(
            jax.ShapeDtypeStruct((CX * CY, 2 * LZ, 512), BF16),
            jax.ShapeDtypeStruct((CX * CY, 32, 512), F32),
        ),
        in_specs=[VMEM] * 2,
        out_specs=(VMEM, VMEM),
        compiler_params=params(8),
        cost_estimate=pl.CostEstimate(flops=1 << 28, bytes_accessed=1 << 20, transcendentals=0),
    )(rows, tz)
    fields, here, modes, edges = lax.optimization_barrier((fields, here, modes, edges))
    mesh_force = pl.pallas_call(
        force_kernel,
        out_shape=jax.ShapeDtypeStruct((3, CELLS, SLOTS), F32),
        in_specs=[ANY, VMEM, VMEM, VMEM],
        out_specs=VMEM,
        scratch_shapes=[
            pltpu.VMEM((3, LZ, BLOCK), F32),
            pltpu.VMEM((BLOCK, LZ), F32),
            pltpu.VMEM((3, BY, 40, LZ), F32),
            pltpu.VMEM((3, GROUPS, 128), F32),
            pltpu.SemaphoreType.DMA((3,)),
        ],
        compiler_params=params(20),
    )(fields, modes, edges, tab["swap"])
    mesh_force, here = lax.optimization_barrier((mesh_force, here))
    pair_force = pl.pallas_call(
        join_kernel,
        out_shape=jax.ShapeDtypeStruct((3, CELLS, SLOTS), F32),
        in_specs=[VMEM] * 6,
        out_specs=VMEM,
        compiler_params=params(4),
    )(here, *sides)

    slot_first = lambda a: jnp.moveaxis(a.reshape(3, CX, CY, CZ, SLOTS), -1, 1)
    return slot_first(pair_force), slot_first(mesh_force)


def solution(mesh):
    placed = (
        P(None, None, "gx", "gy", None),
        P(None, "gx", "gy", None),
        P(None, "gx", "gy", None),
        P("gx", "gy", None),
        P(),
        P(),
    )
    return jax.shard_map(
        body,
        mesh=mesh,
        in_specs=placed,
        out_specs=(P(None, None, "gx", "gy", None), P(None, None, "gx", "gy", None)),
        check_vma=False,
    )
```

```python
import functools
import math

import jax
import jax.numpy as jnp
import ml_dtypes
import numpy as np
from jax import lax
from jax.experimental import pallas as pl
from jax.experimental.pallas import tpu as pltpu
from jax.sharding import PartitionSpec as P

CELL = 8
GEWALD = 0.7
CUT = 64.0
F32 = jnp.float32
BF16 = jnp.bfloat16

SLOTS = 32
CX, CY, CZ = 4, 2, 16
CELLS = CX * CY * CZ
COLUMNS = CY * CZ
DX, DY = 8, 16
LX, LY, LZ = 256, 256, 128
BX, BY = CX * CELL + 4, CY * CELL + 4
BLOCK = 768
GROUPS = CELLS // 4
KZ = 48
KX = 64
KY = 384
LENGTH = math.sqrt(GEWALD * GEWALD * math.log2(math.e))
FAR = CUT * LENGTH * LENGTH
SCALES = (LENGTH, LENGTH, LENGTH, 1.0, 1.0 / math.sqrt(8.0 * FAR * LENGTH), 0.5 * LENGTH)
VMEM = pl.BlockSpec(memory_space=pltpu.VMEM)
ANY = pl.BlockSpec(memory_space=pl.ANY)


def params(mib=40):
    return pltpu.CompilerParams(vmem_limit_bytes=mib << 20)


def split(array):
    high = array.astype(ml_dtypes.bfloat16)
    low = (array - high.astype(np.float64)).astype(ml_dtypes.bfloat16)
    return high, low


def left_parts(array):
    high, low = split(array)
    return np.concatenate([high, high, low], axis=-1)


def basis(length):
    half = length // 2
    modes = np.concatenate([np.arange(half + 1), np.arange(1, half)])
    sines = np.arange(length) > half
    return modes, sines


def wave(points, modes, sines, length):
    angle = 2.0 * np.pi * (np.outer(modes, points) % length) / length
    return np.where(sines[:, None], np.sin(angle), np.cos(angle))


def wave_slope(points, modes, sines, length):
    angle = 2.0 * np.pi * (np.outer(modes, points) % length) / length
    k = 2.0 * np.pi * modes / length
    k = np.where(modes == length // 2, 0.0, k)[:, None]
    return np.where(sines[:, None], -k * np.cos(angle), k * np.sin(angle))


def damping(modes, length):
    k = 2.0 * np.pi * modes / length
    return np.exp(-k * k / (4.0 * GEWALD * GEWALD)) / np.sinc(modes / length) ** 8


def norms(modes, length):
    return np.where((modes == 0) | (modes == length // 2), 1.0, 2.0) / length


@functools.cache
def tables():
    mz, sz = basis(LZ)
    tz = np.zeros((4, LZ, KZ))
    for zg in range(4):
        tz[zg, :, :36] = wave(32 * zg - 2 + np.arange(36), mz, sz, LZ)
    mx, sx = basis(LX)
    my, sy = basis(LY)
    tx = np.zeros((DX // 2, 128, LX))
    gain_x = damping(mx, LX) * norms(mx, LX)
    ix = np.zeros((2, LX, DX * BX))
    for gx in range(DX):
        points = gx * CX * CELL - 2 + np.arange(BX)
        at = KX * (gx % 2)
        tx[gx // 2, at : at + BX] = (wave(points, mx, sx, LX) * gain_x[:, None]).T
        ix[0, :, gx * BX : (gx + 1) * BX] = wave(points, mx, sx, LX)
        ix[1, :, gx * BX : (gx + 1) * BX] = wave_slope(points, mx, sx, LX)
    points = (np.arange(DY)[None, :] * CY * CELL - 2 + np.arange(BY)[:, None]).reshape(-1)
    gain_y = damping(my, LY) * norms(my, LY)
    ty = wave(points, my, sy, LY) * gain_y[:, None]
    iy = np.concatenate([wave(points, my, sy, LY).T, wave_slope(points, my, sy, LY).T])
    kz = 2.0 * np.pi * mz / LZ
    plane = np.zeros((8, LZ))
    plane[6:] = kz * kz, 4.0 * np.pi * damping(mz, LZ) * norms(mz, LZ)
    half = LZ // 2
    swap = 2.0 * np.pi * np.arange(half) / LZ
    swap = np.concatenate([-swap, swap]).astype(np.float32)[None, :]
    return dict(
        tz=left_parts(tz),
        tx=np.concatenate(split(tx), axis=1).reshape(-1, LX),
        ty=np.concatenate(split(np.pad(ty, ((0, 0), (0, KY - BY * DY)))), axis=1),
        iy=np.concatenate(split(iy), axis=1),
        ix=np.concatenate(split(np.concatenate([ix[0], ix[1]], axis=1))),
        plane=plane.astype(np.float32),
        swap=swap,
    )


def halves(value):
    high = value.astype(BF16)
    return high, (value - high.astype(F32)).astype(BF16)


def left_split(value):
    high, low = halves(value)
    return jnp.concatenate([high, high, low], axis=1)


def right_split(value, axis=0):
    high, low = halves(value)
    return jnp.concatenate([high, low, high], axis=axis)


def dot(left, right, dims=((1,), (0,))):
    return lax.dot_general(left, right, (dims, ((), ())), preferred_element_type=F32)


def spline(offset):
    span = jnp.abs(offset)
    outer = jnp.maximum(2.0 - span, 0.0)
    inner = jnp.maximum(1.0 - span, 0.0)
    return (outer * outer * outer) * (1.0 / 6.0) - (inner * inner * inner) * (2.0 / 3.0)


def weights(rows_ref, tz_ref, col):
    point = (lax.broadcasted_iota(jnp.int32, (16, 128), 0) - 2).astype(F32)
    point_z = (lax.broadcasted_iota(jnp.int32, (KZ, 128), 0) - 2).astype(F32)
    shift = ((lax.broadcasted_iota(jnp.int32, (1, 128), 1) // SLOTS) * CELL).astype(F32)
    modes, edges = [], []
    for zg in range(4):
        row = [rows_ref[c, pl.ds(col * 4 + zg, 1), :] for c in range(4)]
        along_x = spline(row[0] - point)
        along_y = spline(row[1] - point) * row[3]
        along_z = spline(row[2] + shift - point_z)
        modes.append(dot(tz_ref[zg], right_split(along_z)))
        edges.append(jnp.concatenate([along_x, along_y], axis=0))
    return jnp.concatenate(modes, axis=1), jnp.concatenate(edges, axis=1)


def products(edges):
    return (edges[16:28][:, None, :] * edges[:16][None, :, :]).reshape(192, edges.shape[1])


def started(*copies):
    copies = [pltpu.make_async_copy(*copy) for copy in copies]
    for copy in copies:
        copy.start()
    return copies


def table_kernel(*refs):
    sources, (atoms_ref, first_ref, last_ref, rows_ref, tz_ref) = refs[:7], refs[7:12]
    pos_ref, charge_ref, type_ref, count_ref, eps_ref, sig_ref, sems = refs[12:]
    targets = refs[12:18] + (tz_ref,)
    incoming = started(*((s, t, sems.at[n]) for n, (s, t) in enumerate(zip(sources, targets))))
    for copy in incoming[:-1]:
        copy.wait()
    slots = lax.broadcasted_iota(jnp.int32, (SLOTS, CELLS), 0)
    counts = [count_ref[cx, cy : cy + 1, :] for cx in range(CX) for cy in range(CY)]
    occupied = slots < jnp.concatenate(counts, axis=1)
    kinds = type_ref[...].T
    eps = jnp.zeros((SLOTS, CELLS), F32)
    sig = jnp.zeros((SLOTS, CELLS), F32)
    for kind in range(eps_ref.shape[0]):
        match = kinds == kind
        eps = jnp.where(match, eps_ref[kind], eps)
        sig = jnp.where(match, sig_ref[kind], sig)
    charge = jnp.where(occupied, charge_ref[...].T, 0.0)
    root = jnp.where(occupied, jnp.sqrt(eps), 0.0)
    for c, value in enumerate([pos_ref[d].T for d in range(3)] + [charge, root, sig]):
        value = value * SCALES[c]
        atoms_ref[c] = value
        first_ref[c] = value[:, :COLUMNS]
        last_ref[c] = value[:, CELLS - COLUMNS :]
    charge = charge.T
    for c in range(4):
        value = pos_ref[c] if c < 3 else charge
        value = value.reshape(GROUPS, 4, SLOTS)
        rows_ref[c] = jnp.concatenate([value[:, s, :] for s in range(4)], axis=1)
    incoming[-1].wait()


def spread_kernel(rows_ref, tz_ref, plane_ref, spread_out, total, packed, turned, sems):
    (plane,) = started((plane_ref, packed.at[BLOCK - 8 :, :], sems.at[0]))
    total[...] = jnp.zeros_like(total)

    def column(col, carry):
        modes, edges = weights(rows_ref, tz_ref, col)
        part = dot(left_split(products(edges)), right_split(modes, 1), ((1,), (1,)))
        y = (col % CY) * CELL
        x = pl.multiple_of((col // CY) * CELL, CELL)
        total[pl.ds(y, 12), pl.ds(x, 16), :] += part.reshape(12, 16, LZ)
        return carry

    lax.fori_loop(0, CX * CY, column, 0, unroll=8)
    for y in range(BY):
        packed[y * BX : (y + 1) * BX, :] = total[y, :BX, :]
    packed[BX * BY : BLOCK - 8, :] = jnp.zeros((BLOCK - 8 - BX * BY, LZ), F32)
    plane.wait()
    turned[...] = packed[...].T
    for copy in started((turned, spread_out.at[:, 0, :], sems.at[1])):
        copy.wait()


def weight_kernel(rows_ref, tz_ref, modes_ref, edges_ref):
    def column(col, carry):
        modes, edges_ref[col] = weights(rows_ref, tz_ref, col)
        modes_ref[col] = jnp.concatenate(halves(modes), axis=0)
        return carry

    lax.fori_loop(0, CX * CY, column, 0, unroll=8)


def plane_kernel(in_ref, *refs):
    sources, out_ref, held = refs[:4], refs[4], refs[5:9]
    lines, stacked, turned, sems = refs[9:]
    tx, ty, iy, ix = held
    (arrival,) = started((in_ref.at[:, 0, :], lines, sems.at[3]))
    copies = [(s, t, sems.at[4 + n]) for n, (s, t) in enumerate(zip(sources, held))]
    constants = started(*copies[:2])
    arrival.wait()
    constants += started(*copies[2:])
    kz2, gain = lines[:1, BLOCK - 2 : BLOCK - 1], lines[:1, BLOCK - 1 :]
    for y in range(BY):
        value = lines[:, y * BX : y * BX + KX]
        for gx in range(DX):
            at = KX * (gx % 2)
            stacked[gx // 2, y * DY : (y + 1) * DY, at : at + KX] = value[gx * DY : (gx + 1) * DY]
    pairs = jnp.concatenate([left_split(stacked[n]) for n in range(DX // 2)], axis=1)
    constants[0].wait()
    table = []
    for n in range(DX // 2):
        table += [tx[256 * n : 256 * (n + 1)], tx[256 * n : 256 * n + 128]]
    high, low = halves(dot(pairs, jnp.concatenate(table, axis=0)))
    empty = jnp.zeros((KY - BY * DY, LX), BF16)
    constants[1].wait()
    modes = dot(
        jnp.concatenate([ty[:, :KY], ty[:, :KY], ty[:, KY:]], axis=1),
        jnp.concatenate([high, empty, low, empty, high, empty], axis=0),
    )
    k2 = kz2
    for axis, length in ((0, LY), (1, LX)):
        mode = lax.broadcasted_iota(jnp.int32, (LY, LX), axis)
        mode = jnp.where(mode > length // 2, mode - length // 2, mode).astype(F32)
        k = mode * (2.0 * math.pi / length)
        k2 = k2 + k * k
    positive = k2 > 0.0
    modes = jnp.where(positive, modes * (gain / jnp.where(positive, k2, 1.0)), 0.0)
    constants[2].wait()
    table = [iy[:, :LY], iy[:, :LY], iy[:, LY:]]
    both = dot(jnp.concatenate(table, axis=1), right_split(modes))
    constants[3].wait()
    rows = BY * DY
    width = DX * BX
    table = jnp.concatenate([ix[...], ix[:LX]], axis=0)
    plain = dot(left_split(both[:rows]), table)
    slope = dot(left_split(both[rows:]), table[:, :width])
    fields = (plain[:, width:], slope, plain[:, :width])
    outgoing = []
    for d in range(3):
        turned[d, :, BX * BY :] = jnp.zeros((DX * DY, BLOCK - BX * BY), F32)
        for gx in range(DX):
            piece = fields[d][:, gx * BX : (gx + 1) * BX]
            for y in range(BY):
                lane = y * BX
                turned[d, gx * DY : (gx + 1) * DY, lane : lane + BX] = piece[y * DY : (y + 1) * DY]
        outgoing += started(
            (turned.at[d], out_ref.at[:, 0, d * BLOCK : (d + 1) * BLOCK], sems.at[d])
        )
    for copy in outgoing:
        copy.wait()


def force_kernel(
    in_ref, modes_ref, edges_ref, swap_ref, out_ref, turned, packed, padded, rows_out, sems
):
    incoming = started(
        *(
            (in_ref.at[:, 0, d * BLOCK : (d + 1) * BLOCK], turned.at[d], sems.at[d])
            for d in range(3)
        )
    )
    for d in range(3):
        incoming[d].wait()
        value = turned[d].T
        if d == 2:
            value = pltpu.roll(value, LZ // 2, 1) * swap_ref[...]
        packed[...] = value
        for y in range(BY):
            padded[d, y, :BX, :] = packed[y * BX : (y + 1) * BX, :]
            padded[d, y, BX:, :] = jnp.zeros((40 - BX, LZ), F32)

    def column(col, carry):
        y = (col % CY) * CELL
        x = pl.multiple_of((col // CY) * CELL, CELL)
        planes = products(edges_ref[col])
        modes = modes_ref[col]
        modes = jnp.concatenate([modes, modes[:LZ]], axis=0)
        for d in range(3):
            block = padded[d, pl.ds(y, 12), pl.ds(x, 16), :].reshape(192, LZ)
            along = dot(left_split(block), modes)
            force = jnp.sum(along * planes, axis=0, keepdims=True)
            for zg in range(4):
                rows_out[d, pl.ds(col * 4 + zg, 1), :] = force[:, 128 * zg : 128 * (zg + 1)]
        return carry

    lax.fori_loop(0, CX * CY, column, 0, unroll=8)
    for d in range(3):
        value = rows_out[d]
        pieces = [value[:, s * SLOTS : (s + 1) * SLOTS][:, None, :] for s in range(4)]
        out_ref[d] = jnp.concatenate(pieces, axis=1).reshape(CELLS, SLOTS)


COULOMB = (
    -0.006156452396320011,
    -0.0004198503476764426,
    0.4251962050951751,
    -0.035971568956237085,
    0.5422242920959217,
    -0.3965913855606964,
    0.1962617265017834,
    -0.05766279059061346,
    0.007452967624700701,
)


def pair_term(own, other):
    dx = other[0] - own[0]
    dy = other[1] - own[1]
    dz = other[2] - own[2]
    r2 = dx * dx + dy * dy + dz * dz
    gap = FAR - r2
    fade = jnp.maximum(gap, 0.0)
    t = lax.rsqrt(r2 + LENGTH * LENGTH)
    scale = -2.0 * math.exp(-GEWALD * GEWALD) * 2.0**-FAR / (FAR * LENGTH)
    terms = [scale * c * LENGTH**n for n, c in enumerate(COULOMB)]
    poly = terms[-1] * t + terms[-2]
    for c in terms[-3::-1]:
        poly = poly * t + c
    sigma = own[5] + other[5]
    square = sigma * sigma
    inverse = 1.0 / (r2 + square)
    x = square * inverse
    x3 = x * x * x
    rest = 1.0 - (x3 + x3)
    lj = x3 * (rest * ((fade * inverse) * 3.0 + 1.0) + 1.0)
    w = fade * ((own[4] * other[4]) * lj + (own[3] * other[3]) * (jnp.exp2(gap) * poly))
    return w * dx, w * dy, w * dz


def shifted_z(value, at_z, step):
    if step == 0:
        return value
    if step > 0:
        return jnp.where(
            at_z == CZ - 1, pltpu.roll(value, CZ - 1, 1), pltpu.roll(value, CELLS - 1, 1)
        )
    return jnp.where(at_z == 0, pltpu.roll(value, CELLS - CZ + 1, 1), pltpu.roll(value, 1, 1))


def pair_kernel(*refs, passes, single, sources, begun, unroll):
    blocks, start, outs = refs[:sources], refs[sources : sources + begun], refs[sources + begun : -3]
    others, own, back = refs[-3:]
    low = (lax.broadcasted_iota(jnp.int32, (SLOTS, 256), 1) & CZ) == 0
    at_z = lax.broadcasted_iota(jnp.int32, (SLOTS, CELLS), 1) & (CZ - 1)
    empty = jnp.zeros((SLOTS, 64), F32)
    for c in range(6):
        wide = jnp.concatenate([blocks[1][c], blocks[0][c], blocks[2][c], empty], axis=1)
        own[c] = blocks[0][c]
        layers = {0: wide}
        if sources > 3:
            above = jnp.concatenate([blocks[4][c], blocks[3][c], blocks[5][c], empty], axis=1)
            layers[1] = jnp.where(low, pltpu.roll(wide, 256 - CZ, 1), pltpu.roll(above, CZ, 1))
        for n, offset in enumerate(passes):
            at = COLUMNS * (offset[0] + 1)
            value = layers[offset[1]][:, at : at + CELLS]
            value = shifted_z(value, at_z, offset[2])
            others[c, n * SLOTS : (n + 1) * SLOTS] = (
                value + offset[c] * CELL * LENGTH if c < 3 else value
            )

    def step(n, sums, reverse):
        sums = list(sums)
        for jj in range(unroll):
            j = n * unroll + jj
            other = [others[c, pl.ds(j, 8, stride=0), :] for c in range(6)]
            total = [None] * 3
            for block in range(4):
                mine = [own[c, 8 * block : 8 * block + 8, :] for c in range(6)]
                force = pair_term(mine, other)
                for d in range(3):
                    sums[block * 3 + d] = sums[block * 3 + d] + force[d]
                    total[d] = force[d] if block == 0 else total[d] + force[d]
            if reverse:
                for d in range(3):
                    back[d, pl.ds(pl.multiple_of((j - single * SLOTS) * 8, 8), 8), :] = total[d]
        return tuple(sums)

    per = SLOTS // unroll
    sums = (jnp.zeros((8, CELLS), F32),) * 12
    sums = lax.fori_loop(0, single * per, functools.partial(step, reverse=False), sums)
    sums = lax.fori_loop(
        single * per, len(passes) * per, functools.partial(step, reverse=True), sums
    )
    nothing = jnp.zeros((SLOTS, 128), F32)
    for d in range(3):
        force = jnp.concatenate([sums[block * 3 + d] for block in range(4)], axis=0)
        here = pltpu.roll(jnp.concatenate([force, nothing], axis=1), COLUMNS, 1)
        there = jnp.zeros((SLOTS, 256), F32)
        for n, offset in enumerate(passes):
            if n < single:
                continue
            base = (n - single) * SLOTS * 8
            value = back[d, pl.ds(base, SLOTS, stride=8), :]
            for s in range(1, 8):
                value = value + back[d, pl.ds(base + s, SLOTS, stride=8), :]
            value = shifted_z(value, at_z, -offset[2])
            value = jnp.concatenate([value, nothing], axis=1)
            at = COLUMNS * (offset[0] + 1)
            if offset[1]:
                here = here - pltpu.roll(jnp.where(low, value, 0.0), at + CZ, 1)
                there = there - pltpu.roll(jnp.where(low, 0.0, value), (at - CZ) % 256, 1)
            else:
                here = here - pltpu.roll(value, at, 1)
        if not begun:
            outs[0][d] = here
            outs[1][d] = there
            continue
        here = here + start[0][d]
        there = there + start[1][d]
        for at, total in ((0, here), (3, there)):
            outs[at][d] = total[:, COLUMNS : COLUMNS + CELLS]
            outs[at + 1][d] = total[:, :COLUMNS]
            outs[at + 2][d] = total[:, COLUMNS + CELLS : 2 * COLUMNS + CELLS]


def pair_forces(blocks, passes, single=0, start=(), unroll=16):
    rows = len(passes) * SLOTS
    pairs = rows * SLOTS * CELLS
    widths = (CELLS, COLUMNS, COLUMNS) * 2 if start else (256, 256)
    return pl.pallas_call(
        functools.partial(
            pair_kernel,
            passes=tuple(passes),
            single=single,
            sources=len(blocks),
            begun=len(start),
            unroll=unroll,
        ),
        out_shape=[jax.ShapeDtypeStruct((3, SLOTS, width), F32) for width in widths],
        in_specs=[VMEM] * (len(blocks) + len(start)),
        out_specs=[VMEM] * len(widths),
        scratch_shapes=[
            pltpu.VMEM((6, rows + 8, CELLS), F32),
            pltpu.VMEM((6, SLOTS, CELLS), F32),
            pltpu.VMEM((3, (rows - single * SLOTS) * 8, CELLS), F32),
        ],
        compiler_params=params(8),
        cost_estimate=pl.CostEstimate(flops=70 * pairs, bytes_accessed=1 << 20, transcendentals=0),
    )(*blocks, *start)


def join_kernel(here_ref, down_ref, first_a, first_b, last_a, last_b, out_ref):
    middle = jnp.zeros((SLOTS, CELLS - 2 * COLUMNS), F32)
    for d in range(3):
        sides = [first_a[d] + first_b[d], middle, last_a[d] + last_b[d]]
        out_ref[d] = (here_ref[d] + down_ref[d] + jnp.concatenate(sides, axis=1)).T


def hbm(array):
    return pltpu.with_memory_space_constraint(jnp.asarray(array), pltpu.HBM)


def send(value, step_x, step_y):
    route = [
        (x * DY + y, (x + step_x) % DX * DY + (y + step_y) % DY)
        for x in range(DX)
        for y in range(DY)
    ]
    return lax.ppermute(value, ("gx", "gy"), route)


def body(positions, charges, types, counts, eps_type, sig_type):
    tab = tables()
    slot_last = lambda a: jnp.moveaxis(a, -4, -1).reshape(a.shape[:-4] + (CELLS, SLOTS))
    side = jax.ShapeDtypeStruct((6, SLOTS, COLUMNS), F32)
    atoms, first, last, rows, tz = pl.pallas_call(
        table_kernel,
        out_shape=(
            jax.ShapeDtypeStruct((6, SLOTS, CELLS), F32),
            side,
            side,
            jax.ShapeDtypeStruct((4, GROUPS, 128), F32),
            jax.ShapeDtypeStruct(tab["tz"].shape, BF16),
        ),
        in_specs=[ANY] * 7,
        out_specs=(VMEM,) * 5,
        scratch_shapes=[
            pltpu.VMEM((3, CELLS, SLOTS), F32),
            pltpu.VMEM((CELLS, SLOTS), F32),
            pltpu.VMEM((CELLS, SLOTS), jnp.int32),
            pltpu.VMEM((CX, CY, CZ), jnp.int32),
            pltpu.SMEM(eps_type.shape, F32),
            pltpu.SMEM(sig_type.shape, F32),
            pltpu.SemaphoreType.DMA((7,)),
        ],
        compiler_params=params(8),
    )(
        hbm(slot_last(positions)),
        hbm(slot_last(charges)),
        hbm(slot_last(types)),
        hbm(counts),
        hbm(eps_type),
        hbm(sig_type),
        hbm(tab["tz"]),
    )
    after = send(first, -1, 0)
    before = send(last, 1, 0)
    above = send(atoms, 0, -1)
    above_after = send(first, -1, -1)
    above_before = send(last, 1, -1)

    spread = pl.pallas_call(
        spread_kernel,
        out_shape=jax.ShapeDtypeStruct((LZ, 1, BLOCK), F32),
        in_specs=[VMEM, VMEM, ANY],
        out_specs=ANY,
        scratch_shapes=[
            pltpu.VMEM((BY, 40, LZ), F32),
            pltpu.VMEM((BLOCK, LZ), F32),
            pltpu.VMEM((LZ, BLOCK), F32),
            pltpu.SemaphoreType.DMA((2,)),
        ],
        compiler_params=params(16),
    )(rows, tz, hbm(tab["plane"]))
    spread, after, before, above, above_after, above_before = lax.optimization_barrier(
        (spread, after, before, above, above_after, above_before)
    )
    blocks = (atoms, before, after, above, above_before, above_after)
    lines = lax.all_to_all(hbm(spread), ("gx", "gy"), split_axis=0, concat_axis=0, tiled=True)
    sums = pair_forces(
        blocks,
        [(0, 0, 0), (0, 0, 1), (1, 0, -1), (1, 0, 0), (1, 0, 1), (0, 1, -1), (0, 1, 0)],
        single=1,
    )
    lines, *sums = lax.optimization_barrier((lines, *sums))

    constants = [hbm(tab[name]) for name in ("tx", "ty", "iy", "ix")]
    fields = pl.pallas_call(
        plane_kernel,
        out_shape=jax.ShapeDtypeStruct((DX * DY, 1, 3 * BLOCK), F32),
        in_specs=[ANY] * 5,
        out_specs=ANY,
        scratch_shapes=[
            *(pltpu.VMEM(tab[name].shape, BF16) for name in ("tx", "ty", "iy", "ix")),
            pltpu.VMEM((DX * DY, BLOCK), F32),
            pltpu.VMEM((DX // 2, BY * DY, 128), F32),
            pltpu.VMEM((3, DX * DY, BLOCK), F32),
            pltpu.SemaphoreType.DMA((8,)),
        ],
        compiler_params=params(20),
    )(lines, *constants)
    fields = lax.all_to_all(hbm(fields), ("gx", "gy"), split_axis=0, concat_axis=0, tiled=True)
    here, to_before, to_after, up, up_before, up_after = pair_forces(
        blocks, [(0, 1, 1)] + [(a, 1, c) for a in (-1, 1) for c in (-1, 0, 1)], start=sums
    )
    sides = (
        send(up, 0, 1),
        send(to_after, 1, 0),
        send(up_after, 1, 1),
        send(to_before, -1, 0),
        send(up_before, -1, 1),
    )

    modes, edges = pl.pallas_call(
        weight_kernel,
        out_shape=(
            jax.ShapeDtypeStruct((CX * CY, 2 * LZ, 512), BF16),
            jax.ShapeDtypeStruct((CX * CY, 32, 512), F32),
        ),
        in_specs=[VMEM] * 2,
        out_specs=(VMEM, VMEM),
        compiler_params=params(8),
        cost_estimate=pl.CostEstimate(flops=1 << 28, bytes_accessed=1 << 20, transcendentals=0),
    )(rows, tz)
    fields, here, modes, edges = lax.optimization_barrier((fields, here, modes, edges))
    mesh_force = pl.pallas_call(
        force_kernel,
        out_shape=jax.ShapeDtypeStruct((3, CELLS, SLOTS), F32),
        in_specs=[ANY, VMEM, VMEM, VMEM],
        out_specs=VMEM,
        scratch_shapes=[
            pltpu.VMEM((3, LZ, BLOCK), F32),
            pltpu.VMEM((BLOCK, LZ), F32),
            pltpu.VMEM((3, BY, 40, LZ), F32),
            pltpu.VMEM((3, GROUPS, 128), F32),
            pltpu.SemaphoreType.DMA((3,)),
        ],
        compiler_params=params(20),
    )(fields, modes, edges, tab["swap"])
    mesh_force, here = lax.optimization_barrier((mesh_force, here))
    pair_force = pl.pallas_call(
        join_kernel,
        out_shape=jax.ShapeDtypeStruct((3, CELLS, SLOTS), F32),
        in_specs=[VMEM] * 6,
        out_specs=VMEM,
        compiler_params=params(4),
    )(here, *sides)

    slot_first = lambda a: jnp.moveaxis(a.reshape(3, CX, CY, CZ, SLOTS), -1, 1)
    return slot_first(pair_force), slot_first(mesh_force)


def solution(mesh):
    placed = (
        P(None, None, "gx", "gy", None),
        P(None, "gx", "gy", None),
        P(None, "gx", "gy", None),
        P("gx", "gy", None),
        P(),
        P(),
    )
    return jax.shard_map(
        body,
        mesh=mesh,
        in_specs=placed,
        out_specs=(P(None, None, "gx", "gy", None), P(None, None, "gx", "gy", None)),
        check_vma=False,
    )
```

```python
import functools
import math

import jax
import jax.numpy as jnp
import ml_dtypes
import numpy as np
from jax import lax
from jax.experimental import pallas as pl
from jax.experimental.pallas import tpu as pltpu
from jax.sharding import PartitionSpec as P

CELL = 8
GEWALD = 0.7
CUT = 64.0
F32 = jnp.float32
BF16 = jnp.bfloat16

SLOTS = 32
CX, CY, CZ = 4, 2, 16
CELLS = CX * CY * CZ
COLUMNS = CY * CZ
DX, DY = 8, 16
LX, LY, LZ = 256, 256, 128
BX, BY = CX * CELL + 4, CY * CELL + 4
BLOCK = 768
GROUPS = CELLS // 4
KZ = 48
KX = 64
KY = 384
LENGTH = math.sqrt(GEWALD * GEWALD * math.log2(math.e))
FAR = CUT * LENGTH * LENGTH
SCALES = (LENGTH, LENGTH, LENGTH, 1.0, 1.0 / math.sqrt(8.0 * FAR * LENGTH), 0.5 * LENGTH)
VMEM = pl.BlockSpec(memory_space=pltpu.VMEM)
ANY = pl.BlockSpec(memory_space=pl.ANY)


def params(mib=40):
    return pltpu.CompilerParams(vmem_limit_bytes=mib << 20)


def split(array):
    high = array.astype(ml_dtypes.bfloat16)
    low = (array - high.astype(np.float64)).astype(ml_dtypes.bfloat16)
    return high, low


def left_parts(array):
    high, low = split(array)
    return np.concatenate([high, high, low], axis=-1)


def basis(length):
    half = length // 2
    modes = np.concatenate([np.arange(half + 1), np.arange(1, half)])
    sines = np.arange(length) > half
    return modes, sines


def wave(points, modes, sines, length):
    angle = 2.0 * np.pi * (np.outer(modes, points) % length) / length
    return np.where(sines[:, None], np.sin(angle), np.cos(angle))


def wave_slope(points, modes, sines, length):
    angle = 2.0 * np.pi * (np.outer(modes, points) % length) / length
    k = 2.0 * np.pi * modes / length
    k = np.where(modes == length // 2, 0.0, k)[:, None]
    return np.where(sines[:, None], -k * np.cos(angle), k * np.sin(angle))


def damping(modes, length):
    k = 2.0 * np.pi * modes / length
    return np.exp(-k * k / (4.0 * GEWALD * GEWALD)) / np.sinc(modes / length) ** 8


def norms(modes, length):
    return np.where((modes == 0) | (modes == length // 2), 1.0, 2.0) / length


@functools.cache
def tables():
    mz, sz = basis(LZ)
    tz = np.zeros((4, LZ, KZ))
    for zg in range(4):
        tz[zg, :, :36] = wave(32 * zg - 2 + np.arange(36), mz, sz, LZ)
    mx, sx = basis(LX)
    my, sy = basis(LY)
    tx = np.zeros((DX // 2, 128, LX))
    gain_x = damping(mx, LX) * norms(mx, LX)
    ix = np.zeros((2, LX, DX * BX))
    for gx in range(DX):
        points = gx * CX * CELL - 2 + np.arange(BX)
        at = KX * (gx % 2)
        tx[gx // 2, at : at + BX] = (wave(points, mx, sx, LX) * gain_x[:, None]).T
        ix[0, :, gx * BX : (gx + 1) * BX] = wave(points, mx, sx, LX)
        ix[1, :, gx * BX : (gx + 1) * BX] = wave_slope(points, mx, sx, LX)
    points = (np.arange(DY)[None, :] * CY * CELL - 2 + np.arange(BY)[:, None]).reshape(-1)
    gain_y = damping(my, LY) * norms(my, LY)
    ty = wave(points, my, sy, LY) * gain_y[:, None]
    iy = np.concatenate([wave(points, my, sy, LY).T, wave_slope(points, my, sy, LY).T])
    kz = 2.0 * np.pi * mz / LZ
    plane = np.zeros((8, LZ))
    plane[6:] = kz * kz, 4.0 * np.pi * damping(mz, LZ) * norms(mz, LZ)
    half = LZ // 2
    swap = 2.0 * np.pi * np.arange(half) / LZ
    swap = np.concatenate([-swap, swap]).astype(np.float32)[None, :]
    return dict(
        tz=left_parts(tz),
        tx=np.concatenate(split(tx), axis=1).reshape(-1, LX),
        ty=np.concatenate(split(np.pad(ty, ((0, 0), (0, KY - BY * DY)))), axis=1),
        iy=np.concatenate(split(iy), axis=1),
        ix=np.concatenate(split(np.concatenate([ix[0], ix[1]], axis=1))),
        plane=plane.astype(np.float32),
        swap=swap,
    )


def halves(value):
    high = value.astype(BF16)
    return high, (value - high.astype(F32)).astype(BF16)


def left_split(value):
    high, low = halves(value)
    return jnp.concatenate([high, high, low], axis=1)


def right_split(value, axis=0):
    high, low = halves(value)
    return jnp.concatenate([high, low, high], axis=axis)


def dot(left, right, dims=((1,), (0,))):
    return lax.dot_general(left, right, (dims, ((), ())), preferred_element_type=F32)


def spline(offset):
    span = jnp.abs(offset)
    outer = jnp.maximum(2.0 - span, 0.0)
    inner = jnp.maximum(1.0 - span, 0.0)
    return (outer * outer * outer) * (1.0 / 6.0) - (inner * inner * inner) * (2.0 / 3.0)


def weights(rows_ref, tz_ref, col):
    point = (lax.broadcasted_iota(jnp.int32, (16, 128), 0) - 2).astype(F32)
    point_z = (lax.broadcasted_iota(jnp.int32, (KZ, 128), 0) - 2).astype(F32)
    shift = ((lax.broadcasted_iota(jnp.int32, (1, 128), 1) // SLOTS) * CELL).astype(F32)
    modes, edges = [], []
    for zg in range(4):
        row = [rows_ref[c, pl.ds(col * 4 + zg, 1), :] for c in range(4)]
        along_x = spline(row[0] - point)
        along_y = spline(row[1] - point) * row[3]
        along_z = spline(row[2] + shift - point_z)
        modes.append(dot(tz_ref[zg], right_split(along_z)))
        edges.append(jnp.concatenate([along_x, along_y], axis=0))
    return jnp.concatenate(modes, axis=1), jnp.concatenate(edges, axis=1)


def products(edges):
    return (edges[16:28][:, None, :] * edges[:16][None, :, :]).reshape(192, edges.shape[1])


def started(*copies):
    copies = [pltpu.make_async_copy(*copy) for copy in copies]
    for copy in copies:
        copy.start()
    return copies


def table_kernel(*refs):
    sources, (atoms_ref, first_ref, last_ref, rows_ref, tz_ref) = refs[:7], refs[7:12]
    pos_ref, charge_ref, type_ref, count_ref, eps_ref, sig_ref, sems = refs[12:]
    targets = refs[12:18] + (tz_ref,)
    incoming = started(*((s, t, sems.at[n]) for n, (s, t) in enumerate(zip(sources, targets))))
    for copy in incoming[:-1]:
        copy.wait()
    slots = lax.broadcasted_iota(jnp.int32, (SLOTS, CELLS), 0)
    counts = [count_ref[cx, cy : cy + 1, :] for cx in range(CX) for cy in range(CY)]
    occupied = slots < jnp.concatenate(counts, axis=1)
    kinds = type_ref[...].T
    eps = jnp.zeros((SLOTS, CELLS), F32)
    sig = jnp.zeros((SLOTS, CELLS), F32)
    for kind in range(eps_ref.shape[0]):
        match = kinds == kind
        eps = jnp.where(match, eps_ref[kind], eps)
        sig = jnp.where(match, sig_ref[kind], sig)
    charge = jnp.where(occupied, charge_ref[...].T, 0.0)
    root = jnp.where(occupied, jnp.sqrt(eps), 0.0)
    for c, value in enumerate([pos_ref[d].T for d in range(3)] + [charge, root, sig]):
        value = value * SCALES[c]
        atoms_ref[c] = value
        first_ref[c] = value[:, :COLUMNS]
        last_ref[c] = value[:, CELLS - COLUMNS :]
    charge = charge.T
    for c in range(4):
        value = pos_ref[c] if c < 3 else charge
        value = value.reshape(GROUPS, 4, SLOTS)
        rows_ref[c] = jnp.concatenate([value[:, s, :] for s in range(4)], axis=1)
    incoming[-1].wait()


def spread_kernel(rows_ref, tz_ref, plane_ref, spread_out, total, packed, turned, sems):
    (plane,) = started((plane_ref, packed.at[BLOCK - 8 :, :], sems.at[0]))
    total[...] = jnp.zeros_like(total)

    def column(col, carry):
        modes, edges = weights(rows_ref, tz_ref, col)
        part = dot(left_split(products(edges)), right_split(modes, 1), ((1,), (1,)))
        y = (col % CY) * CELL
        x = pl.multiple_of((col // CY) * CELL, CELL)
        total[pl.ds(y, 12), pl.ds(x, 16), :] += part.reshape(12, 16, LZ)
        return carry

    lax.fori_loop(0, CX * CY, column, 0, unroll=8)
    for y in range(BY):
        packed[y * BX : (y + 1) * BX, :] = total[y, :BX, :]
    packed[BX * BY : BLOCK - 8, :] = jnp.zeros((BLOCK - 8 - BX * BY, LZ), F32)
    plane.wait()
    turned[...] = packed[...].T
    for copy in started((turned, spread_out.at[:, 0, :], sems.at[1])):
        copy.wait()


def weight_kernel(rows_ref, tz_ref, modes_ref, edges_ref):
    def column(col, carry):
        modes, edges_ref[col] = weights(rows_ref, tz_ref, col)
        modes_ref[col] = jnp.concatenate(halves(modes), axis=0)
        return carry

    lax.fori_loop(0, CX * CY, column, 0, unroll=8)


def plane_kernel(in_ref, *refs):
    sources, out_ref, held = refs[:4], refs[4], refs[5:9]
    lines, stacked, turned, sems = refs[9:]
    tx, ty, iy, ix = held
    (arrival,) = started((in_ref.at[:, 0, :], lines, sems.at[3]))
    copies = [(s, t, sems.at[4 + n]) for n, (s, t) in enumerate(zip(sources, held))]
    constants = started(*copies[:2])
    arrival.wait()
    constants += started(*copies[2:])
    kz2, gain = lines[:1, BLOCK - 2 : BLOCK - 1], lines[:1, BLOCK - 1 :]
    for y in range(BY):
        value = lines[:, y * BX : y * BX + KX]
        for gx in range(DX):
            at = KX * (gx % 2)
            stacked[gx // 2, y * DY : (y + 1) * DY, at : at + KX] = value[gx * DY : (gx + 1) * DY]
    pairs = jnp.concatenate([left_split(stacked[n]) for n in range(DX // 2)], axis=1)
    constants[0].wait()
    table = []
    for n in range(DX // 2):
        table += [tx[256 * n : 256 * (n + 1)], tx[256 * n : 256 * n + 128]]
    high, low = halves(dot(pairs, jnp.concatenate(table, axis=0)))
    empty = jnp.zeros((KY - BY * DY, LX), BF16)
    constants[1].wait()
    modes = dot(
        jnp.concatenate([ty[:, :KY], ty[:, :KY], ty[:, KY:]], axis=1),
        jnp.concatenate([high, empty, low, empty, high, empty], axis=0),
    )
    k2 = kz2
    for axis, length in ((0, LY), (1, LX)):
        mode = lax.broadcasted_iota(jnp.int32, (LY, LX), axis)
        mode = jnp.where(mode > length // 2, mode - length // 2, mode).astype(F32)
        k = mode * (2.0 * math.pi / length)
        k2 = k2 + k * k
    positive = k2 > 0.0
    modes = jnp.where(positive, modes * (gain / jnp.where(positive, k2, 1.0)), 0.0)
    constants[2].wait()
    table = [iy[:, :LY], iy[:, :LY], iy[:, LY:]]
    both = dot(jnp.concatenate(table, axis=1), right_split(modes))
    constants[3].wait()
    rows = BY * DY
    width = DX * BX
    table = jnp.concatenate([ix[...], ix[:LX]], axis=0)
    plain = dot(left_split(both[:rows]), table)
    slope = dot(left_split(both[rows:]), table[:, :width])
    fields = (plain[:, width:], slope, plain[:, :width])
    outgoing = []
    for d in range(3):
        turned[d, :, BX * BY :] = jnp.zeros((DX * DY, BLOCK - BX * BY), F32)
        for gx in range(DX):
            piece = fields[d][:, gx * BX : (gx + 1) * BX]
            for y in range(BY):
                lane = y * BX
                turned[d, gx * DY : (gx + 1) * DY, lane : lane + BX] = piece[y * DY : (y + 1) * DY]
        outgoing += started(
            (turned.at[d], out_ref.at[:, 0, d * BLOCK : (d + 1) * BLOCK], sems.at[d])
        )
    for copy in outgoing:
        copy.wait()


def force_kernel(
    in_ref, modes_ref, edges_ref, swap_ref, out_ref, turned, packed, padded, rows_out, sems
):
    incoming = started(
        *(
            (in_ref.at[:, 0, d * BLOCK : (d + 1) * BLOCK], turned.at[d], sems.at[d])
            for d in range(3)
        )
    )
    for d in range(3):
        incoming[d].wait()
        value = turned[d].T
        if d == 2:
            value = pltpu.roll(value, LZ // 2, 1) * swap_ref[...]
        packed[...] = value
        for y in range(BY):
            padded[d, y, :BX, :] = packed[y * BX : (y + 1) * BX, :]
            padded[d, y, BX:, :] = jnp.zeros((40 - BX, LZ), F32)

    def column(col, carry):
        y = (col % CY) * CELL
        x = pl.multiple_of((col // CY) * CELL, CELL)
        planes = products(edges_ref[col])
        modes = modes_ref[col]
        modes = jnp.concatenate([modes, modes[:LZ]], axis=0)
        for d in range(3):
            block = padded[d, pl.ds(y, 12), pl.ds(x, 16), :].reshape(192, LZ)
            along = dot(left_split(block), modes)
            force = jnp.sum(along * planes, axis=0, keepdims=True)
            for zg in range(4):
                rows_out[d, pl.ds(col * 4 + zg, 1), :] = force[:, 128 * zg : 128 * (zg + 1)]
        return carry

    lax.fori_loop(0, CX * CY, column, 0, unroll=8)
    for d in range(3):
        value = rows_out[d]
        pieces = [value[:, s * SLOTS : (s + 1) * SLOTS][:, None, :] for s in range(4)]
        out_ref[d] = jnp.concatenate(pieces, axis=1).reshape(CELLS, SLOTS)


COULOMB = (
    -0.006156452396320011,
    -0.0004198503476764426,
    0.4251962050951751,
    -0.035971568956237085,
    0.5422242920959217,
    -0.3965913855606964,
    0.1962617265017834,
    -0.05766279059061346,
    0.007452967624700701,
)


def pair_term(own, other):
    dx = other[0] - own[0]
    dy = other[1] - own[1]
    dz = other[2] - own[2]
    r2 = dx * dx + dy * dy + dz * dz
    gap = FAR - r2
    fade = jnp.maximum(gap, 0.0)
    t = lax.rsqrt(r2 + LENGTH * LENGTH)
    scale = -2.0 * math.exp(-GEWALD * GEWALD) * 2.0**-FAR / (FAR * LENGTH)
    terms = [scale * c * LENGTH**n for n, c in enumerate(COULOMB)]
    poly = terms[-1] * t + terms[-2]
    for c in terms[-3::-1]:
        poly = poly * t + c
    sigma = own[5] + other[5]
    square = sigma * sigma
    inverse = 1.0 / (r2 + square)
    x = square * inverse
    x3 = x * x * x
    rest = 1.0 - (x3 + x3)
    lj = x3 * (rest * ((fade * inverse) * 3.0 + 1.0) + 1.0)
    w = fade * ((own[4] * other[4]) * lj + (own[3] * other[3]) * (jnp.exp2(gap) * poly))
    return w * dx, w * dy, w * dz


def shifted_z(value, at_z, step):
    if step == 0:
        return value
    if step > 0:
        return jnp.where(
            at_z == CZ - 1, pltpu.roll(value, CZ - 1, 1), pltpu.roll(value, CELLS - 1, 1)
        )
    return jnp.where(at_z == 0, pltpu.roll(value, CELLS - CZ + 1, 1), pltpu.roll(value, 1, 1))


def pair_kernel(*refs, passes, single, sources, begun, unroll):
    blocks, start, outs = refs[:sources], refs[sources : sources + begun], refs[sources + begun : -3]
    others, own, back = refs[-3:]
    low = (lax.broadcasted_iota(jnp.int32, (SLOTS, 256), 1) & CZ) == 0
    at_z = lax.broadcasted_iota(jnp.int32, (SLOTS, CELLS), 1) & (CZ - 1)
    empty = jnp.zeros((SLOTS, 64), F32)
    for c in range(6):
        wide = jnp.concatenate([blocks[1][c], blocks[0][c], blocks[2][c], empty], axis=1)
        own[c] = blocks[0][c]
        layers = {0: wide}
        if sources > 3:
            above = jnp.concatenate([blocks[4][c], blocks[3][c], blocks[5][c], empty], axis=1)
            layers[1] = jnp.where(low, pltpu.roll(wide, 256 - CZ, 1), pltpu.roll(above, CZ, 1))
        for n, offset in enumerate(passes):
            at = COLUMNS * (offset[0] + 1)
            value = layers[offset[1]][:, at : at + CELLS]
            value = shifted_z(value, at_z, offset[2])
            others[c, n * SLOTS : (n + 1) * SLOTS] = (
                value + offset[c] * CELL * LENGTH if c < 3 else value
            )

    def step(n, sums, reverse):
        sums = list(sums)
        for jj in range(unroll):
            j = n * unroll + jj
            other = [others[c, pl.ds(j, 8, stride=0), :] for c in range(6)]
            total = [None] * 3
            for block in range(4):
                mine = [own[c, 8 * block : 8 * block + 8, :] for c in range(6)]
                force = pair_term(mine, other)
                for d in range(3):
                    sums[block * 3 + d] = sums[block * 3 + d] + force[d]
                    total[d] = force[d] if block == 0 else total[d] + force[d]
            if reverse:
                for d in range(3):
                    back[d, pl.ds(pl.multiple_of((j - single * SLOTS) * 8, 8), 8), :] = total[d]
        return tuple(sums)

    per = SLOTS // unroll
    sums = (jnp.zeros((8, CELLS), F32),) * 12
    sums = lax.fori_loop(0, single * per, functools.partial(step, reverse=False), sums)
    sums = lax.fori_loop(
        single * per, len(passes) * per, functools.partial(step, reverse=True), sums
    )
    nothing = jnp.zeros((SLOTS, 128), F32)
    for d in range(3):
        force = jnp.concatenate([sums[block * 3 + d] for block in range(4)], axis=0)
        here = pltpu.roll(jnp.concatenate([force, nothing], axis=1), COLUMNS, 1)
        there = jnp.zeros((SLOTS, 256), F32)
        for n, offset in enumerate(passes):
            if n < single:
                continue
            base = (n - single) * SLOTS * 8
            value = back[d, pl.ds(base, SLOTS, stride=8), :]
            for s in range(1, 8):
                value = value + back[d, pl.ds(base + s, SLOTS, stride=8), :]
            value = shifted_z(value, at_z, -offset[2])
            value = jnp.concatenate([value, nothing], axis=1)
            at = COLUMNS * (offset[0] + 1)
            if offset[1]:
                here = here - pltpu.roll(jnp.where(low, value, 0.0), at + CZ, 1)
                there = there - pltpu.roll(jnp.where(low, 0.0, value), (at - CZ) % 256, 1)
            else:
                here = here - pltpu.roll(value, at, 1)
        if not begun:
            outs[0][d] = here
            outs[1][d] = there
            continue
        here = here + start[0][d]
        there = there + start[1][d]
        for at, total in ((0, here), (3, there)):
            outs[at][d] = total[:, COLUMNS : COLUMNS + CELLS]
            outs[at + 1][d] = total[:, :COLUMNS]
            outs[at + 2][d] = total[:, COLUMNS + CELLS : 2 * COLUMNS + CELLS]


def pair_forces(blocks, passes, single=0, start=(), unroll=16):
    rows = len(passes) * SLOTS
    pairs = rows * SLOTS * CELLS
    widths = (CELLS, COLUMNS, COLUMNS) * 2 if start else (256, 256)
    return pl.pallas_call(
        functools.partial(
            pair_kernel,
            passes=tuple(passes),
            single=single,
            sources=len(blocks),
            begun=len(start),
            unroll=unroll,
        ),
        out_shape=[jax.ShapeDtypeStruct((3, SLOTS, width), F32) for width in widths],
        in_specs=[VMEM] * (len(blocks) + len(start)),
        out_specs=[VMEM] * len(widths),
        scratch_shapes=[
            pltpu.VMEM((6, rows + 8, CELLS), F32),
            pltpu.VMEM((6, SLOTS, CELLS), F32),
            pltpu.VMEM((3, (rows - single * SLOTS) * 8, CELLS), F32),
        ],
        compiler_params=params(8),
        cost_estimate=pl.CostEstimate(flops=70 * pairs, bytes_accessed=1 << 20, transcendentals=0),
    )(*blocks, *start)


def join_kernel(here_ref, down_ref, first_a, first_b, last_a, last_b, out_ref):
    middle = jnp.zeros((SLOTS, CELLS - 2 * COLUMNS), F32)
    for d in range(3):
        sides = [first_a[d] + first_b[d], middle, last_a[d] + last_b[d]]
        out_ref[d] = (here_ref[d] + down_ref[d] + jnp.concatenate(sides, axis=1)).T


def hbm(array):
    return pltpu.with_memory_space_constraint(jnp.asarray(array), pltpu.HBM)


def send(value, step_x, step_y):
    route = [
        (x * DY + y, (x + step_x) % DX * DY + (y + step_y) % DY)
        for x in range(DX)
        for y in range(DY)
    ]
    return lax.ppermute(value, ("gx", "gy"), route)


def body(positions, charges, types, counts, eps_type, sig_type):
    tab = tables()
    slot_last = lambda a: jnp.moveaxis(a, -4, -1).reshape(a.shape[:-4] + (CELLS, SLOTS))
    side = jax.ShapeDtypeStruct((6, SLOTS, COLUMNS), F32)
    atoms, first, last, rows, tz = pl.pallas_call(
        table_kernel,
        out_shape=(
            jax.ShapeDtypeStruct((6, SLOTS, CELLS), F32),
            side,
            side,
            jax.ShapeDtypeStruct((4, GROUPS, 128), F32),
            jax.ShapeDtypeStruct(tab["tz"].shape, BF16),
        ),
        in_specs=[ANY] * 7,
        out_specs=(VMEM,) * 5,
        scratch_shapes=[
            pltpu.VMEM((3, CELLS, SLOTS), F32),
            pltpu.VMEM((CELLS, SLOTS), F32),
            pltpu.VMEM((CELLS, SLOTS), jnp.int32),
            pltpu.VMEM((CX, CY, CZ), jnp.int32),
            pltpu.SMEM(eps_type.shape, F32),
            pltpu.SMEM(sig_type.shape, F32),
            pltpu.SemaphoreType.DMA((7,)),
        ],
        compiler_params=params(8),
    )(
        hbm(slot_last(positions)),
        hbm(slot_last(charges)),
        hbm(slot_last(types)),
        hbm(counts),
        hbm(eps_type),
        hbm(sig_type),
        hbm(tab["tz"]),
    )
    after = send(first, -1, 0)
    before = send(last, 1, 0)
    above = send(atoms, 0, -1)
    above_after = send(first, -1, -1)
    above_before = send(last, 1, -1)

    spread = pl.pallas_call(
        spread_kernel,
        out_shape=jax.ShapeDtypeStruct((LZ, 1, BLOCK), F32),
        in_specs=[VMEM, VMEM, ANY],
        out_specs=ANY,
        scratch_shapes=[
            pltpu.VMEM((BY, 40, LZ), F32),
            pltpu.VMEM((BLOCK, LZ), F32),
            pltpu.VMEM((LZ, BLOCK), F32),
            pltpu.SemaphoreType.DMA((2,)),
        ],
        compiler_params=params(16),
    )(rows, tz, hbm(tab["plane"]))
    spread, after, before, above, above_after, above_before = lax.optimization_barrier(
        (spread, after, before, above, above_after, above_before)
    )
    blocks = (atoms, before, after, above, above_before, above_after)
    lines = lax.all_to_all(hbm(spread), ("gx", "gy"), split_axis=0, concat_axis=0, tiled=True)
    sums = pair_forces(
        blocks,
        [(0, 0, 0), (0, 0, 1), (1, 0, -1), (1, 0, 0), (1, 0, 1), (0, 1, -1), (0, 1, 0)],
        single=1,
    )
    modes, edges = pl.pallas_call(
        weight_kernel,
        out_shape=(
            jax.ShapeDtypeStruct((CX * CY, 2 * LZ, 512), BF16),
            jax.ShapeDtypeStruct((CX * CY, 32, 512), F32),
        ),
        in_specs=[VMEM] * 2,
        out_specs=(VMEM, VMEM),
        compiler_params=params(8),
        cost_estimate=pl.CostEstimate(flops=1 << 28, bytes_accessed=1 << 20, transcendentals=0),
    )(rows, tz)
    lines, modes, edges, *sums = lax.optimization_barrier((lines, modes, edges, *sums))

    constants = [hbm(tab[name]) for name in ("tx", "ty", "iy", "ix")]
    fields = pl.pallas_call(
        plane_kernel,
        out_shape=jax.ShapeDtypeStruct((DX * DY, 1, 3 * BLOCK), F32),
        in_specs=[ANY] * 5,
        out_specs=ANY,
        scratch_shapes=[
            *(pltpu.VMEM(tab[name].shape, BF16) for name in ("tx", "ty", "iy", "ix")),
            pltpu.VMEM((DX * DY, BLOCK), F32),
            pltpu.VMEM((DX // 2, BY * DY, 128), F32),
            pltpu.VMEM((3, DX * DY, BLOCK), F32),
            pltpu.SemaphoreType.DMA((8,)),
        ],
        compiler_params=params(20),
    )(lines, *constants)
    fields = lax.all_to_all(hbm(fields), ("gx", "gy"), split_axis=0, concat_axis=0, tiled=True)
    here, to_before, to_after, up, up_before, up_after = pair_forces(
        blocks, [(0, 1, 1)] + [(a, 1, c) for a in (-1, 1) for c in (-1, 0, 1)], start=sums
    )
    sides = (
        send(up, 0, 1),
        send(to_after, 1, 0),
        send(up_after, 1, 1),
        send(to_before, -1, 0),
        send(up_before, -1, 1),
    )

    fields, here = lax.optimization_barrier((fields, here))
    mesh_force = pl.pallas_call(
        force_kernel,
        out_shape=jax.ShapeDtypeStruct((3, CELLS, SLOTS), F32),
        in_specs=[ANY, VMEM, VMEM, VMEM],
        out_specs=VMEM,
        scratch_shapes=[
            pltpu.VMEM((3, LZ, BLOCK), F32),
            pltpu.VMEM((BLOCK, LZ), F32),
            pltpu.VMEM((3, BY, 40, LZ), F32),
            pltpu.VMEM((3, GROUPS, 128), F32),
            pltpu.SemaphoreType.DMA((3,)),
        ],
        compiler_params=params(20),
    )(fields, modes, edges, tab["swap"])
    mesh_force, here = lax.optimization_barrier((mesh_force, here))
    pair_force = pl.pallas_call(
        join_kernel,
        out_shape=jax.ShapeDtypeStruct((3, CELLS, SLOTS), F32),
        in_specs=[VMEM] * 6,
        out_specs=VMEM,
        compiler_params=params(4),
    )(here, *sides)

    slot_first = lambda a: jnp.moveaxis(a.reshape(3, CX, CY, CZ, SLOTS), -1, 1)
    return slot_first(pair_force), slot_first(mesh_force)


def solution(mesh):
    placed = (
        P(None, None, "gx", "gy", None),
        P(None, "gx", "gy", None),
        P(None, "gx", "gy", None),
        P("gx", "gy", None),
        P(),
        P(),
    )
    return jax.shard_map(
        body,
        mesh=mesh,
        in_specs=placed,
        out_specs=(P(None, None, "gx", "gy", None), P(None, None, "gx", "gy", None)),
        check_vma=False,
    )
```
